128 devices in a mesh: space: 32 (over y, x, core), probe: 4 (over z).
Axes of the slice: x: 4, y: 4, z: 4, core: 2. Of those that a mesh axis runs over, the one named last changes fastest.
Arguments:
- points: float32 [1024, 3, 512], P('space')
- probes: float32 [1024, 32, 512], P('space', 'probe'), may hold values from -6 to 6
- counts: int32 [1024], P('space'), may hold values from 128 to 512, as said below
- near_list: int32 [1024, 8], P('space'), may hold values from 0 to 1023, as said below
- far_list: int32 [1024, 32], P('space'), may hold values from 0 to 1023, as said below
- coarse_list: int32 [56, 16], replicated, may hold values from 0 to 31, as said below
- leaf_proxy: float32 [1024, 3, 64], P('space')
- box_proxy: float32 [56, 3, 64], replicated
Outputs:
- result: float32 [1024, 32, 512], P('space', 'probe')
The draws below stay inside these ranges and needn't reach their ends.
Inputs may be any that keep to these rules, and one draw needn't show every extreme that they name: `counts`: the first leaf of every block of 32 is full. `near_list`: entry 0 of row i is i; every entry lies within 32 of its row's index. `far_list`: every entry lies within 32 of its row's index. `coarse_list`: rows 0 to 31 belong to device boxes, the next 16 to pair boxes, the last 8 to quad boxes; each entry is a box index within its row's level and never the row's own box.
All inputs are finite; a program needn't handle non-finite values.
Results may differ from the reference program's by a relative error of at most 0.00018.
Values sent between devices are 32-bit elements; how exact they have to be, the bound alone decides.
No kernel may reach another device: no remote copies, remote signals or barrier semaphores. Data moves between devices by JAX's collectives and lax.ppermute only.
A program may use at most 64 MiB of HBM per device.

```python
import jax
import jax.numpy as jnp
from jax import lax

LEAF = 512
RANK = 64
PROBES = 32
NEAR = 8
FAR = 32
FARC = 16
L_DEV = 32
NODES = 32
NLEAF = 1024
NBOX = 56


cloud_width = 6.0


proxy_width = 4.0


def leaf_centers(leaf_index):
    coords = []
    for axis_index in range(3):
        coord_value = jnp.zeros_like(leaf_index)
        for bit_index in range(7):
            shifted = jnp.right_shift(leaf_index, 3 * bit_index + axis_index)
            coord_value = coord_value + jnp.bitwise_and(shifted, 1) * 2 ** bit_index
        coords.append(coord_value)
    return jnp.stack(coords, axis=-1).astype(jnp.float32)


def draw_points(key, part):
    centers = leaf_centers(jnp.arange(NLEAF, dtype=jnp.int32))
    jitter = jax.random.uniform(jax.random.fold_in(key, 11), (NLEAF, 3, LEAF), jnp.float32, 0.5 - 0.5 * cloud_width, 0.5 + 0.5 * cloud_width)
    return centers[:, :, None] + jitter


def draw_leaf_proxy(key, part):
    centers = leaf_centers(jnp.arange(NLEAF, dtype=jnp.int32))
    jitter = jax.random.uniform(jax.random.fold_in(key, 12), (NLEAF, 3, RANK), jnp.float32, 0.5 - 0.5 * proxy_width, 0.5 + 0.5 * proxy_width)
    return centers[:, :, None] + jitter


def level_layout():
    rows_all = jnp.arange(NBOX, dtype=jnp.int32)
    pair_beginning = NODES
    quad_start = NODES + NODES // 2
    box_span = jnp.where(rows_all < pair_beginning, L_DEV, jnp.where(rows_all < quad_start, 2 * L_DEV, 4 * L_DEV))
    in_level = jnp.where(rows_all < pair_beginning, rows_all, jnp.where(rows_all < quad_start, rows_all - pair_beginning, rows_all - quad_start))
    box_count = jnp.where(rows_all < pair_beginning, NODES, jnp.where(rows_all < quad_start, NODES // 2, NODES // 4))
    return (box_span.astype(jnp.int32), in_level.astype(jnp.int32), box_count.astype(jnp.int32))


def draw_box_proxy(key, part):
    box_span, in_level, box_count = level_layout()
    first_leaf = in_level * box_span
    picks = first_leaf[:, None] + jax.random.randint(jax.random.fold_in(key, 13), (NBOX, RANK), 0, box_span[:, None])
    centers = leaf_centers(picks)
    jitter = jax.random.uniform(jax.random.fold_in(key, 14), (NBOX, 3, RANK), jnp.float32)
    return jnp.transpose(centers, (0, 2, 1)) + jitter


def draw_counts(key, part):
    leaf_index = jnp.arange(NLEAF, dtype=jnp.int32)
    drawn = jax.random.randint(jax.random.fold_in(key, 15), (NLEAF,), LEAF // 4, LEAF + 1)
    drawn = jnp.where(leaf_index % L_DEV == 0, LEAF, drawn)
    return jnp.where(leaf_index % L_DEV == 1, LEAF // 4, drawn).astype(jnp.int32)


def draw_near_list(key, part):
    leaf_index = jnp.arange(NLEAF, dtype=jnp.int32)
    offsets = jax.random.randint(jax.random.fold_in(key, 16), (NLEAF, NEAR), -L_DEV, L_DEV + 1)
    listed = jnp.clip(leaf_index[:, None] + offsets, 0, NLEAF - 1)
    reach = jnp.where(leaf_index + L_DEV < NLEAF, leaf_index + L_DEV, leaf_index - L_DEV)
    listed = listed.at[:, 0].set(leaf_index).at[:, 1].set(reach)
    return listed.astype(jnp.int32)


def draw_far_list(key, part):
    leaf_index = jnp.arange(NLEAF, dtype=jnp.int32)
    offsets = jax.random.randint(jax.random.fold_in(key, 17), (NLEAF, FAR), -L_DEV, L_DEV + 1)
    listed = jnp.clip(leaf_index[:, None] + offsets, 0, NLEAF - 1)
    reach = jnp.where(leaf_index >= L_DEV, leaf_index - L_DEV, leaf_index + L_DEV)
    listed = listed.at[:, 0].set(reach)
    return listed.astype(jnp.int32)


def draw_coarse_list(key, part):
    box_span, in_level, box_count = level_layout()
    stepped = jax.random.randint(jax.random.fold_in(key, 18), (NBOX, FARC), 1, box_count[:, None])
    listed = (in_level[:, None] + stepped) % box_count[:, None]
    listed = listed.at[0, 0].set(NODES - 1).at[1, 0].set(0)
    return listed.astype(jnp.int32)


def steps_of(stream_key, extent, shards, smallest, largest):
    factor_of = 1.0
    for dim, shards_of in shards:
        steps = jax.random.uniform(jax.random.fold_in(jax.random.fold_in(stream_key, 6), dim), (shards_of,), jnp.float32, smallest / len(shards), largest / len(shards))
        factor_of = factor_of * jnp.repeat(jnp.exp(steps), extent[dim] // shards_of).reshape((-1,) + (1,) * (len(extent) - 1 - dim))
    return factor_of


def normal_values(stream_key, extent, width, most, cuts=(), held_as=jnp.bfloat16):
    level = steps_of(stream_key, extent, cuts, -0.22, 0.18) if cuts else 1.0
    values = jax.random.normal(stream_key, extent, jnp.float32) * width * level
    return jnp.minimum(jnp.maximum(values, -most), most).astype(held_as)


def setup_inputs(seed: int = 0) -> dict:
    seeds = jax.random.split(jax.random.key(seed), 9)
    return {
        "points": draw_points(jax.random.fold_in(seeds[8], 71), 0),
        "probes": normal_values(seeds[1], (NLEAF, PROBES, LEAF), 1.0, 6.0, ((0, 32), (1, 4)), jnp.float32),
        "counts": draw_counts(jax.random.fold_in(seeds[8], 71), 0),
        "near_list": draw_near_list(jax.random.fold_in(seeds[8], 71), 0),
        "far_list": draw_far_list(jax.random.fold_in(seeds[8], 71), 0),
        "coarse_list": draw_coarse_list(jax.random.fold_in(seeds[8], 71), 0),
        "leaf_proxy": draw_leaf_proxy(jax.random.fold_in(seeds[8], 71), 0),
        "box_proxy": draw_box_proxy(jax.random.fold_in(seeds[8], 71), 0),
    }


ROOT_THREE = 1.7320508075688772
LENGTH_SCALE = 2.0
TOP_ACCURACY = lax.Precision.HIGHEST

def kernel_value(source, target):
    offset = source[:, :, None] - target[:, None, :]
    scaled = ROOT_THREE * jnp.sqrt(lax.optimization_barrier(jnp.sum(offset * offset, axis=0))) / LENGTH_SCALE
    return (1.0 + scaled) * jnp.exp(-scaled)

def kernel_slope(source, target):
    offset = source[:, :, None] - target[:, None, :]
    scaled = ROOT_THREE * jnp.sqrt(lax.optimization_barrier(jnp.sum(offset * offset, axis=0))) / LENGTH_SCALE
    return scaled * scaled * jnp.exp(-scaled) / LENGTH_SCALE

def far_single(every_moment, proxies, listing_row, target, reciprocal_rank):
    sources = proxies[listing_row]
    slope_panel = jax.vmap(kernel_slope, in_axes=(0, None))(sources, target) * reciprocal_rank
    return jnp.einsum('dgm,dmi->gi', every_moment[listing_row], slope_panel, precision=TOP_ACCURACY)

def far_level(every_moment, proxies, list_rows, targets, reciprocal_rank):
    return lax.map(lambda pair_args: far_single(every_moment, proxies, pair_args[0], pair_args[1], reciprocal_rank), (list_rows, targets))

def reference(points, probes, counts, near_list, far_list, coarse_list, leaf_proxy, box_proxy):
    factor = LEAF ** (-0.5)
    reciprocal_rank = 1.0 / RANK
    slot_index = lax.broadcasted_iota(jnp.int32, (NLEAF, LEAF), 1)
    live_mask = (slot_index < counts[:, None]).astype(jnp.float32)
    masked = probes * live_mask[:, None, :]
    leaf_basis = jax.vmap(kernel_value)(points, leaf_proxy)
    moments = jnp.einsum('lqp,lpr->lqr', masked, leaf_basis, precision=TOP_ACCURACY) * factor
    owner = jnp.arange(NLEAF, dtype=jnp.int32) // L_DEV
    proxy_dev = box_proxy[:NODES]
    proxy_pair = box_proxy[NODES:NODES + NODES // 2]
    proxy_quad = box_proxy[NODES + NODES // 2:]
    up_leaf = jax.vmap(kernel_value)(leaf_proxy, proxy_dev[owner]) * reciprocal_rank
    terms = jnp.einsum('lqr,lrs->lqs', moments, up_leaf, precision=TOP_ACCURACY)
    moments_dev = lax.optimization_barrier(jnp.sum(terms.reshape(NODES, L_DEV, PROBES, RANK), axis=1))
    pair_index = jnp.arange(NODES, dtype=jnp.int32) // 2
    up_dev = jax.vmap(kernel_value)(proxy_dev, proxy_pair[pair_index]) * reciprocal_rank
    terms = jnp.einsum('nqr,nrs->nqs', moments_dev, up_dev, precision=TOP_ACCURACY)
    moments_pair = lax.optimization_barrier(jnp.sum(terms.reshape(NODES // 2, 2, PROBES, RANK), axis=1))
    quad_index = jnp.arange(NODES // 2, dtype=jnp.int32) // 2
    up_pair = jax.vmap(kernel_value)(proxy_pair, proxy_quad[quad_index]) * reciprocal_rank
    terms = jnp.einsum('nqr,nrs->nqs', moments_pair, up_pair, precision=TOP_ACCURACY)
    moments_quad = lax.optimization_barrier(jnp.sum(terms.reshape(NODES // 4, 2, PROBES, RANK), axis=1))
    local_quad = far_level(moments_quad, proxy_quad, coarse_list[NODES + NODES // 2:], proxy_quad, reciprocal_rank)
    down_pair = jax.vmap(kernel_value)(proxy_quad[quad_index], proxy_pair) * reciprocal_rank
    local_pair = jnp.einsum('nqr,nrs->nqs', local_quad[quad_index], down_pair, precision=TOP_ACCURACY)
    local_pair = local_pair + far_level(moments_pair, proxy_pair, coarse_list[NODES:NODES + NODES // 2], proxy_pair, reciprocal_rank)
    down_dev = jax.vmap(kernel_value)(proxy_pair[pair_index], proxy_dev) * reciprocal_rank
    local_dev = jnp.einsum('nqr,nrs->nqs', local_pair[pair_index], down_dev, precision=TOP_ACCURACY)
    local_dev = local_dev + far_level(moments_dev, proxy_dev, coarse_list[:NODES], proxy_dev, reciprocal_rank)
    down_leaf = jax.vmap(kernel_value)(proxy_dev[owner], leaf_proxy) * reciprocal_rank
    local_leaf = jnp.einsum('lqr,lrs->lqs', local_dev[owner], down_leaf, precision=TOP_ACCURACY)
    local_leaf = local_leaf + far_level(moments, leaf_proxy, far_list, leaf_proxy, reciprocal_rank)
    far_out = jnp.einsum('lqr,lpr->lqp', local_leaf, leaf_basis, precision=TOP_ACCURACY) * factor

    def near_single(pair_args):
        listing_row, target = pair_args
        slope_panel = jax.vmap(kernel_slope, in_axes=(0, None))(points[listing_row], target)
        return jnp.einsum('eqs,esp->qp', masked[listing_row], slope_panel, precision=TOP_ACCURACY) * factor
    near_field = lax.map(near_single, (near_list, points))
    return (near_field + far_out) * live_mask[:, None, :]
```

```python
import functools

import jax
import jax.numpy as jnp
from jax import lax
from jax.experimental import pallas as pl
from jax.experimental.pallas import tpu as pltpu
from jax.sharding import PartitionSpec as P

F32 = jnp.float32
BF16 = jnp.bfloat16
LOG2E = 1.4426950408889634
LN2 = 0.6931471805599453
SCALE = LOG2E * 1.7320508075688772 / 2.0
SLOPE = 0.5 / (LOG2E * LOG2E)
TINY = 1e-30
FEATURES = 48
CN = (((0,), (0,)), ((), ()))
NT = (((1,), (1,)), ((), ()))
NN = (((1,), (0,)), ((), ()))


def dot(left, right, dims):
    return lax.dot_general(left, right, dims, preferred_element_type=F32)


def split(value):
    high = value.astype(BF16)
    return high, (value - high.astype(F32)).astype(BF16)


def stacked(value):
    high = value.astype(BF16).astype(F32)
    return jnp.concatenate([high, value - high], axis=0).astype(BF16)


def exact_dot(left, right, dims):
    rows = left.shape[0]
    high, low = split(right)
    both = stacked(left)
    total = dot(both, high, dims) + dot(both, low, dims)
    return total[:rows] + total[rows:]


def slope_of(u):
    u = jnp.maximum(u, TINY)
    return u * jnp.exp2(-(u * lax.rsqrt(u)))


def value_of(u):
    u = jnp.maximum(u, TINY)
    w = u * lax.rsqrt(u)
    return (1.0 + LN2 * w) * jnp.exp2(-w)


def pieces(value):
    high = value.astype(BF16).astype(F32)
    rest = value - high
    middle = rest.astype(BF16).astype(F32)
    return high, middle, rest - middle


def features(rows, center, source, target):
    row = lax.broadcasted_iota(jnp.int32, rows.shape, 0)
    scaled = jnp.where(row < 3, (rows - center) * SCALE, 0.0)
    norm = jnp.sum(scaled * scaled, axis=0, keepdims=True)
    out = []
    if source:
        h, m, l = pieces(jnp.where(row == 3, norm, jnp.where(row == 4, 1.0, scaled)))
        out.append(jnp.concatenate([h, h, m, h, l, m], axis=0))
    if target:
        h, m, l = pieces(jnp.where(row == 3, 1.0, jnp.where(row == 4, norm, -2.0 * scaled)))
        out.append(jnp.concatenate([h, m, h, l, h, m], axis=0))
    return out


def twice(value):
    return jnp.concatenate([value, value], axis=1)


def left_half(shape):
    return lax.broadcasted_iota(jnp.int32, shape, 1) < 64


def store_source(slot, leaf, center, fs, ms):
    (source,) = features(leaf[8:16], center, True, False)
    source = source.astype(BF16)
    moments = stacked(leaf[0:8])
    for b in range(4):
        fs[slot * 4 + b] = source[:, b * 128 : (b + 1) * 128]
        ms[slot * 4 + b] = moments[:, b * 128 : (b + 1) * 128]


def store_target(slot, leaf, center, ft):
    (target,) = features(leaf[8:16], center, False, True)
    target = target.astype(BF16)
    for b in range(2):
        ft[slot * 2 + b] = target[:, b * 256 : (b + 1) * 256]


def build_items(near, place, target_count, targets, empty, blocks, items):
    def per_leaf(i, n):
        nb = jnp.int32(0)
        for e in range(8):
            ok, slot, count = place(near[i, e])
            for b in range(4):
                blocks[nb + b] = slot * 4 + b
            nb = nb + jnp.where(ok, (count + 127) >> 7, 0)
        blocks[nb] = empty
        pairs = (nb + 1) >> 1

        def put(q, carry):
            code = (blocks[2 * q] << 9) | blocks[2 * q + 1]
            items[n + q] = code | ((2 * i) << 18)
            items[n + pairs + q] = code | ((2 * i + 1) << 18)
            return carry

        lax.fori_loop(0, pairs, put, 0)
        return n + jnp.where(target_count(i) > 256, 2 * pairs, pairs)

    n = lax.fori_loop(0, targets, per_leaf, jnp.int32(0))
    for t in range(3):
        items[n + t] = (empty << 9) | empty
    return n


def run_items(items, n, fs, ft, ms, acc, u0, u1):
    slots = (u0, u1)

    def distances(code, u):
        left = jnp.concatenate([fs[(code >> 9) & 511], fs[code & 511]], axis=1)
        u[...] = dot(left, ft[code >> 18], CN)

    def contract(code, u):
        high, low = split(slope_of(u[...]))
        m = jnp.concatenate([ms[(code >> 9) & 511], ms[code & 511]], axis=1)
        acc[code >> 18] += dot(m, high, NN) + dot(m, low, NN)

    distances(items[0], u0)

    def body(t, carry):
        for s in range(2):
            distances(items[2 * t + s + 1], slots[1 - s])
            contract(items[2 * t + s], slots[s])
        return carry

    lax.fori_loop(0, (n + 1) >> 1, body, 0)


def moments_kernel(payload, leafp, own, center, pay2, dev, *, leaves, factor):
    c = center[:, 0:1]
    (own_target,) = features(own[...], c, False, True)
    own_target = own_target.astype(BF16)[:, :64]

    def body(t, total):
        for s in range(4):
            i = t * 4 + s
            leaf = payload[i]
            (target,) = features(leaf[8:16], c, False, True)
            (source,) = features(leafp[i], c, True, False)
            source = source.astype(BF16)[:, :64]
            basis = value_of(dot(source, target.astype(BF16), CN))
            moments = exact_dot(leaf[0:8], basis, NT) * factor
            pay2[i, 0:8, :] = twice(moments)
            pay2[i, 8:16, :] = leafp[i]
            up = value_of(dot(own_target, source, CN))
            total = total + exact_dot(moments, up, NT) * (1.0 / 64)
        return total

    total = lax.fori_loop(0, leaves // 4, body, jnp.zeros((8, 64), F32))
    dev[...] = twice(total)


def own_kernel(near, counts, payload, center, acc, fs, ms, ft, u0, u1, blocks, items, *, leaves):
    c = center[:, 0:1]

    def prep(i, carry):
        leaf = payload[i]
        store_source(i, leaf, c, fs, ms)
        store_target(i, leaf, c, ft)
        return carry

    lax.fori_loop(0, leaves, prep, 0)
    for b in range(4):
        fs[leaves * 4 + b] = jnp.zeros((FEATURES, 128), BF16)
        ms[leaves * 4 + b] = jnp.zeros((16, 128), BF16)
    acc[...] = jnp.zeros_like(acc)

    def place(j):
        ok = (j >= leaves) & (j < 2 * leaves)
        slot = jnp.where(ok, j - leaves, 0)
        return ok, slot, counts[slot]

    n = build_items(near, place, lambda i: counts[i], leaves, leaves * 4, blocks, items)
    run_items(items, n, fs, ft, ms, acc, u0, u1)


def far_sum(lists, count, source_of, moment_of, target):
    half = left_half((FEATURES, 128))
    half8 = left_half((8, 128))
    total = jnp.zeros((8, 64), F32)
    for chunk in range(count // 8):
        sources, moments = [], []
        for q in range(4):
            a, b = lists(chunk * 8 + 2 * q), lists(chunk * 8 + 2 * q + 1)
            sources.append(jnp.where(half, source_of(a), source_of(b)).astype(BF16))
            moments.append(jnp.where(half8, moment_of(a), moment_of(b)))
        panel = slope_of(dot(target, jnp.concatenate(sources, axis=1), CN))
        total = total + exact_dot(jnp.concatenate(moments, axis=1), panel, NT)
    return total * (SLOPE / 64)


def upper_levels(coarse, me, box8, roots, c, fbs, fbt, pm, qm):
    def prep(b, carry):
        fbs[b], fbt[b] = features(box8[b], c, True, True)
        return carry

    lax.fori_loop(0, 56, prep, 0)
    half = left_half((FEATURES, 128))
    half8 = left_half((8, 128))

    def merge(child, parent, moments, out, count):
        def body(t, carry):
            for s in range(4):
                m = t * 4 + s
                source = jnp.where(half, fbs[child + 2 * m], fbs[child + 2 * m + 1]).astype(BF16)
                target = fbt[parent + m].astype(BF16)[:, :64]
                panel = value_of(dot(target, source, CN))
                pair = jnp.where(half8, moments[2 * m], moments[2 * m + 1])
                out[m] = twice(exact_dot(pair, panel, NT) * (1.0 / 64))
            return carry

        lax.fori_loop(0, count // 4, body, 0)

    merge(0, 32, roots, pm, 16)
    merge(32, 48, pm, qm, 8)
    n = me
    m = n >> 1
    t = n >> 2

    def far(base, row, moments):
        target = fbt[row].astype(BF16)[:, :64]
        return far_sum(
            lambda e: coarse[row, e], 16, lambda b: fbs[base + b], lambda b: moments[b], target
        )

    def down(local, source, target):
        panel = value_of(dot(fbt[target].astype(BF16)[:, :64], fbs[source].astype(BF16)[:, :64], CN))
        return exact_dot(local, panel, NT) * (1.0 / 64)

    quad = far(48, 48 + t, qm)
    pair = down(quad, 48 + t, 32 + m) + far(32, 32 + m, pm)
    return down(pair, 32 + m, n) + far(0, n, roots)


def rest_kernel(
    near, far, coarse, counts, me,
    own, low, high, near0, pay_own, pay_low, pay_high, box8, roots, center,
    out,
    acc, fs, ms, ft, u0, u1, fps, fpt, mps, fbs, fbt, pm, qm, blocks, items,
    *, leaves, factor,
):
    c = center[:, 0:1]

    def prep(i, carry):
        store_source(i, low[i], c, fs, ms)
        store_source(leaves + i, high[i], c, fs, ms)
        store_target(i, own[i], c, ft)
        return carry

    lax.fori_loop(0, leaves, prep, 0)
    empty = 2 * leaves * 4
    for b in range(4):
        fs[empty + b] = jnp.zeros((FEATURES, 128), BF16)
        ms[empty + b] = jnp.zeros((16, 128), BF16)
    acc[...] = near0[...]

    def place(j):
        ok = (j < leaves) | (j >= 2 * leaves)
        slot = jnp.where(j < leaves, j, j - leaves)
        slot = jnp.where(ok, slot, 0)
        return ok, slot, counts[jnp.where(ok, j, 0)]

    n = build_items(near, place, lambda i: counts[leaves + i], leaves, empty, blocks, items)
    run_items(items, n, fs, ft, ms, acc, u0, u1)

    def prep_far(i, carry):
        for k, page in enumerate((pay_low, pay_own, pay_high)):
            (fps[k * leaves + i],) = features(page[i, 8:16], c, True, False)
            mps[k * leaves + i] = page[i, 0:8]
        (fpt[i],) = features(pay_own[i, 8:16], c, False, True)
        return carry

    lax.fori_loop(0, leaves, prep_far, 0)
    dev = me[0]
    local_dev = upper_levels(coarse, dev, box8, roots, c, fbs, fbt, pm, qm)
    own_source = fbs[dev].astype(BF16)[:, :64]
    lane = lax.broadcasted_iota(jnp.int32, (8, 512), 1)

    def finish(t, carry):
        for s in range(2):
            i = t * 2 + s
            target = fpt[i].astype(BF16)[:, :64]
            local = far_sum(lambda e: far[i, e], 32, lambda b: fps[b], lambda b: mps[b], target)
            panel = value_of(dot(target, own_source, CN))
            local = local + exact_dot(local_dev, panel, NT) * (1.0 / 64)
            source = fps[leaves + i].astype(BF16)[:, :64]
            points = jnp.concatenate([ft[2 * i], ft[2 * i + 1]], axis=1)
            basis = value_of(dot(source, points, CN))
            far_out = exact_dot(local, basis, NN)
            both = jnp.concatenate([acc[2 * i], acc[2 * i + 1]], axis=1)
            near_out = (both[0:8] + both[8:16]) * SLOPE
            out[i] = jnp.where(lane < counts[leaves + i], (near_out + far_out) * factor, 0.0)
        return carry

    lax.fori_loop(0, leaves // 2, finish, 0)


def wide(array):
    rows = jnp.concatenate([array, array], axis=2)
    return jnp.pad(rows, ((0, 0), (0, 8 - array.shape[1]), (0, 0)))


def local(points, probes, counts, near_list, far_list, coarse_list, leaf_proxy, box_proxy):
    leaves = points.shape[0]
    size = points.shape[2]
    nodes = lax.axis_size("space")
    device = lax.axis_index("space")
    factor = size ** (-0.5)
    slot = lax.broadcasted_iota(jnp.int32, (leaves, 1, size), 2)
    masked = jnp.where(slot < counts[:, None, None], probes, 0.0)
    count_row = jnp.broadcast_to(counts.astype(F32)[:, None, None], (leaves, 5, size))
    payload = jnp.concatenate([masked, points, count_row], axis=1)
    forward = [(i, i + 1) for i in range(nodes - 1)]
    backward = [(i + 1, i) for i in range(nodes - 1)]
    low = lax.ppermute(payload, "space", forward)
    high = lax.ppermute(payload, "space", backward)
    leafp = wide(leaf_proxy)
    box8 = wide(box_proxy)
    center = jnp.broadcast_to(jnp.pad(points[0, :, 0], (0, 5))[:, None], (8, 128))
    own = lax.dynamic_index_in_dim(box8, device, 0, keepdims=False)
    params = pltpu.CompilerParams(vmem_limit_bytes=56 << 20)
    vmem = pl.BlockSpec(memory_space=pltpu.VMEM)
    smem = pl.BlockSpec(memory_space=pltpu.SMEM)
    pay2, dev = pl.pallas_call(
        functools.partial(moments_kernel, leaves=leaves, factor=factor),
        out_shape=(
            jax.ShapeDtypeStruct((leaves, 16, 128), F32),
            jax.ShapeDtypeStruct((8, 128), F32),
        ),
        in_specs=[vmem] * 4,
        out_specs=(vmem, vmem),
        compiler_params=params,
        name="moments",
    )(payload, leafp, own, center)
    low2 = lax.ppermute(pay2, "space", forward)
    high2 = lax.ppermute(pay2, "space", backward)
    roots = lax.all_to_all(
        jnp.broadcast_to(dev[None], (nodes, 8, 128)), "space", split_axis=0, concat_axis=0, tiled=True
    )
    near = near_list - (device - 1) * leaves
    far = far_list - (device - 1) * leaves
    vm = pltpu.VMEM
    work = lambda blocks: [
        vm((blocks, FEATURES, 128), BF16),
        vm((blocks, 16, 128), BF16),
        vm((leaves * 2, FEATURES, 256), BF16),
        vm((256, 256), F32),
        vm((256, 256), F32),
    ]
    lists = [pltpu.SMEM((48,), jnp.int32), pltpu.SMEM((leaves * 32 + 48,), jnp.int32)]
    near0 = pl.pallas_call(
        functools.partial(own_kernel, leaves=leaves),
        out_shape=jax.ShapeDtypeStruct((leaves * 2, 16, 256), F32),
        in_specs=[smem, smem, vmem, vmem],
        out_specs=vmem,
        scratch_shapes=work((leaves + 1) * 4) + lists,
        compiler_params=params,
        name="near_own",
    )(near, counts, payload, center)
    counts3 = jnp.concatenate(
        [low[:, 11, 0].astype(jnp.int32), counts, high[:, 11, 0].astype(jnp.int32)]
    )
    return pl.pallas_call(
        functools.partial(rest_kernel, leaves=leaves, factor=factor),
        out_shape=jax.ShapeDtypeStruct(probes.shape, F32),
        in_specs=[smem] * 5 + [vmem] * 10,
        out_specs=vmem,
        scratch_shapes=[vm((leaves * 2, 16, 256), F32)]
        + work((2 * leaves + 1) * 4)
        + [
            vm((3 * leaves, FEATURES, 128), F32),
            vm((leaves, FEATURES, 128), F32),
            vm((3 * leaves, 8, 128), F32),
            vm((56, FEATURES, 128), F32),
            vm((56, FEATURES, 128), F32),
            vm((nodes // 2, 8, 128), F32),
            vm((nodes // 4, 8, 128), F32),
        ]
        + lists,
        compiler_params=params,
        name="near_far",
    )(
        near, far, coarse_list, counts3, device.reshape(1).astype(jnp.int32),
        payload, low, high, near0, pay2, low2, high2, box8, roots, center,
    )


def solution(mesh):
    return jax.shard_map(
        local,
        mesh=mesh,
        in_specs=(
            P("space", None, None),
            P("space", "probe", None),
            P("space"),
            P("space", None),
            P("space", None),
            P(),
            P("space", None, None),
            P(),
        ),
        out_specs=P("space", "probe", None),
        check_vma=False,
    )
```

```python
import functools

import jax
import jax.numpy as jnp
from jax import lax
from jax.experimental import pallas as pl
from jax.experimental.pallas import tpu as pltpu
from jax.sharding import PartitionSpec as P

F32 = jnp.float32
BF16 = jnp.bfloat16
LOG2E = 1.4426950408889634
LN2 = 0.6931471805599453
SCALE = LOG2E * 1.7320508075688772 / 2.0
SLOPE = 0.5 / (LOG2E * LOG2E)
TINY = 1e-30
FEATURES = 48
UNITS = 4
CN = (((0,), (0,)), ((), ()))
NT = (((1,), (1,)), ((), ()))
NN = (((1,), (0,)), ((), ()))


def dot(left, right, dims):
    return lax.dot_general(left, right, dims, preferred_element_type=F32)


def split(value):
    high = value.astype(BF16)
    return high, (value - high.astype(F32)).astype(BF16)


def stacked(value):
    high = value.astype(BF16).astype(F32)
    return jnp.concatenate([high, value - high], axis=0).astype(BF16)


def exact_dot(left, right, dims):
    rows = left.shape[0]
    high, low = split(right)
    both = stacked(left)
    total = dot(both, high, dims) + dot(both, low, dims)
    return total[:rows] + total[rows:]


def slope_of(u):
    u = jnp.maximum(u, TINY)
    return u * jnp.exp2(-(u * lax.rsqrt(u)))


def value_of(u):
    u = jnp.maximum(u, TINY)
    w = u * lax.rsqrt(u)
    return (1.0 + LN2 * w) * jnp.exp2(-w)


def pieces(value):
    high = value.astype(BF16).astype(F32)
    rest = value - high
    middle = rest.astype(BF16).astype(F32)
    return high, middle, rest - middle


def features(rows, center, source, target):
    row = lax.broadcasted_iota(jnp.int32, rows.shape, 0)
    scaled = jnp.where(row < 3, (rows - center) * SCALE, 0.0)
    norm = jnp.sum(scaled * scaled, axis=0, keepdims=True)
    out = []
    if source:
        h, m, l = pieces(jnp.where(row == 3, norm, jnp.where(row == 4, 1.0, scaled)))
        out.append(jnp.concatenate([h, h, m, h, l, m], axis=0))
    if target:
        h, m, l = pieces(jnp.where(row == 3, 1.0, jnp.where(row == 4, norm, -2.0 * scaled)))
        out.append(jnp.concatenate([h, m, h, l, h, m], axis=0))
    return out


def twice(value):
    return jnp.concatenate([value, value], axis=1)


def left_half(shape):
    return lax.broadcasted_iota(jnp.int32, shape, 1) < 64


def store_source(slot, leaf, partner, center, fs, ms):
    (source,) = features(leaf[8:16], center, True, False)
    source = source.astype(BF16)
    lane = lax.broadcasted_iota(jnp.int32, partner.shape, 1).astype(F32)
    other = jnp.where(lane < leaf[11:12], partner, 0.0)
    moments = stacked(jnp.concatenate([leaf[0:8], other], axis=0))
    for b in range(4):
        fs[slot * 4 + b] = source[:, b * 128 : (b + 1) * 128]
        ms[slot * 4 + b] = moments[:, b * 128 : (b + 1) * 128]


def store_target(slot, leaf, center, ft):
    (target,) = features(leaf[8:16], center, False, True)
    target = target.astype(BF16)
    for b in range(2):
        ft[slot * 2 + b] = target[:, b * 256 : (b + 1) * 256]


def build_items(place, target_count, targets, empty, blocks, items):
    def per_leaf(i, n):
        nb = jnp.int32(0)
        for e in range(8):
            ok, slot, count = place(i, e)
            for b in range(4):
                blocks[nb + b] = slot * 4 + b
            nb = nb + jnp.where(ok, (count + 127) >> 7, 0)
        blocks[nb] = empty
        pairs = (nb + 1) >> 1

        def put(q, carry):
            code = (blocks[2 * q] << 9) | blocks[2 * q + 1]
            items[n + q] = code | ((2 * i) << 18)
            items[n + pairs + q] = code | ((2 * i + 1) << 18)
            return carry

        lax.fori_loop(0, pairs, put, 0)
        return n + jnp.where(target_count(i) > 256, 2 * pairs, pairs)

    n = lax.fori_loop(0, targets, per_leaf, jnp.int32(0))
    for t in range(2 * UNITS):
        items[n + t] = (empty << 9) | empty
    return n


def run_items(items, n, fs, ft, ms, acc, slots):
    def distances(code, u):
        left = jnp.concatenate([fs[(code >> 9) & 511], fs[code & 511]], axis=1)
        u[...] = dot(left, ft[code >> 18], CN)

    def contract(code, u):
        high, low = split(slope_of(u[...]))
        m = jnp.concatenate([ms[(code >> 9) & 511], ms[code & 511]], axis=1)
        acc[code >> 18] += dot(m, high, NN) + dot(m, low, NN)

    for s in range(UNITS):
        distances(items[s], slots[s])

    def body(t, carry):
        for s in range(UNITS):
            contract(items[UNITS * t + s], slots[s])
            distances(items[UNITS * (t + 1) + s], slots[s])
        return carry

    lax.fori_loop(0, (n + UNITS - 1) // UNITS, body, 0)


def moments_kernel(payload, leafp, own, center, pay2, dev, *, leaves, factor):
    c = center[:, 0:1]
    (own_target,) = features(own[...], c, False, True)
    own_target = own_target.astype(BF16)[:, :64]

    def body(t, total):
        for s in range(4):
            i = t * 4 + s
            leaf = payload[i]
            (target,) = features(leaf[8:16], c, False, True)
            (source,) = features(leafp[i], c, True, False)
            source = source.astype(BF16)[:, :64]
            basis = value_of(dot(source, target.astype(BF16), CN))
            moments = exact_dot(leaf[0:8], basis, NT) * factor
            pay2[i, 0:8, :] = twice(moments)
            pay2[i, 8:16, :] = leafp[i]
            up = value_of(dot(own_target, source, CN))
            total = total + exact_dot(moments, up, NT) * (1.0 / 64)
        return total

    total = lax.fori_loop(0, leaves // 4, body, jnp.zeros((8, 64), F32))
    dev[...] = twice(total)


def clear_empty(empty, fs, ms):
    fs[empty] = jnp.zeros(fs.shape[1:], BF16)
    ms[empty] = jnp.zeros(ms.shape[1:], BF16)


def own_kernel(
    near, counts, me, payload, partner, center, acc,
    fs, ms, ft, blocks, items, *slots, leaves, targets,
):
    c = center[:, 0:1]
    first = me[1] * targets

    def prep(t, carry):
        for s in range(2):
            i = 2 * t + s
            store_source(i, payload[i], partner[i], c, fs, ms)
        store_target(t, payload[first + t], c, ft)
        return carry

    lax.fori_loop(0, leaves // 2, prep, 0)
    clear_empty(leaves * 4, fs, ms)
    acc[...] = jnp.zeros_like(acc)

    def place(i, e):
        j = near[first + i, e] - me[0] * leaves
        ok = (j >= 0) & (j < leaves)
        slot = jnp.where(ok, j, 0)
        return ok, slot, counts[slot]

    n = build_items(place, lambda i: counts[first + i], targets, leaves * 4, blocks, items)
    run_items(items, n, fs, ft, ms, acc, slots)


def halo_kernel(
    near, counts, me, own, low, high, partner_low, partner_high, center, acc0,
    mine, theirs,
    acc, fs, ms, ft, blocks, items, *slots, leaves, targets, factor,
):
    c = center[:, 0:1]
    first = me[1] * targets

    def prep(i, carry):
        store_source(i, low[i], partner_low[i], c, fs, ms)
        store_source(leaves + i, high[i], partner_high[i], c, fs, ms)
        return carry

    def prep_target(i, carry):
        store_target(i, own[first + i], c, ft)
        return carry

    lax.fori_loop(0, leaves, prep, 0)
    lax.fori_loop(0, targets, prep_target, 0)
    empty = 2 * leaves * 4
    clear_empty(empty, fs, ms)
    acc[...] = acc0[...]

    def place(i, e):
        j = near[first + i, e] - (me[0] - 1) * leaves
        ok = (j < leaves) | (j >= 2 * leaves)
        slot = jnp.where(ok, jnp.where(j < leaves, j, j - leaves), 0)
        return ok, slot, counts[jnp.where(ok, j, 0)]

    n = build_items(place, lambda i: counts[leaves + first + i], targets, empty, blocks, items)
    run_items(items, n, fs, ft, ms, acc, slots)
    scale = SLOPE * factor

    def finish(i, carry):
        for b in range(2):
            total = acc[2 * i + b]
            total = (total[0:16] + total[16:32]) * scale
            mine[i, :, b * 256 : (b + 1) * 256] = total[0:8]
            theirs[i, :, b * 256 : (b + 1) * 256] = total[8:16]
        return carry

    lax.fori_loop(0, targets, finish, 0)


def far_sum(lists, count, source_of, moment_of, target):
    half = left_half((FEATURES, 128))
    half8 = left_half((8, 128))
    total = jnp.zeros((8, 64), F32)
    for chunk in range(count // 8):
        sources, moments = [], []
        for q in range(4):
            a, b = lists(chunk * 8 + 2 * q), lists(chunk * 8 + 2 * q + 1)
            sources.append(jnp.where(half, source_of(a), source_of(b)).astype(BF16))
            moments.append(jnp.where(half8, moment_of(a), moment_of(b)))
        panel = slope_of(dot(target, jnp.concatenate(sources, axis=1), CN))
        total = total + exact_dot(jnp.concatenate(moments, axis=1), panel, NT)
    return total * (SLOPE / 64)


class Relative:
    def __init__(self, array, me):
        self.array, self.me = array, me

    def __getitem__(self, n):
        return self.array[n ^ self.me]


def upper_levels(coarse, me, box8, roots, c, fbs, fbt, pm, qm):
    def prep(b, carry):
        fbs[b], fbt[b] = features(box8[b], c, True, True)
        return carry

    lax.fori_loop(0, 56, prep, 0)
    half = left_half((FEATURES, 128))
    half8 = left_half((8, 128))

    def merge(child, parent, moments, out, count):
        def body(t, carry):
            for s in range(4):
                m = t * 4 + s
                source = jnp.where(half, fbs[child + 2 * m], fbs[child + 2 * m + 1]).astype(BF16)
                target = fbt[parent + m].astype(BF16)[:, :64]
                panel = value_of(dot(target, source, CN))
                pair = jnp.where(half8, moments[2 * m], moments[2 * m + 1])
                out[m] = twice(exact_dot(pair, panel, NT) * (1.0 / 64))
            return carry

        lax.fori_loop(0, count // 4, body, 0)

    merge(0, 32, Relative(roots, me), pm, 16)
    merge(32, 48, pm, qm, 8)
    n = me
    m = n >> 1
    t = n >> 2

    def far(base, row, moments):
        target = fbt[row].astype(BF16)[:, :64]
        return far_sum(
            lambda e: coarse[row, e], 16, lambda b: fbs[base + b], lambda b: moments[b], target
        )

    def down(local, source, target):
        panel = value_of(dot(fbt[target].astype(BF16)[:, :64], fbs[source].astype(BF16)[:, :64], CN))
        return exact_dot(local, panel, NT) * (1.0 / 64)

    quad = far(48, 48 + t, qm)
    pair = down(quad, 48 + t, 32 + m) + far(32, 32 + m, pm)
    return down(pair, 32 + m, n) + far(0, n, Relative(roots, me))


def far_kernel(
    far, coarse, counts, me, own, pay_own, pay_low, pay_high, box8, roots, center,
    out,
    fps, fpt, mps, fbs, fbt, pm, qm,
    *, leaves, factor,
):
    c = center[:, 0:1]

    def prep_far(i, carry):
        for k, page in enumerate((pay_low, pay_own, pay_high)):
            (fps[k * leaves + i],) = features(page[i, 8:16], c, True, False)
            mps[k * leaves + i] = page[i, 0:8]
        (fpt[i],) = features(pay_own[i, 8:16], c, False, True)
        return carry

    lax.fori_loop(0, leaves, prep_far, 0)
    dev = me[0]
    base = (dev - 1) * leaves
    local_dev = upper_levels(coarse, dev, box8, roots, c, fbs, fbt, pm, qm)
    own_source = fbs[dev].astype(BF16)[:, :64]
    def finish(t, carry):
        for s in range(2):
            i = t * 2 + s
            target = fpt[i].astype(BF16)[:, :64]
            local = far_sum(
                lambda e: far[i, e] - base, 32, lambda b: fps[b], lambda b: mps[b], target
            )
            panel = value_of(dot(target, own_source, CN))
            local = local + exact_dot(local_dev, panel, NT) * (1.0 / 64)
            source = fps[leaves + i].astype(BF16)[:, :64]
            (points,) = features(own[i, 8:16], c, False, True)
            basis = value_of(dot(source, points.astype(BF16), CN))
            out[i] = exact_dot(local, basis, NN) * factor
        return carry

    lax.fori_loop(0, leaves // 2, finish, 0)


def wide(array):
    rows = jnp.concatenate([array, array], axis=2)
    return jnp.pad(rows, ((0, 0), (0, 8 - array.shape[1]), (0, 0)))


def local(points, probes, counts, near_list, far_list, coarse_list, leaf_proxy, box_proxy):
    leaves = points.shape[0]
    size = points.shape[2]
    nodes = lax.axis_size("space")
    device = lax.axis_index("space")
    factor = size ** (-0.5)
    slot = lax.broadcasted_iota(jnp.int32, (leaves, 1, size), 2)
    masked = jnp.where(slot < counts[:, None, None], probes, 0.0)
    count_row = jnp.broadcast_to(counts.astype(F32)[:, None, None], (leaves, 5, size))
    payload = jnp.concatenate([masked, points, count_row], axis=1)
    forward = [(i, i + 1) for i in range(nodes - 1)]
    backward = [(i + 1, i) for i in range(nodes - 1)]
    pairs = [(i, i ^ 1) for i in range(lax.axis_size("probe"))]
    partner = lax.ppermute(probes, "probe", pairs)
    low = lax.ppermute(payload, "space", forward)
    high = lax.ppermute(payload, "space", backward)
    partner_low = lax.ppermute(partner, "space", forward)
    partner_high = lax.ppermute(partner, "space", backward)
    leafp = wide(leaf_proxy)
    box8 = wide(box_proxy)
    center = jnp.broadcast_to(jnp.pad(points[0, :, 0], (0, 5))[:, None], (8, 128))
    own = lax.dynamic_index_in_dim(box8, device, 0, keepdims=False)
    half = lax.axis_index("probe") & 1
    me = jnp.stack([device, half]).astype(jnp.int32)
    params = pltpu.CompilerParams(vmem_limit_bytes=56 << 20)
    vm = pltpu.VMEM
    vmem = pl.BlockSpec(memory_space=vm)
    smem = pl.BlockSpec(memory_space=pltpu.SMEM)
    shape = jax.ShapeDtypeStruct
    pay2, dev = pl.pallas_call(
        functools.partial(moments_kernel, leaves=leaves, factor=factor),
        out_shape=(shape((leaves, 16, 128), F32), shape((8, 128), F32)),
        in_specs=[vmem] * 4,
        out_specs=(vmem, vmem),
        compiler_params=params,
        name="moments",
    )(payload, leafp, own, center)
    low2 = lax.ppermute(pay2, "space", forward)
    high2 = lax.ppermute(pay2, "space", backward)
    roots = dev[None]
    for bit in range(nodes.bit_length() - 1):
        swap = [(i, i ^ (1 << bit)) for i in range(nodes)]
        roots = jnp.concatenate([roots, lax.ppermute(roots, "space", swap)], axis=0)
    targets = leaves // 2

    def work(blocks):
        return (
            [
                vm((blocks, FEATURES, 128), BF16),
                vm((blocks, 32, 128), BF16),
                vm((targets * 2, FEATURES, 256), BF16),
                pltpu.SMEM((48,), jnp.int32),
                pltpu.SMEM((targets * 32 + 64,), jnp.int32),
            ]
            + [vm((256, 256), F32)] * UNITS
        )

    acc0 = pl.pallas_call(
        functools.partial(own_kernel, leaves=leaves, targets=targets),
        out_shape=shape((targets * 2, 32, 256), F32),
        in_specs=[smem] * 3 + [vmem] * 3,
        out_specs=vmem,
        scratch_shapes=work(leaves * 4 + 1),
        compiler_params=params,
        name="near_own",
    )(near_list, counts, me, payload, partner, center)
    counts3 = jnp.concatenate(
        [low[:, 11, 0].astype(jnp.int32), counts, high[:, 11, 0].astype(jnp.int32)]
    )
    mine, theirs = pl.pallas_call(
        functools.partial(halo_kernel, leaves=leaves, targets=targets, factor=factor),
        out_shape=(shape((targets, 8, size), F32),) * 2,
        in_specs=[smem] * 3 + [vmem] * 7,
        out_specs=(vmem, vmem),
        scratch_shapes=[vm((targets * 2, 32, 256), F32)] + work(2 * leaves * 4 + 1),
        compiler_params=params,
        name="near_halo",
    )(near_list, counts3, me, payload, low, high, partner_low, partner_high, center, acc0)
    back = lax.ppermute(theirs, "probe", pairs)
    far = pl.pallas_call(
        functools.partial(far_kernel, leaves=leaves, factor=factor),
        out_shape=shape(probes.shape, F32),
        in_specs=[smem] * 4 + [vmem] * 7,
        out_specs=vmem,
        scratch_shapes=[
            vm((3 * leaves, FEATURES, 128), F32),
            vm((leaves, FEATURES, 128), F32),
            vm((3 * leaves, 8, 128), F32),
            vm((56, FEATURES, 128), F32),
            vm((56, FEATURES, 128), F32),
            vm((nodes // 2, 8, 128), F32),
            vm((nodes // 4, 8, 128), F32),
        ],
        compiler_params=params,
        name="far",
    )(far_list, coarse_list, counts, me, payload, pay2, low2, high2, box8, roots, center)
    first = jnp.where(half == 0, mine, back)
    second = jnp.where(half == 0, back, mine)
    near = jnp.concatenate([first, second], axis=0)
    return jnp.where(slot < counts[:, None, None], near + far, 0.0)


def solution(mesh):
    return jax.shard_map(
        local,
        mesh=mesh,
        in_specs=(
            P("space", None, None),
            P("space", "probe", None),
            P("space"),
            P("space", None),
            P("space", None),
            P(),
            P("space", None, None),
            P(),
        ),
        out_specs=P("space", "probe", None),
        check_vma=False,
    )
```

```python
import functools

import jax
import jax.numpy as jnp
from jax import lax
from jax.experimental import pallas as pl
from jax.experimental.pallas import tpu as pltpu
from jax.sharding import PartitionSpec as P

F32 = jnp.float32
BF16 = jnp.bfloat16
LOG2E = 1.4426950408889634
LN2 = 0.6931471805599453
SCALE = LOG2E * 1.7320508075688772 / 2.0
SLOPE = 0.5 / (LOG2E * LOG2E)
TINY = 1e-30
FEATURES = 48
UNITS = 8
ACROSS = False
COPIES = 8
CN = (((0,), (0,)), ((), ()))
NT = (((1,), (1,)), ((), ()))
NN = (((1,), (0,)), ((), ()))


def dot(left, right, dims):
    return lax.dot_general(left, right, dims, preferred_element_type=F32)


def split(value):
    high = value.astype(BF16)
    return high, (value - high.astype(F32)).astype(BF16)


def stacked(value):
    high = value.astype(BF16).astype(F32)
    return jnp.concatenate([high, value - high], axis=0).astype(BF16)


def exact_dot(left, right, dims):
    rows = left.shape[0]
    high, low = split(right)
    both = stacked(left)
    total = dot(both, high, dims) + dot(both, low, dims)
    return total[:rows] + total[rows:]


def small_dot(small, panel):
    high, low = split(panel)
    both = stacked(small)
    return dot(high, both, NT) + dot(low, both, NT)


def joined(columns):
    rows = columns.T
    return rows[0:8] + rows[8:16]


def slope_of(u):
    u = jnp.maximum(u, TINY)
    return u * jnp.exp2(-(u * lax.rsqrt(u)))


def value_of(u):
    u = jnp.maximum(u, TINY)
    w = u * lax.rsqrt(u)
    return (1.0 + LN2 * w) * jnp.exp2(-w)


def pieces(value):
    high = value.astype(BF16).astype(F32)
    rest = value - high
    middle = rest.astype(BF16).astype(F32)
    return high, middle, rest - middle


def features(rows, center, source, target):
    row = lax.broadcasted_iota(jnp.int32, rows.shape, 0)
    scaled = jnp.where(row < 3, (rows - center) * SCALE, 0.0)
    norm = jnp.sum(scaled * scaled, axis=0, keepdims=True)
    out = []
    if source:
        h, m, l = pieces(jnp.where(row == 3, norm, jnp.where(row == 4, 1.0, scaled)))
        out.append(jnp.concatenate([h, h, m, h, l, m], axis=0))
    if target:
        h, m, l = pieces(jnp.where(row == 3, 1.0, jnp.where(row == 4, norm, -2.0 * scaled)))
        out.append(jnp.concatenate([h, m, h, l, h, m], axis=0))
    return out


def twice(value):
    return jnp.concatenate([value, value], axis=1)


def left_half(shape):
    return lax.broadcasted_iota(jnp.int32, shape, 1) < 64


def store_source(slot, leaf, partner, center, fs, ms):
    (source,) = features(leaf[8:16], center, True, False)
    source = source.astype(BF16)
    lane = lax.broadcasted_iota(jnp.int32, partner.shape, 1).astype(F32)
    other = jnp.where(lane < leaf[11:12], partner, 0.0)
    moments = stacked(jnp.concatenate([leaf[0:8], other], axis=0))
    for b in range(4):
        fs[slot * 4 + b] = source[:, b * 128 : (b + 1) * 128]
        ms[slot * 4 + b] = moments[:, b * 128 : (b + 1) * 128]


def store_target(slot, leaf, center, ft):
    (target,) = features(leaf[8:16], center, False, True)
    target = target.astype(BF16)
    for b in range(2):
        ft[slot * 2 + b] = target[:, b * 256 : (b + 1) * 256]


def build_items(place, target_count, targets, empty, blocks, items):
    def per_leaf(i, n):
        nb = jnp.int32(0)
        for e in range(8):
            ok, slot, count = place(i, e)
            for b in range(4):
                blocks[nb + b] = slot * 4 + b
            nb = nb + jnp.where(ok, (count + 127) >> 7, 0)
        blocks[nb] = empty
        pairs = (nb + 1) >> 1

        def put(q, carry):
            code = (blocks[2 * q] << 9) | blocks[2 * q + 1]
            items[n + q] = code | ((2 * i) << 18)
            items[n + pairs + q] = code | ((2 * i + 1) << 18)
            return carry

        lax.fori_loop(0, pairs, put, 0)
        return n + jnp.where(target_count(i) > 256, 2 * pairs, pairs)

    n = lax.fori_loop(0, targets, per_leaf, jnp.int32(0))
    for t in range(2 * UNITS):
        items[n + t] = (empty << 9) | empty
    return n


def run_items(items, n, fs, ft, ms, acc, slots):
    def distances(code, u):
        left = jnp.concatenate([fs[(code >> 9) & 511], fs[code & 511]], axis=1)
        u[...] = dot(left, ft[code >> 18], CN)

    def contract(code, u):
        high, low = split(slope_of(u[...]))
        m = jnp.concatenate([ms[(code >> 9) & 511], ms[code & 511]], axis=1)
        acc[code >> 18] += dot(m, high, NN) + dot(m, low, NN)

    for s in range(UNITS):
        distances(items[s], slots[s])

    def body(t, carry):
        for s in range(UNITS):
            contract(items[UNITS * t + s], slots[s])
            distances(items[UNITS * (t + 1) + s], slots[s])
        return carry

    lax.fori_loop(0, (n + UNITS - 1) // UNITS, body, 0)


def moments_kernel(payload, leafp, own, center, pay2, dev, fp, *, leaves, factor):
    c = center[:, 0:1]
    (own_target,) = features(own[...], c, False, True)
    own_target = own_target.astype(BF16)[:, :64]

    def body(t, carry):
        for s in range(8):
            i = t * 8 + s
            leaf = payload[i]
            (target,) = features(leaf[8:16], c, False, True)
            (source,) = features(leafp[i], c, True, False)
            fp[i] = source
            basis = value_of(dot(target.astype(BF16), source.astype(BF16)[:, :64], CN))
            pay2[i, 0:8, :] = twice(exact_dot(leaf[0:8], basis, NN) * factor)
            pay2[i, 8:16, :] = leafp[i]
        return carry

    lax.fori_loop(0, leaves // 8, body, 0)
    half = left_half((FEATURES, 128))
    half8 = left_half((8, 128))
    total = jnp.zeros((8, 64), F32)
    for g in range(leaves // 8):
        sources, moments = [], []
        for q in range(4):
            i = 8 * g + 2 * q
            sources.append(jnp.where(half, fp[i], fp[i + 1]).astype(BF16))
            moments.append(jnp.where(half8, pay2[i, 0:8, :], pay2[i + 1, 0:8, :]))
        panel = value_of(dot(jnp.concatenate(sources, axis=1), own_target, CN))
        total = total + exact_dot(jnp.concatenate(moments, axis=1), panel, NN)
    dev[...] = twice(total * (1.0 / 64))


def assign(count_of, leaves, order):
    def tally(i, n):
        return n + (count_of(i) > 256).astype(jnp.int32)

    odd = lax.fori_loop(0, leaves, tally, jnp.int32(0)) & 1

    def deal(i, carry):
        large, taken = carry
        wide_leaf = (count_of(i) > 256).astype(jnp.int32)
        rank = jnp.where(wide_leaf == 1, large, i - large + odd)
        side = rank & 1
        place = jnp.where(side == 1, taken, i - taken)
        order[side * (leaves // 2) + place] = i
        return large + wide_leaf, taken + side

    lax.fori_loop(0, leaves, deal, (jnp.int32(0), jnp.int32(0)))


def clear_empty(empty, fs, ms):
    fs[empty] = jnp.zeros(fs.shape[1:], BF16)
    ms[empty] = jnp.zeros(ms.shape[1:], BF16)


def own_kernel(
    near, counts, me, payload, partner, center, acc,
    fs, ms, ft, blocks, items, order, *slots, leaves, targets,
):
    c = center[:, 0:1]
    assign(lambda i: counts[i], leaves, order)
    first = me[1] * targets

    def prep(t, carry):
        for s in range(2):
            i = 2 * t + s
            store_source(i, payload[i], partner[i], c, fs, ms)
        store_target(t, payload[order[first + t]], c, ft)
        return carry

    lax.fori_loop(0, leaves // 2, prep, 0)
    clear_empty(leaves * 4, fs, ms)
    acc[...] = jnp.zeros_like(acc)

    def place(i, e):
        j = near[order[first + i], e] - me[0] * leaves
        ok = (j >= 0) & (j < leaves)
        slot = jnp.where(ok, j, 0)
        return ok, slot, counts[slot]

    n = build_items(place, lambda i: counts[order[first + i]], targets, leaves * 4, blocks, items)
    run_items(items, n, fs, ft, ms, acc, slots)


def halo_kernel(
    near, counts, me, own, low, high, partner_low, partner_high, center, acc0,
    mine, theirs,
    acc, fs, ms, ft, blocks, items, order, *slots, leaves, targets, factor,
):
    c = center[:, 0:1]
    assign(lambda i: counts[leaves + i], leaves, order)
    first = me[1] * targets

    def prep(i, carry):
        store_source(i, low[i], partner_low[i], c, fs, ms)
        store_source(leaves + i, high[i], partner_high[i], c, fs, ms)
        return carry

    def prep_target(i, carry):
        store_target(i, own[order[first + i]], c, ft)
        return carry

    lax.fori_loop(0, leaves, prep, 0)
    lax.fori_loop(0, targets, prep_target, 0)
    empty = 2 * leaves * 4
    clear_empty(empty, fs, ms)
    acc[...] = acc0[...]

    def place(i, e):
        j = near[order[first + i], e] - (me[0] - 1) * leaves
        ok = (j < leaves) | (j >= 2 * leaves)
        slot = jnp.where(ok, jnp.where(j < leaves, j, j - leaves), 0)
        return ok, slot, counts[jnp.where(ok, j, 0)]

    n = build_items(place, lambda i: counts[leaves + order[first + i]], targets, empty, blocks, items)
    run_items(items, n, fs, ft, ms, acc, slots)
    scale = SLOPE * factor

    def finish(i, carry):
        for b in range(2):
            total = acc[2 * i + b]
            total = (total[0:16] + total[16:32]) * scale
            mine[i, :, b * 256 : (b + 1) * 256] = total[0:8]
            theirs[i, :, b * 256 : (b + 1) * 256] = total[8:16]
        return carry

    lax.fori_loop(0, targets, finish, 0)


def far_sum(lists, count, source_of, moment_of, target, across):
    half = left_half((FEATURES, 128))
    half8 = left_half((8, 128))
    total = jnp.zeros((8, 64), F32)
    for chunk in range(count // 8):
        sources, moments = [], []
        for q in range(4):
            a, b = lists(chunk * 8 + 2 * q), lists(chunk * 8 + 2 * q + 1)
            sources.append(jnp.where(half, source_of(a), source_of(b)).astype(BF16))
            moments.append(jnp.where(half8, moment_of(a), moment_of(b)))
        sources = jnp.concatenate(sources, axis=1)
        moments = jnp.concatenate(moments, axis=1)
        if across:
            columns = small_dot(moments, slope_of(dot(target, sources, CN)))
            total = columns if chunk == 0 else total + columns
        else:
            total = total + exact_dot(moments, slope_of(dot(sources, target, CN)), NN)
    return (joined(total) if across else total) * (SLOPE / 64)


class Strided:
    def __init__(self, array):
        self.array = array

    def __getitem__(self, n):
        return self.array[n * COPIES]


def upper_levels(coarse, me, box8, roots, c, fbs, fbt, pm, qm):
    def prep(t, carry):
        for s in range(8):
            b = 8 * t + s
            fbs[b], fbt[b] = features(box8[b], c, True, True)
        return carry

    lax.fori_loop(0, 7, prep, 0)
    half = left_half((FEATURES, 128))
    half8 = left_half((8, 128))

    def merge(child, parent, moments, out, count):
        def body(t, carry):
            for s in range(8):
                m = t * 8 + s
                source = jnp.where(half, fbs[child + 2 * m], fbs[child + 2 * m + 1]).astype(BF16)
                target = fbt[parent + m].astype(BF16)[:, :64]
                panel = value_of(dot(source, target, CN))
                pair = jnp.where(half8, moments[2 * m], moments[2 * m + 1])
                out[m] = twice(exact_dot(pair, panel, NN) * (1.0 / 64))
            return carry

        lax.fori_loop(0, count // 8, body, 0)

    merge(0, 32, Strided(roots), pm, 16)
    merge(32, 48, pm, qm, 8)
    n = me
    m = n >> 1
    t = n >> 2

    def far(base, row, moments):
        target = fbt[row].astype(BF16)[:, :64]
        return far_sum(
            lambda e: coarse[row, e], 16, lambda b: fbs[base + b], lambda b: moments[b], target, False
        )

    def down(local, source, target):
        panel = value_of(dot(fbs[source].astype(BF16)[:, :64], fbt[target].astype(BF16)[:, :64], CN))
        return exact_dot(local, panel, NN) * (1.0 / 64)

    quad = far(48, 48 + t, qm)
    pair = down(quad, 48 + t, 32 + m) + far(32, 32 + m, pm)
    return down(pair, 32 + m, n) + far(0, n, Strided(roots))


def far_kernel(
    far, coarse, counts, me, own, pay_own, pay_low, pay_high, box8, roots, center,
    out,
    fps, fpt, mps, fbs, fbt, pm, qm, local,
    *, leaves, factor,
):
    c = center[:, 0:1]

    def prep_far(t, carry):
        for s in range(4):
            i = t * 4 + s
            for k, page in enumerate((pay_low, pay_own, pay_high)):
                (fps[k * leaves + i],) = features(page[i, 8:16], c, True, False)
                mps[k * leaves + i] = page[i, 0:8]
            (fpt[i],) = features(pay_own[i, 8:16], c, False, True)
        return carry

    lax.fori_loop(0, leaves // 4, prep_far, 0)
    dev = me[0]
    base = (dev - 1) * leaves

    def gather(t, carry):
        for s in range(4):
            i = t * 4 + s
            target = fpt[i].astype(BF16)[:, :64]
            local[i] = far_sum(
                lambda e: far[i, e] - base, 32, lambda b: fps[b], lambda b: mps[b], target, ACROSS
            )
        return carry

    lax.fori_loop(0, leaves // 4, gather, 0)
    local_dev = upper_levels(coarse, dev, box8, roots, c, fbs, fbt, pm, qm)
    own_source = fbs[dev].astype(BF16)[:, :64]

    def down(t, carry):
        for s in range(8):
            i = t * 8 + s
            target = fpt[i].astype(BF16)[:, :64]
            panel = value_of(dot(own_source, target, CN))
            local[i] += exact_dot(local_dev, panel, NN) * (1.0 / 64)
        return carry

    lax.fori_loop(0, leaves // 8, down, 0)

    def finish(t, carry):
        for s in range(8):
            i = t * 8 + s
            source = fps[leaves + i].astype(BF16)[:, :64]
            (points,) = features(own[i, 8:16], c, False, True)
            basis = value_of(dot(source, points.astype(BF16), CN))
            out[i] = exact_dot(local[i], basis, NN) * factor
        return carry

    lax.fori_loop(0, leaves // 8, finish, 0)


def sum_kernel(counts, me, far, mine, back, out, order, *, leaves):
    assign(lambda i: counts[i], leaves, order)
    half = leaves // 2
    lane = lax.broadcasted_iota(jnp.int32, far.shape[1:], 1)

    def body(t, carry):
        for s in range(4):
            k = 4 * t + s
            for side, part in ((me[1], mine), (1 - me[1], back)):
                i = order[side * half + k]
                out[i] = jnp.where(lane < counts[i], far[i] + part[k], 0.0)
        return carry

    lax.fori_loop(0, half // 4, body, 0)


def cost(microseconds):
    flops = int(microseconds * 1.1e9)
    return pl.CostEstimate(flops=flops, transcendentals=0, bytes_accessed=1 << 20)


def wide(array):
    rows = jnp.concatenate([array, array], axis=2)
    return jnp.pad(rows, ((0, 0), (0, 8 - array.shape[1]), (0, 0)))


def local(points, probes, counts, near_list, far_list, coarse_list, leaf_proxy, box_proxy):
    leaves = points.shape[0]
    size = points.shape[2]
    nodes = lax.axis_size("space")
    device = lax.axis_index("space")
    factor = size ** (-0.5)
    slot = lax.broadcasted_iota(jnp.int32, (leaves, 1, size), 2)
    masked = jnp.where(slot < counts[:, None, None], probes, 0.0)
    count_row = jnp.broadcast_to(counts.astype(F32)[:, None, None], (leaves, 5, size))
    payload = jnp.concatenate([masked, points, count_row], axis=1)
    forward = [(i, i + 1) for i in range(nodes - 1)]
    backward = [(i + 1, i) for i in range(nodes - 1)]
    pairs = [(i, i ^ 1) for i in range(lax.axis_size("probe"))]
    partner = lax.ppermute(probes, "probe", pairs)
    low = lax.ppermute(payload, "space", forward)
    high = lax.ppermute(payload, "space", backward)
    partner_low = lax.ppermute(partner, "space", forward)
    partner_high = lax.ppermute(partner, "space", backward)
    leafp = wide(leaf_proxy)
    box8 = wide(box_proxy)
    center = jnp.broadcast_to(jnp.pad(points[0, :, 0], (0, 5))[:, None], (8, 128))
    own = lax.dynamic_index_in_dim(box8, device, 0, keepdims=False)
    half = lax.axis_index("probe") & 1
    me = jnp.stack([device, half]).astype(jnp.int32)
    params = pltpu.CompilerParams(vmem_limit_bytes=56 << 20)
    vm = pltpu.VMEM
    vmem = pl.BlockSpec(memory_space=vm)
    smem = pl.BlockSpec(memory_space=pltpu.SMEM)
    shape = jax.ShapeDtypeStruct
    pay2, dev = pl.pallas_call(
        functools.partial(moments_kernel, leaves=leaves, factor=factor),
        out_shape=(shape((leaves, 16, 128), F32), shape((8, 128), F32)),
        in_specs=[vmem] * 4,
        out_specs=(vmem, vmem),
        scratch_shapes=[vm((leaves, FEATURES, 128), F32)],
        compiler_params=params,
        cost_estimate=cost(8),
        name="moments",
    )(payload, leafp, own, center)
    low2 = lax.ppermute(pay2, "space", forward)
    high2 = lax.ppermute(pay2, "space", backward)
    copies = jnp.broadcast_to(dev[None], (COPIES, 8, 128))
    roots = lax.all_gather(copies, "space", axis=0, tiled=True)
    targets = leaves // 2

    def work(blocks):
        return (
            [
                vm((blocks, FEATURES, 128), BF16),
                vm((blocks, 32, 128), BF16),
                vm((targets * 2, FEATURES, 256), BF16),
                pltpu.SMEM((48,), jnp.int32),
                pltpu.SMEM((targets * 32 + 64,), jnp.int32),
                pltpu.SMEM((leaves,), jnp.int32),
            ]
            + [vm((256, 256), F32)] * UNITS
        )

    acc0 = pl.pallas_call(
        functools.partial(own_kernel, leaves=leaves, targets=targets),
        out_shape=shape((targets * 2, 32, 256), F32),
        in_specs=[smem] * 3 + [vmem] * 3,
        out_specs=vmem,
        scratch_shapes=work(leaves * 4 + 1),
        compiler_params=params,
        cost_estimate=cost(28),
        name="near_own",
    )(near_list, counts, me, payload, partner, center)
    low, high, low2, high2 = lax.optimization_barrier((low, high, low2, high2))
    counts3 = jnp.concatenate(
        [low[:, 11, 0].astype(jnp.int32), counts, high[:, 11, 0].astype(jnp.int32)]
    )
    mine, theirs = pl.pallas_call(
        functools.partial(halo_kernel, leaves=leaves, targets=targets, factor=factor),
        out_shape=(shape((targets, 8, size), F32),) * 2,
        in_specs=[smem] * 3 + [vmem] * 7,
        out_specs=(vmem, vmem),
        scratch_shapes=[vm((targets * 2, 32, 256), F32)] + work(2 * leaves * 4 + 1),
        compiler_params=params,
        cost_estimate=cost(30),
        name="near_halo",
    )(near_list, counts3, me, payload, low, high, partner_low, partner_high, center, acc0)
    back = lax.ppermute(theirs, "probe", pairs)
    far = pl.pallas_call(
        functools.partial(far_kernel, leaves=leaves, factor=factor),
        out_shape=shape(probes.shape, F32),
        in_specs=[smem] * 4 + [vmem] * 7,
        out_specs=vmem,
        scratch_shapes=[
            vm((3 * leaves, FEATURES, 128), F32),
            vm((leaves, FEATURES, 128), F32),
            vm((3 * leaves, 8, 128), F32),
            vm((56, FEATURES, 128), F32),
            vm((56, FEATURES, 128), F32),
            vm((nodes // 2, 8, 128), F32),
            vm((nodes // 4, 8, 128), F32),
            vm((leaves, 8, 64), F32),
        ],
        compiler_params=params,
        cost_estimate=cost(30),
        name="far",
    )(far_list, coarse_list, counts, me, payload, pay2, low2, high2, box8, roots, center)
    return pl.pallas_call(
        functools.partial(sum_kernel, leaves=leaves),
        out_shape=shape(probes.shape, F32),
        in_specs=[smem] * 2 + [vmem] * 3,
        out_specs=vmem,
        scratch_shapes=[pltpu.SMEM((leaves,), jnp.int32)],
        compiler_params=params,
        name="sum",
    )(counts, me, far, mine, back)


def solution(mesh):
    return jax.shard_map(
        local,
        mesh=mesh,
        in_specs=(
            P("space", None, None),
            P("space", "probe", None),
            P("space"),
            P("space", None),
            P("space", None),
            P(),
            P("space", None, None),
            P(),
        ),
        out_specs=P("space", "probe", None),
        check_vma=False,
    )
```

```python
import functools

import jax
import jax.numpy as jnp
from jax import lax
from jax.experimental import pallas as pl
from jax.experimental.pallas import tpu as pltpu
from jax.sharding import PartitionSpec as P

F32 = jnp.float32
BF16 = jnp.bfloat16
LOG2E = 1.4426950408889634
LN2 = 0.6931471805599453
SCALE = LOG2E * 1.7320508075688772 / 2.0
SLOPE = 0.5 / (LOG2E * LOG2E)
TINY = 1e-30
FEATURES = 48
UNITS = 8
ACROSS = False
CN = (((0,), (0,)), ((), ()))
NT = (((1,), (1,)), ((), ()))
NN = (((1,), (0,)), ((), ()))


def dot(left, right, dims):
    return lax.dot_general(left, right, dims, preferred_element_type=F32)


def split(value):
    high = value.astype(BF16)
    return high, (value - high.astype(F32)).astype(BF16)


def stacked(value):
    high = value.astype(BF16).astype(F32)
    return jnp.concatenate([high, value - high], axis=0).astype(BF16)


def exact_dot(left, right, dims):
    rows = left.shape[0]
    high, low = split(right)
    both = stacked(left)
    total = dot(both, high, dims) + dot(both, low, dims)
    return total[:rows] + total[rows:]


def small_dot(small, panel):
    high, low = split(panel)
    both = stacked(small)
    return dot(high, both, NT) + dot(low, both, NT)


def joined(columns):
    rows = columns.T
    return rows[0:8] + rows[8:16]


def slope_of(u):
    u = jnp.maximum(u, TINY)
    return u * jnp.exp2(-(u * lax.rsqrt(u)))


def value_of(u):
    u = jnp.maximum(u, TINY)
    w = u * lax.rsqrt(u)
    return (1.0 + LN2 * w) * jnp.exp2(-w)


def pieces(value):
    high = value.astype(BF16).astype(F32)
    rest = value - high
    middle = rest.astype(BF16).astype(F32)
    return high, middle, rest - middle


def features(rows, center, source, target):
    row = lax.broadcasted_iota(jnp.int32, rows.shape, 0)
    scaled = jnp.where(row < 3, (rows - center) * SCALE, 0.0)
    norm = jnp.sum(scaled * scaled, axis=0, keepdims=True)
    out = []
    if source:
        h, m, l = pieces(jnp.where(row == 3, norm, jnp.where(row == 4, 1.0, scaled)))
        out.append(jnp.concatenate([h, h, m, h, l, m], axis=0))
    if target:
        h, m, l = pieces(jnp.where(row == 3, 1.0, jnp.where(row == 4, norm, -2.0 * scaled)))
        out.append(jnp.concatenate([h, m, h, l, h, m], axis=0))
    return out


def twice(value):
    return jnp.concatenate([value, value], axis=1)


def left_half(shape):
    return lax.broadcasted_iota(jnp.int32, shape, 1) < 64


def lanes_of(page, i, start):
    return jnp.concatenate([page[i, 16 * b + start : 16 * b + start + 8, :] for b in range(4)], axis=1)


def center_of(page):
    return page[0, 8:16, 0:1]


def store_source(slot, page, i, partner, center, fs, ms):
    rows = lanes_of(page, i, 8)
    (source,) = features(rows, center, True, False)
    source = source.astype(BF16)
    lane = lax.broadcasted_iota(jnp.int32, partner.shape, 1).astype(F32)
    other = jnp.where(lane < rows[3:4], partner, 0.0)
    moments = stacked(jnp.concatenate([lanes_of(page, i, 0), other], axis=0))
    for b in range(4):
        fs[slot * 4 + b] = source[:, b * 128 : (b + 1) * 128]
        ms[slot * 4 + b] = moments[:, b * 128 : (b + 1) * 128]


def store_target(slot, page, i, center, ft):
    (target,) = features(lanes_of(page, i, 8), center, False, True)
    target = target.astype(BF16)
    for b in range(2):
        ft[slot * 2 + b] = target[:, b * 256 : (b + 1) * 256]


def build_items(place, target_count, targets, empty, blocks, items):
    def per_leaf(i, n):
        nb = jnp.int32(0)
        for e in range(8):
            ok, slot, count = place(i, e)
            for b in range(4):
                blocks[nb + b] = slot * 4 + b
            nb = nb + jnp.where(ok, (count + 127) >> 7, 0)
        blocks[nb] = empty
        pairs = (nb + 1) >> 1

        def put(q, carry):
            code = (blocks[2 * q] << 9) | blocks[2 * q + 1]
            items[n + q] = code | ((2 * i) << 18)
            items[n + pairs + q] = code | ((2 * i + 1) << 18)
            return carry

        lax.fori_loop(0, pairs, put, 0)
        return n + jnp.where(target_count(i) > 256, 2 * pairs, pairs)

    n = lax.fori_loop(0, targets, per_leaf, jnp.int32(0))
    for t in range(2 * UNITS):
        items[n + t] = (empty << 9) | empty
    return n


def run_items(items, n, fs, ft, ms, acc, slots):
    def distances(code, u):
        left = jnp.concatenate([fs[(code >> 9) & 511], fs[code & 511]], axis=1)
        u[...] = dot(left, ft[code >> 18], CN)

    def contract(code, u):
        high, low = split(slope_of(u[...]))
        m = jnp.concatenate([ms[(code >> 9) & 511], ms[code & 511]], axis=1)
        acc[code >> 18] += dot(m, high, NN) + dot(m, low, NN)

    for s in range(UNITS):
        distances(items[s], slots[s])

    def body(t, carry):
        for s in range(UNITS):
            contract(items[UNITS * t + s], slots[s])
            distances(items[UNITS * (t + 1) + s], slots[s])
        return carry

    lax.fori_loop(0, (n + UNITS - 1) // UNITS, body, 0)


def rows_of(planes, i, extra):
    rows = [planes[d, pl.ds(i, 1), :] for d in range(3)]
    width = rows[0].shape[1]
    return jnp.concatenate(
        rows + [jnp.full((1, width), extra, F32), jnp.zeros((4, width), F32)], axis=0
    )


def moments_kernel(counts, me, probes, points, leafp, boxp, page, dev, fp, *, leaves, factor):
    c = rows_of(points, 0, 0.0)[:, 0:1]
    (own_target,) = features(rows_of(boxp, me[0], 0.0), c, False, True)
    own_target = own_target.astype(BF16)
    lane = lax.broadcasted_iota(jnp.int32, probes.shape[1:], 1)

    def body(t, carry):
        for s in range(8):
            i = t * 8 + s
            count = counts[i]
            masked = jnp.where(lane < count, probes[i], 0.0)
            rows = rows_of(points, i, count.astype(F32))
            for b in range(4):
                page[i, 16 * b : 16 * b + 8, :] = masked[:, b * 128 : (b + 1) * 128]
                page[i, 16 * b + 8 : 16 * b + 16, :] = rows[:, b * 128 : (b + 1) * 128]
            proxies = twice(rows_of(leafp, i, 0.0))
            (target,) = features(rows, c, False, True)
            (source,) = features(proxies, c, True, False)
            fp[i] = source
            basis = value_of(dot(target.astype(BF16), source.astype(BF16)[:, :64], CN))
            page[i, 64:72, :] = twice(exact_dot(masked, basis, NN) * factor)
            page[i, 72:80, :] = proxies
        return carry

    lax.fori_loop(0, leaves // 8, body, 0)
    half = left_half((FEATURES, 128))
    half8 = left_half((8, 128))
    total = jnp.zeros((8, 64), F32)
    for g in range(leaves // 8):
        sources, moments = [], []
        for q in range(4):
            i = 8 * g + 2 * q
            sources.append(jnp.where(half, fp[i], fp[i + 1]).astype(BF16))
            moments.append(jnp.where(half8, page[i, 64:72, :], page[i + 1, 64:72, :]))
        panel = value_of(dot(jnp.concatenate(sources, axis=1), own_target, CN))
        total = total + exact_dot(jnp.concatenate(moments, axis=1), panel, NN)
    dev[...] = twice(total * (1.0 / 64))


def assign(count_of, leaves, order):
    def tally(i, n):
        return n + (count_of(i) > 256).astype(jnp.int32)

    odd = lax.fori_loop(0, leaves, tally, jnp.int32(0)) & 1

    def deal(i, carry):
        large, taken = carry
        wide_leaf = (count_of(i) > 256).astype(jnp.int32)
        rank = jnp.where(wide_leaf == 1, large, i - large + odd)
        side = rank & 1
        place = jnp.where(side == 1, taken, i - taken)
        order[side * (leaves // 2) + place] = i
        return large + wide_leaf, taken + side

    lax.fori_loop(0, leaves, deal, (jnp.int32(0), jnp.int32(0)))


def clear_empty(empty, fs, ms):
    fs[empty] = jnp.zeros(fs.shape[1:], BF16)
    ms[empty] = jnp.zeros(ms.shape[1:], BF16)


def own_kernel(
    near, counts, me, page, partner, acc,
    fs, ms, ft, blocks, items, order, *slots, leaves, targets,
):
    c = center_of(page)
    assign(lambda i: counts[i], leaves, order)
    first = me[1] * targets

    def prep(t, carry):
        for s in range(2):
            i = 2 * t + s
            store_source(i, page, i, partner[i], c, fs, ms)
        store_target(t, page, order[first + t], c, ft)
        return carry

    lax.fori_loop(0, leaves // 2, prep, 0)
    clear_empty(leaves * 4, fs, ms)
    acc[...] = jnp.zeros_like(acc)

    def place(i, e):
        j = near[e, order[first + i]] - me[0] * leaves
        ok = (j >= 0) & (j < leaves)
        slot = jnp.where(ok, j, 0)
        return ok, slot, counts[slot]

    n = build_items(place, lambda i: counts[order[first + i]], targets, leaves * 4, blocks, items)
    run_items(items, n, fs, ft, ms, acc, slots)


def halo_kernel(
    near, counts, me, own, low, high, partner_low, partner_high, acc0,
    mine, theirs,
    acc, fs, ms, ft, blocks, items, order, *slots, leaves, targets, factor,
):
    c = center_of(own)
    assign(lambda i: counts[leaves + i], leaves, order)
    first = me[1] * targets

    def prep(i, carry):
        store_source(i, low, i, partner_low[i], c, fs, ms)
        store_source(leaves + i, high, i, partner_high[i], c, fs, ms)
        return carry

    def prep_target(i, carry):
        store_target(i, own, order[first + i], c, ft)
        return carry

    lax.fori_loop(0, leaves, prep, 0)
    lax.fori_loop(0, targets, prep_target, 0)
    empty = 2 * leaves * 4
    clear_empty(empty, fs, ms)
    acc[...] = acc0[...]

    def place(i, e):
        j = near[e, order[first + i]] - (me[0] - 1) * leaves
        ok = (j < leaves) | (j >= 2 * leaves)
        slot = jnp.where(ok, jnp.where(j < leaves, j, j - leaves), 0)
        return ok, slot, counts[jnp.where(ok, j, 0)]

    n = build_items(place, lambda i: counts[leaves + order[first + i]], targets, empty, blocks, items)
    run_items(items, n, fs, ft, ms, acc, slots)
    scale = SLOPE * factor

    def finish(i, carry):
        for b in range(2):
            total = acc[2 * i + b]
            total = (total[0:16] + total[16:32]) * scale
            mine[i, :, b * 256 : (b + 1) * 256] = total[0:8]
            theirs[i, :, b * 256 : (b + 1) * 256] = total[8:16]
        return carry

    lax.fori_loop(0, targets, finish, 0)


def far_sum(lists, count, source_of, moment_of, target, across):
    half = left_half((FEATURES, 128))
    half8 = left_half((8, 128))
    total = jnp.zeros((8, 64), F32)
    for chunk in range(count // 8):
        sources, moments = [], []
        for q in range(4):
            a, b = lists(chunk * 8 + 2 * q), lists(chunk * 8 + 2 * q + 1)
            sources.append(jnp.where(half, source_of(a), source_of(b)).astype(BF16))
            moments.append(jnp.where(half8, moment_of(a), moment_of(b)))
        sources = jnp.concatenate(sources, axis=1)
        moments = jnp.concatenate(moments, axis=1)
        if across:
            columns = small_dot(moments, slope_of(dot(target, sources, CN)))
            total = columns if chunk == 0 else total + columns
        else:
            total = total + exact_dot(moments, slope_of(dot(sources, target, CN)), NN)
    return (joined(total) if across else total) * (SLOPE / 64)


class Relative:
    def __init__(self, array, me):
        self.array, self.me = array, me

    def __getitem__(self, n):
        return self.array[n ^ self.me]


def upper_levels(coarse, me, box8, roots, c, fbs, fbt, pm, qm):
    def prep(t, carry):
        for s in range(8):
            b = 8 * t + s
            fbs[b], fbt[b] = features(twice(rows_of(box8, b, 0.0)), c, True, True)
        return carry

    lax.fori_loop(0, 7, prep, 0)
    half = left_half((FEATURES, 128))
    half8 = left_half((8, 128))

    def merge(child, parent, moments, out, count):
        def body(t, carry):
            for s in range(8):
                m = t * 8 + s
                source = jnp.where(half, fbs[child + 2 * m], fbs[child + 2 * m + 1]).astype(BF16)
                target = fbt[parent + m].astype(BF16)[:, :64]
                panel = value_of(dot(source, target, CN))
                pair = jnp.where(half8, moments[2 * m], moments[2 * m + 1])
                out[m] = twice(exact_dot(pair, panel, NN) * (1.0 / 64))
            return carry

        lax.fori_loop(0, count // 8, body, 0)

    merge(0, 32, Relative(roots, me), pm, 16)
    merge(32, 48, pm, qm, 8)
    n = me
    m = n >> 1
    t = n >> 2

    def far(base, row, moments):
        target = fbt[row].astype(BF16)[:, :64]
        return far_sum(
            lambda e: coarse[e, row], 16, lambda b: fbs[base + b], lambda b: moments[b], target, False
        )

    def down(local, source, target):
        panel = value_of(dot(fbs[source].astype(BF16)[:, :64], fbt[target].astype(BF16)[:, :64], CN))
        return exact_dot(local, panel, NN) * (1.0 / 64)

    quad = far(48, 48 + t, qm)
    pair = down(quad, 48 + t, 32 + m) + far(32, 32 + m, pm)
    return down(pair, 32 + m, n) + far(0, n, Relative(roots, me))


def far_kernel(
    far, coarse, me, own, low, high, box8, *rest, leaves, factor
):
    *parts, out, fps, fpt, mps, fbs, fbt, pm, qm, local, roots = rest
    roots[0] = parts[0][0]
    for part in parts[1:]:
        count = part.shape[0]
        roots[count : 2 * count] = part[...]
    c = center_of(own)

    def prep_far(t, carry):
        for s in range(4):
            i = t * 4 + s
            for k, (page, at) in enumerate(((low, 0), (own, 64), (high, 0))):
                (fps[k * leaves + i],) = features(page[i, at + 8 : at + 16], c, True, False)
                mps[k * leaves + i] = page[i, at : at + 8]
            (fpt[i],) = features(own[i, 72:80], c, False, True)
        return carry

    lax.fori_loop(0, leaves // 4, prep_far, 0)
    dev = me[0]
    base = (dev - 1) * leaves

    def gather(t, carry):
        for s in range(4):
            i = t * 4 + s
            target = fpt[i].astype(BF16)[:, :64]
            local[i] = far_sum(
                lambda e: far[i, e] - base, 32, lambda b: fps[b], lambda b: mps[b], target, ACROSS
            )
        return carry

    lax.fori_loop(0, leaves // 4, gather, 0)
    local_dev = upper_levels(coarse, dev, box8, roots, c, fbs, fbt, pm, qm)
    own_source = fbs[dev].astype(BF16)[:, :64]

    def down(t, carry):
        for s in range(8):
            i = t * 8 + s
            target = fpt[i].astype(BF16)[:, :64]
            panel = value_of(dot(own_source, target, CN))
            local[i] += exact_dot(local_dev, panel, NN) * (1.0 / 64)
        return carry

    lax.fori_loop(0, leaves // 8, down, 0)

    def finish(t, carry):
        for s in range(8):
            i = t * 8 + s
            source = fps[leaves + i].astype(BF16)[:, :64]
            (points,) = features(lanes_of(own, i, 8), c, False, True)
            basis = value_of(dot(source, points.astype(BF16), CN))
            out[i] = exact_dot(local[i], basis, NN) * factor
        return carry

    lax.fori_loop(0, leaves // 8, finish, 0)


def sum_kernel(counts, me, far, mine, back, out, order, *, leaves):
    assign(lambda i: counts[i], leaves, order)
    half = leaves // 2
    lane = lax.broadcasted_iota(jnp.int32, far.shape[1:], 1)

    def body(t, carry):
        for s in range(4):
            k = 4 * t + s
            for side, part in ((me[1], mine), (1 - me[1], back)):
                i = order[side * half + k]
                out[i] = jnp.where(lane < counts[i], far[i] + part[k], 0.0)
        return carry

    lax.fori_loop(0, half // 4, body, 0)


def cost(microseconds):
    flops = int(microseconds * 1.1e9)
    return pl.CostEstimate(flops=flops, transcendentals=0, bytes_accessed=1 << 20)


def local(points, probes, counts, near_list, far_list, coarse_list, leaf_proxy, box_proxy):
    leaves = points.shape[0]
    size = points.shape[2]
    nodes = lax.axis_size("space")
    device = lax.axis_index("space")
    factor = size ** (-0.5)
    half = lax.axis_index("probe") & 1
    me = jnp.stack([device, half]).astype(jnp.int32)
    points = jnp.transpose(points, (1, 0, 2))
    leafp = jnp.transpose(leaf_proxy, (1, 0, 2))
    boxp = jnp.transpose(box_proxy, (1, 0, 2))
    near = near_list.T
    forward = [(i, i + 1) for i in range(nodes - 1)]
    backward = [(i + 1, i) for i in range(nodes - 1)]
    pairs = [(i, i ^ 1) for i in range(lax.axis_size("probe"))]
    partner = lax.ppermute(probes, "probe", pairs)
    params = pltpu.CompilerParams(vmem_limit_bytes=56 << 20)
    vm = pltpu.VMEM
    vmem = pl.BlockSpec(memory_space=vm)
    smem = pl.BlockSpec(memory_space=pltpu.SMEM)
    shape = jax.ShapeDtypeStruct
    page, dev = pl.pallas_call(
        functools.partial(moments_kernel, leaves=leaves, factor=factor),
        out_shape=(shape((leaves, 80, 128), F32), shape((8, 128), F32)),
        in_specs=[smem] * 2 + [vmem] * 4,
        out_specs=(vmem, vmem),
        scratch_shapes=[vm((leaves, FEATURES, 128), F32)],
        compiler_params=params,
        cost_estimate=cost(8),
        name="moments",
    )(counts, me, probes, points, leafp, boxp)
    low = lax.ppermute(page, "space", forward)
    high = lax.ppermute(page, "space", backward)
    parts = [dev[None]]
    for bit in range(nodes.bit_length() - 1):
        swap = [(i, i ^ (1 << bit)) for i in range(nodes)]
        parts.append(lax.ppermute(jnp.concatenate(parts, axis=0), "space", swap))
    partner_low = lax.ppermute(partner, "space", forward)
    partner_high = lax.ppermute(partner, "space", backward)
    targets = leaves // 2

    def work(blocks):
        return (
            [
                vm((blocks, FEATURES, 128), BF16),
                vm((blocks, 32, 128), BF16),
                vm((targets * 2, FEATURES, 256), BF16),
                pltpu.SMEM((48,), jnp.int32),
                pltpu.SMEM((targets * 32 + 64,), jnp.int32),
                pltpu.SMEM((leaves,), jnp.int32),
            ]
            + [vm((256, 256), F32)] * UNITS
        )

    page, *parts = lax.optimization_barrier((page, *parts))
    acc0 = pl.pallas_call(
        functools.partial(own_kernel, leaves=leaves, targets=targets),
        out_shape=shape((targets * 2, 32, 256), F32),
        in_specs=[smem] * 3 + [vmem] * 2,
        out_specs=vmem,
        scratch_shapes=work(leaves * 4 + 1),
        compiler_params=params,
        cost_estimate=cost(28),
        name="near_own",
    )(near, counts, me, page, partner)
    counts3 = jnp.concatenate(
        [low[:, 11, 0].astype(jnp.int32), counts, high[:, 11, 0].astype(jnp.int32)]
    )
    mine, theirs = pl.pallas_call(
        functools.partial(halo_kernel, leaves=leaves, targets=targets, factor=factor),
        out_shape=(shape((targets, 8, size), F32),) * 2,
        in_specs=[smem] * 3 + [vmem] * 6,
        out_specs=(vmem, vmem),
        scratch_shapes=[vm((targets * 2, 32, 256), F32)] + work(2 * leaves * 4 + 1),
        compiler_params=params,
        cost_estimate=cost(30),
        name="near_halo",
    )(near, counts3, me, page, low, high, partner_low, partner_high, acc0)
    back = lax.ppermute(theirs, "probe", pairs)
    whole = lambda dims: pl.BlockSpec(dims, lambda i: (0,) * len(dims))
    tail = pl.BlockSpec((leaves, 16, 128), lambda i: (0, 4, 0))
    far = pl.pallas_call(
        functools.partial(far_kernel, leaves=leaves, factor=factor),
        out_shape=shape(probes.shape, F32),
        grid=(1,),
        in_specs=[smem] * 3 + [whole(page.shape), tail, tail, whole(boxp.shape)]
        + [whole(part.shape) for part in parts],
        out_specs=whole(probes.shape),
        scratch_shapes=[
            vm((3 * leaves, FEATURES, 128), F32),
            vm((leaves, FEATURES, 128), F32),
            vm((3 * leaves, 8, 128), F32),
            vm((56, FEATURES, 128), F32),
            vm((56, FEATURES, 128), F32),
            vm((nodes // 2, 8, 128), F32),
            vm((nodes // 4, 8, 128), F32),
            vm((leaves, 8, 64), F32),
            vm((nodes, 8, 128), F32),
        ],
        compiler_params=params,
        cost_estimate=cost(30),
        name="far",
    )(far_list, coarse_list.T, me, page, low, high, boxp, *parts)
    return pl.pallas_call(
        functools.partial(sum_kernel, leaves=leaves),
        out_shape=shape(probes.shape, F32),
        in_specs=[smem] * 2 + [vmem] * 3,
        out_specs=vmem,
        scratch_shapes=[pltpu.SMEM((leaves,), jnp.int32)],
        compiler_params=params,
        name="sum",
    )(counts, me, far, mine, back)


def solution(mesh):
    return jax.shard_map(
        local,
        mesh=mesh,
        in_specs=(
            P("space", None, None),
            P("space", "probe", None),
            P("space"),
            P("space", None),
            P("space", None),
            P(),
            P("space", None, None),
            P(),
        ),
        out_specs=P("space", "probe", None),
        check_vma=False,
    )
```

```python
import functools

import jax
import jax.numpy as jnp
from jax import lax
from jax.experimental import pallas as pl
from jax.experimental.pallas import tpu as pltpu
from jax.sharding import PartitionSpec as P

F32 = jnp.float32
BF16 = jnp.bfloat16
LOG2E = 1.4426950408889634
LN2 = 0.6931471805599453
SCALE = LOG2E * 1.7320508075688772 / 2.0
SLOPE = 0.5 / (LOG2E * LOG2E)
TINY = 1e-30
FEATURES = 48
UNITS = 8
CN = (((0,), (0,)), ((), ()))
NT = (((1,), (1,)), ((), ()))
NN = (((1,), (0,)), ((), ()))


def dot(left, right, dims):
    return lax.dot_general(left, right, dims, preferred_element_type=F32)


def split(value):
    high = value.astype(BF16)
    return high, (value - high.astype(F32)).astype(BF16)


def stacked(value):
    high = value.astype(BF16).astype(F32)
    return jnp.concatenate([high, value - high], axis=0).astype(BF16)


def exact_dot(left, right, dims):
    rows = left.shape[0]
    high, low = split(right)
    both = stacked(left)
    total = dot(both, high, dims) + dot(both, low, dims)
    return total[:rows] + total[rows:]


def slope_of(u):
    u = jnp.maximum(u, TINY)
    return u * jnp.exp2(-(u * lax.rsqrt(u)))


def value_of(u):
    u = jnp.maximum(u, TINY)
    w = u * lax.rsqrt(u)
    return (1.0 + LN2 * w) * jnp.exp2(-w)


def pieces(value):
    high = value.astype(BF16).astype(F32)
    rest = value - high
    middle = rest.astype(BF16).astype(F32)
    return high, middle, rest - middle


def features(rows, center, source, target):
    row = lax.broadcasted_iota(jnp.int32, rows.shape, 0)
    scaled = jnp.where(row < 3, (rows - center) * SCALE, 0.0)
    norm = jnp.sum(scaled * scaled, axis=0, keepdims=True)
    out = []
    if source:
        h, m, l = pieces(jnp.where(row == 3, norm, jnp.where(row == 4, 1.0, scaled)))
        out.append(jnp.concatenate([h, h, m, h, l, m], axis=0))
    if target:
        h, m, l = pieces(jnp.where(row == 3, 1.0, jnp.where(row == 4, norm, -2.0 * scaled)))
        out.append(jnp.concatenate([h, m, h, l, h, m], axis=0))
    return out


def twice(value):
    return jnp.concatenate([value, value], axis=1)


def left_half(shape):
    return lax.broadcasted_iota(jnp.int32, shape, 1) < 64


def lanes_of(page, i, start):
    return jnp.concatenate([page[i, 16 * b + start : 16 * b + start + 8, :] for b in range(4)], axis=1)


def center_of(page):
    return page[0, 8:16, 0:1]


def store_source(slot, page, i, partner, center, fs, ms):
    rows = lanes_of(page, i, 8)
    (source,) = features(rows, center, True, False)
    source = source.astype(BF16)
    lane = lax.broadcasted_iota(jnp.int32, partner.shape, 1).astype(F32)
    other = jnp.where(lane < rows[3:4], partner, 0.0)
    moments = stacked(jnp.concatenate([lanes_of(page, i, 0), other], axis=0))
    for b in range(4):
        fs[slot * 4 + b] = source[:, b * 128 : (b + 1) * 128]
        ms[slot * 4 + b] = moments[:, b * 128 : (b + 1) * 128]


def store_target(slot, page, i, center, ft):
    (target,) = features(lanes_of(page, i, 8), center, False, True)
    target = target.astype(BF16)
    for b in range(2):
        ft[slot * 2 + b] = target[:, b * 256 : (b + 1) * 256]


def build_items(place, target_count, targets, empty, blocks, items):
    def per_leaf(i, n):
        nb = jnp.int32(0)
        for e in range(8):
            ok, slot, count = place(i, e)
            for b in range(4):
                blocks[nb + b] = slot * 4 + b
            nb = nb + jnp.where(ok, (count + 127) >> 7, 0)
        blocks[nb] = empty
        pairs = (nb + 1) >> 1

        def put(q, carry):
            code = (blocks[2 * q] << 9) | blocks[2 * q + 1]
            items[n + q] = code | ((2 * i) << 18)
            items[n + pairs + q] = code | ((2 * i + 1) << 18)
            return carry

        lax.fori_loop(0, pairs, put, 0)
        return n + jnp.where(target_count(i) > 256, 2 * pairs, pairs)

    n = lax.fori_loop(0, targets, per_leaf, jnp.int32(0))
    for t in range(2 * UNITS):
        items[n + t] = (empty << 9) | empty
    return n


def run_items(items, n, fs, ft, ms, acc, slots):
    def distances(code, u):
        left = jnp.concatenate([fs[(code >> 9) & 511], fs[code & 511]], axis=1)
        u[...] = dot(left, ft[code >> 18], CN)

    def contract(code, u):
        high, low = split(slope_of(u[...]))
        m = jnp.concatenate([ms[(code >> 9) & 511], ms[code & 511]], axis=1)
        acc[code >> 18] += dot(m, high, NN) + dot(m, low, NN)

    for s in range(UNITS):
        distances(items[s], slots[s])

    def body(t, carry):
        for s in range(UNITS):
            contract(items[UNITS * t + s], slots[s])
            distances(items[UNITS * (t + 1) + s], slots[s])
        return carry

    lax.fori_loop(0, (n + UNITS - 1) // UNITS, body, 0)


def rows_of(planes, i, extra):
    rows = [planes[d, pl.ds(i, 1), :] for d in range(3)]
    width = rows[0].shape[1]
    return jnp.concatenate(
        rows + [jnp.full((1, width), extra, F32), jnp.zeros((4, width), F32)], axis=0
    )


def moments_kernel(counts, me, probes, points, leafp, boxp, page, dev, fp, *, leaves, factor):
    c = rows_of(points, 0, 0.0)[:, 0:1]
    (own_target,) = features(rows_of(boxp, me[0], 0.0), c, False, True)
    own_target = own_target.astype(BF16)
    lane = lax.broadcasted_iota(jnp.int32, probes.shape[1:], 1)

    def prep(i):
        count = counts[i]
        masked = jnp.where(lane < count, probes[i], 0.0)
        rows = rows_of(points, i, count.astype(F32))
        for b in range(4):
            page[i, 16 * b : 16 * b + 8, :] = masked[:, b * 128 : (b + 1) * 128]
            page[i, 16 * b + 8 : 16 * b + 16, :] = rows[:, b * 128 : (b + 1) * 128]
        proxies = twice(rows_of(leafp, i, 0.0))
        page[i, 72:80, :] = proxies
        (target,) = features(rows, c, False, True)
        (fp[i],) = features(proxies, c, True, False)
        return masked, target.astype(BF16)

    def body(t, carry):
        for s in range(4):
            i = t * 8 + 2 * s
            (left, left_points), (right, right_points) = prep(i), prep(i + 1)
            both = jnp.concatenate([left_points, right_points], axis=0)
            basis = value_of(dot(both, shared(fp[i], fp[i + 1]), CN))
            pair = exact_dot(jnp.concatenate([left, right], axis=0), basis, NN) * factor
            page[i, 64:72, :] = twice(pair[0:8, 0:64])
            page[i + 1, 64:72, :] = twice(pair[8:16, 64:128])
        return carry

    lax.fori_loop(0, leaves // 8, body, 0)
    half = left_half((FEATURES, 128))
    half8 = left_half((8, 128))
    total = jnp.zeros((8, 64), F32)
    for g in range(leaves // 8):
        sources, moments = [], []
        for q in range(4):
            i = 8 * g + 2 * q
            sources.append(jnp.where(half, fp[i], fp[i + 1]).astype(BF16))
            moments.append(jnp.where(half8, page[i, 64:72, :], page[i + 1, 64:72, :]))
        panel = value_of(dot(jnp.concatenate(sources, axis=1), own_target, CN))
        total = total + exact_dot(jnp.concatenate(moments, axis=1), panel, NN)
    dev[...] = twice(total * (1.0 / 64))


def assign(count_of, leaves, order):
    def tally(i, n):
        return n + (count_of(i) > 256).astype(jnp.int32)

    odd = lax.fori_loop(0, leaves, tally, jnp.int32(0)) & 1

    def deal(i, carry):
        large, taken = carry
        wide_leaf = (count_of(i) > 256).astype(jnp.int32)
        rank = jnp.where(wide_leaf == 1, large, i - large + odd)
        side = rank & 1
        place = jnp.where(side == 1, taken, i - taken)
        order[side * (leaves // 2) + place] = i
        return large + wide_leaf, taken + side

    lax.fori_loop(0, leaves, deal, (jnp.int32(0), jnp.int32(0)))


def clear_empty(empty, fs, ms):
    fs[empty] = jnp.zeros(fs.shape[1:], BF16)
    ms[empty] = jnp.zeros(ms.shape[1:], BF16)


def own_kernel(
    near, counts, me, page, partner, acc,
    fs, ms, ft, blocks, items, order, *slots, leaves, targets,
):
    c = center_of(page)
    assign(lambda i: counts[i], leaves, order)
    first = me[1] * targets

    def prep(t, carry):
        for s in range(2):
            i = 2 * t + s
            store_source(i, page, i, partner[i], c, fs, ms)
        store_target(t, page, order[first + t], c, ft)
        return carry

    lax.fori_loop(0, leaves // 2, prep, 0)
    clear_empty(leaves * 4, fs, ms)
    acc[...] = jnp.zeros_like(acc)

    def place(i, e):
        j = near[e, order[first + i]] - me[0] * leaves
        ok = (j >= 0) & (j < leaves)
        slot = jnp.where(ok, j, 0)
        return ok, slot, counts[slot]

    n = build_items(place, lambda i: counts[order[first + i]], targets, leaves * 4, blocks, items)
    run_items(items, n, fs, ft, ms, acc, slots)


def halo_kernel(
    near, counts, me, own, low, high, partner_low, partner_high, acc0,
    mine, theirs,
    acc, fs, ms, ft, blocks, items, order, *slots, leaves, targets, factor,
):
    c = center_of(own)
    assign(lambda i: counts[leaves + i], leaves, order)
    first = me[1] * targets

    def prep(i, carry):
        store_source(i, low, i, partner_low[i], c, fs, ms)
        store_source(leaves + i, high, i, partner_high[i], c, fs, ms)
        return carry

    def prep_target(i, carry):
        store_target(i, own, order[first + i], c, ft)
        return carry

    lax.fori_loop(0, leaves, prep, 0)
    lax.fori_loop(0, targets, prep_target, 0)
    empty = 2 * leaves * 4
    clear_empty(empty, fs, ms)
    acc[...] = acc0[...]

    def place(i, e):
        j = near[e, order[first + i]] - (me[0] - 1) * leaves
        ok = (j < leaves) | (j >= 2 * leaves)
        slot = jnp.where(ok, jnp.where(j < leaves, j, j - leaves), 0)
        return ok, slot, counts[jnp.where(ok, j, 0)]

    n = build_items(place, lambda i: counts[leaves + order[first + i]], targets, empty, blocks, items)
    run_items(items, n, fs, ft, ms, acc, slots)
    scale = SLOPE * factor

    def finish(i, carry):
        for b in range(2):
            total = acc[2 * i + b]
            total = (total[0:16] + total[16:32]) * scale
            mine[i, :, b * 256 : (b + 1) * 256] = total[0:8]
            theirs[i, :, b * 256 : (b + 1) * 256] = total[8:16]
        return carry

    lax.fori_loop(0, targets, finish, 0)


def far_sum(lists, count, source_of, moment_of, target):
    half = left_half((FEATURES, 128))
    half8 = left_half((8, 128))
    total = jnp.zeros((8, 64), F32)
    for chunk in range(count // 8):
        sources, moments = [], []
        for q in range(4):
            a, b = lists(chunk * 8 + 2 * q), lists(chunk * 8 + 2 * q + 1)
            sources.append(jnp.where(half, source_of(a), source_of(b)).astype(BF16))
            moments.append(jnp.where(half8, moment_of(a), moment_of(b)))
        sources = jnp.concatenate(sources, axis=1)
        moments = jnp.concatenate(moments, axis=1)
        total = total + exact_dot(moments, slope_of(dot(sources, target, CN)), NN)
    return total * (SLOPE / 64)


def shared(left, right):
    half = left_half(left.shape)
    pair = [jnp.where(half, left, 0.0), jnp.where(half, 0.0, right)]
    return jnp.concatenate(pair, axis=0).astype(BF16)


def own_halves(rows):
    return jnp.where(left_half((8, 128)), rows[0:8], rows[8:16])


def far_pair(lists, source_of, moment_of, target):
    half = left_half((FEATURES, 128))
    half8 = left_half((8, 128))
    total = jnp.zeros((16, 128), F32)
    for chunk in range(4):
        sources, moments = [], []
        for of in lists:
            row, moment = [], []
            for q in range(4):
                a, b = of(chunk * 8 + 2 * q), of(chunk * 8 + 2 * q + 1)
                row.append(jnp.where(half, source_of(a), source_of(b)).astype(BF16))
                moment.append(jnp.where(half8, moment_of(a), moment_of(b)))
            sources.append(jnp.concatenate(row, axis=1))
            moments.append(jnp.concatenate(moment, axis=1))
        panel = slope_of(dot(jnp.concatenate(sources, axis=0), target, CN))
        total = total + exact_dot(jnp.concatenate(moments, axis=0), panel, NN)
    return own_halves(total) * (SLOPE / 64)


class Relative:
    def __init__(self, array, me):
        self.array, self.me = array, me

    def __getitem__(self, n):
        return self.array[n ^ self.me]


def upper_levels(coarse, me, box8, roots, c, fbs, fbt, pm, qm):
    def prep(t, carry):
        for s in range(8):
            b = 8 * t + s
            fbs[b], fbt[b] = features(twice(rows_of(box8, b, 0.0)), c, True, True)
        return carry

    lax.fori_loop(0, 7, prep, 0)
    half = left_half((FEATURES, 128))
    half8 = left_half((8, 128))

    def merge(child, parent, moments, out, count):
        def body(t, carry):
            for s in range(8):
                m = t * 8 + s
                source = jnp.where(half, fbs[child + 2 * m], fbs[child + 2 * m + 1]).astype(BF16)
                target = fbt[parent + m].astype(BF16)[:, :64]
                panel = value_of(dot(source, target, CN))
                pair = jnp.where(half8, moments[2 * m], moments[2 * m + 1])
                out[m] = twice(exact_dot(pair, panel, NN) * (1.0 / 64))
            return carry

        lax.fori_loop(0, count // 8, body, 0)

    merge(0, 32, Relative(roots, me), pm, 16)
    merge(32, 48, pm, qm, 8)
    n = me
    m = n >> 1
    t = n >> 2

    def far(base, row, moments):
        target = fbt[row].astype(BF16)[:, :64]
        return far_sum(
            lambda e: coarse[e, row], 16, lambda b: fbs[base + b], lambda b: moments[b], target
        )

    def down(local, source, target):
        panel = value_of(dot(fbs[source].astype(BF16)[:, :64], fbt[target].astype(BF16)[:, :64], CN))
        return exact_dot(local, panel, NN) * (1.0 / 64)

    quad = far(48, 48 + t, qm)
    pair = down(quad, 48 + t, 32 + m) + far(32, 32 + m, pm)
    return down(pair, 32 + m, n) + far(0, n, Relative(roots, me))


def far_kernel(
    far, coarse, me, own, low, high, box8, *rest, leaves, factor
):
    *parts, out, fps, fpt, mps, fbs, fbt, pm, qm, local, roots = rest
    roots[0] = parts[0][0]
    for part in parts[1:]:
        count = part.shape[0]
        roots[count : 2 * count] = part[...]
    c = center_of(own)

    def prep_far(t, carry):
        for s in range(4):
            i = t * 4 + s
            for k, (page, at) in enumerate(((low, 0), (own, 64), (high, 0))):
                (fps[k * leaves + i],) = features(page[i, at + 8 : at + 16], c, True, False)
                mps[k * leaves + i] = page[i, at : at + 8]
            (fpt[i],) = features(own[i, 72:80], c, False, True)
        return carry

    lax.fori_loop(0, leaves // 4, prep_far, 0)
    dev = me[0]
    base = (dev - 1) * leaves

    def gather(t, carry):
        for s in range(2):
            k = t * 2 + s
            local[k] = far_pair(
                [lambda e: far[2 * k, e] - base, lambda e: far[2 * k + 1, e] - base],
                lambda b: fps[b], lambda b: mps[b], shared(fpt[2 * k], fpt[2 * k + 1]),
            )
        return carry

    lax.fori_loop(0, leaves // 4, gather, 0)
    local_dev = upper_levels(coarse, dev, box8, roots, c, fbs, fbt, pm, qm)
    own_source = fbs[dev].astype(BF16)[:, :64]
    half = left_half((FEATURES, 128))

    def down(t, carry):
        for s in range(8):
            k = t * 8 + s
            target = jnp.where(half, fpt[2 * k], fpt[2 * k + 1]).astype(BF16)
            panel = value_of(dot(own_source, target, CN))
            local[k] += exact_dot(local_dev, panel, NN) * (1.0 / 64)
        return carry

    lax.fori_loop(0, leaves // 16, down, 0)

    def finish(t, carry):
        for s in range(8):
            i = t * 8 + s
            source = fps[leaves + i].astype(BF16)[:, :64]
            (points,) = features(lanes_of(own, i, 8), c, False, True)
            basis = value_of(dot(source, points.astype(BF16), CN))
            part = local[t * 4 + s // 2][:, (s % 2) * 64 : (s % 2) * 64 + 64]
            out[i] = exact_dot(part, basis, NN) * factor
        return carry

    lax.fori_loop(0, leaves // 8, finish, 0)


def sum_kernel(counts, me, far, mine, back, out, order, *, leaves):
    assign(lambda i: counts[i], leaves, order)
    half = leaves // 2
    lane = lax.broadcasted_iota(jnp.int32, far.shape[1:], 1)

    def body(t, carry):
        for s in range(4):
            k = 4 * t + s
            for side, part in ((me[1], mine), (1 - me[1], back)):
                i = order[side * half + k]
                out[i] = jnp.where(lane < counts[i], far[i] + part[k], 0.0)
        return carry

    lax.fori_loop(0, half // 4, body, 0)


def cost(microseconds):
    flops = int(microseconds * 1.1e9)
    return pl.CostEstimate(flops=flops, transcendentals=0, bytes_accessed=1 << 20)


def local(points, probes, counts, near_list, far_list, coarse_list, leaf_proxy, box_proxy):
    leaves = points.shape[0]
    size = points.shape[2]
    nodes = lax.axis_size("space")
    device = lax.axis_index("space")
    factor = size ** (-0.5)
    half = lax.axis_index("probe") & 1
    me = jnp.stack([device, half]).astype(jnp.int32)
    points = jnp.transpose(points, (1, 0, 2))
    leafp = jnp.transpose(leaf_proxy, (1, 0, 2))
    boxp = jnp.transpose(box_proxy, (1, 0, 2))
    near = near_list.T
    forward = [(i, i + 1) for i in range(nodes - 1)]
    backward = [(i + 1, i) for i in range(nodes - 1)]
    pairs = [(i, i ^ 1) for i in range(lax.axis_size("probe"))]
    partner = lax.ppermute(probes, "probe", pairs)
    params = pltpu.CompilerParams(vmem_limit_bytes=56 << 20)
    vm = pltpu.VMEM
    vmem = pl.BlockSpec(memory_space=vm)
    smem = pl.BlockSpec(memory_space=pltpu.SMEM)
    shape = jax.ShapeDtypeStruct
    page, dev = pl.pallas_call(
        functools.partial(moments_kernel, leaves=leaves, factor=factor),
        out_shape=(shape((leaves, 80, 128), F32), shape((8, 128), F32)),
        in_specs=[smem] * 2 + [vmem] * 4,
        out_specs=(vmem, vmem),
        scratch_shapes=[vm((leaves, FEATURES, 128), F32)],
        compiler_params=params,
        cost_estimate=cost(8),
        name="moments",
    )(counts, me, probes, points, leafp, boxp)
    low = lax.ppermute(page, "space", forward)
    high = lax.ppermute(page, "space", backward)
    parts = [dev[None]]
    for bit in range(nodes.bit_length() - 1):
        swap = [(i, i ^ (1 << bit)) for i in range(nodes)]
        parts.append(lax.ppermute(jnp.concatenate(parts, axis=0), "space", swap))
    partner_low = lax.ppermute(partner, "space", forward)
    partner_high = lax.ppermute(partner, "space", backward)
    targets = leaves // 2

    def work(blocks):
        return (
            [
                vm((blocks, FEATURES, 128), BF16),
                vm((blocks, 32, 128), BF16),
                vm((targets * 2, FEATURES, 256), BF16),
                pltpu.SMEM((48,), jnp.int32),
                pltpu.SMEM((targets * 32 + 64,), jnp.int32),
                pltpu.SMEM((leaves,), jnp.int32),
            ]
            + [vm((256, 256), F32)] * UNITS
        )

    page, *parts = lax.optimization_barrier((page, *parts))
    acc0 = pl.pallas_call(
        functools.partial(own_kernel, leaves=leaves, targets=targets),
        out_shape=shape((targets * 2, 32, 256), F32),
        in_specs=[smem] * 3 + [vmem] * 2,
        out_specs=vmem,
        scratch_shapes=work(leaves * 4 + 1),
        compiler_params=params,
        cost_estimate=cost(28),
        name="near_own",
    )(near, counts, me, page, partner)
    counts3 = jnp.concatenate(
        [low[:, 11, 0].astype(jnp.int32), counts, high[:, 11, 0].astype(jnp.int32)]
    )
    mine, theirs = pl.pallas_call(
        functools.partial(halo_kernel, leaves=leaves, targets=targets, factor=factor),
        out_shape=(shape((targets, 8, size), F32),) * 2,
        in_specs=[smem] * 3 + [vmem] * 6,
        out_specs=(vmem, vmem),
        scratch_shapes=[vm((targets * 2, 32, 256), F32)] + work(2 * leaves * 4 + 1),
        compiler_params=params,
        cost_estimate=cost(30),
        name="near_halo",
    )(near, counts3, me, page, low, high, partner_low, partner_high, acc0)
    back = lax.ppermute(theirs, "probe", pairs)
    whole = lambda dims: pl.BlockSpec(dims, lambda i: (0,) * len(dims))
    tail = pl.BlockSpec((leaves, 16, 128), lambda i: (0, 4, 0))
    far = pl.pallas_call(
        functools.partial(far_kernel, leaves=leaves, factor=factor),
        out_shape=shape(probes.shape, F32),
        grid=(1,),
        in_specs=[smem] * 3 + [whole(page.shape), tail, tail, whole(boxp.shape)]
        + [whole(part.shape) for part in parts],
        out_specs=whole(probes.shape),
        scratch_shapes=[
            vm((3 * leaves, FEATURES, 128), F32),
            vm((leaves, FEATURES, 128), F32),
            vm((3 * leaves, 8, 128), F32),
            vm((56, FEATURES, 128), F32),
            vm((56, FEATURES, 128), F32),
            vm((nodes // 2, 8, 128), F32),
            vm((nodes // 4, 8, 128), F32),
            vm((leaves // 2, 8, 128), F32),
            vm((nodes, 8, 128), F32),
        ],
        compiler_params=params,
        cost_estimate=cost(30),
        name="far",
    )(far_list, coarse_list.T, me, page, low, high, boxp, *parts)
    return pl.pallas_call(
        functools.partial(sum_kernel, leaves=leaves),
        out_shape=shape(probes.shape, F32),
        in_specs=[smem] * 2 + [vmem] * 3,
        out_specs=vmem,
        scratch_shapes=[pltpu.SMEM((leaves,), jnp.int32)],
        compiler_params=params,
        name="sum",
    )(counts, me, far, mine, back)


def solution(mesh):
    return jax.shard_map(
        local,
        mesh=mesh,
        in_specs=(
            P("space", None, None),
            P("space", "probe", None),
            P("space"),
            P("space", None),
            P("space", None),
            P(),
            P("space", None, None),
            P(),
        ),
        out_specs=P("space", "probe", None),
        check_vma=False,
    )
```

```python
import functools

import jax
import jax.numpy as jnp
from jax import lax
from jax.experimental import pallas as pl
from jax.experimental.pallas import tpu as pltpu
from jax.sharding import PartitionSpec as P

F32 = jnp.float32
BF16 = jnp.bfloat16
LOG2E = 1.4426950408889634
LN2 = 0.6931471805599453
SCALE = LOG2E * 1.7320508075688772 / 2.0
SLOPE = 0.5 / (LOG2E * LOG2E)
TINY = 1e-30
FEATURES = 48
UNITS = 8
CN = (((0,), (0,)), ((), ()))
NT = (((1,), (1,)), ((), ()))
NN = (((1,), (0,)), ((), ()))


def dot(left, right, dims):
    return lax.dot_general(left, right, dims, preferred_element_type=F32)


def split(value):
    high = value.astype(BF16)
    return high, (value - high.astype(F32)).astype(BF16)


def stacked(value):
    high = value.astype(BF16).astype(F32)
    return jnp.concatenate([high, value - high], axis=0).astype(BF16)


def exact_dot(left, right, dims):
    rows = left.shape[0]
    high, low = split(right)
    both = stacked(left)
    total = dot(both, high, dims) + dot(both, low, dims)
    return total[:rows] + total[rows:]


def slope_of(u):
    u = jnp.maximum(u, TINY)
    return u * jnp.exp2(-(u * lax.rsqrt(u)))


def value_of(u):
    u = jnp.maximum(u, TINY)
    w = u * lax.rsqrt(u)
    return (1.0 + LN2 * w) * jnp.exp2(-w)


def pieces(value):
    high = value.astype(BF16).astype(F32)
    rest = value - high
    middle = rest.astype(BF16).astype(F32)
    return high, middle, rest - middle


def features(rows, center, source, target):
    row = lax.broadcasted_iota(jnp.int32, rows.shape, 0)
    scaled = jnp.where(row < 3, (rows - center) * SCALE, 0.0)
    norm = jnp.sum(scaled * scaled, axis=0, keepdims=True)
    out = []
    if source:
        h, m, l = pieces(jnp.where(row == 3, norm, jnp.where(row == 4, 1.0, scaled)))
        out.append(jnp.concatenate([h, h, m, h, l, m], axis=0))
    if target:
        h, m, l = pieces(jnp.where(row == 3, 1.0, jnp.where(row == 4, norm, -2.0 * scaled)))
        out.append(jnp.concatenate([h, m, h, l, h, m], axis=0))
    return out


def twice(value):
    return jnp.concatenate([value, value], axis=1)


def left_half(shape):
    return lax.broadcasted_iota(jnp.int32, shape, 1) < 64


def lanes_of(page, i, start):
    return jnp.concatenate([page[i, 16 * b + start : 16 * b + start + 8, :] for b in range(4)], axis=1)


def partner_of(page, i):
    return jnp.concatenate([page[i, 80 + 8 * b : 88 + 8 * b, :] for b in range(4)], axis=1)


def center_of(page):
    return page[0, 8:16, 0:1]


def store_source(slot, page, i, partner, center, fs, ms):
    rows = lanes_of(page, i, 8)
    (source,) = features(rows, center, True, False)
    source = source.astype(BF16)
    lane = lax.broadcasted_iota(jnp.int32, partner.shape, 1).astype(F32)
    other = jnp.where(lane < rows[3:4], partner, 0.0)
    moments = stacked(jnp.concatenate([lanes_of(page, i, 0), other], axis=0))
    for b in range(4):
        fs[slot * 4 + b] = source[:, b * 128 : (b + 1) * 128]
        ms[slot * 4 + b] = moments[:, b * 128 : (b + 1) * 128]


def store_target(slot, page, i, center, ft):
    (target,) = features(lanes_of(page, i, 8), center, False, True)
    target = target.astype(BF16)
    for b in range(2):
        ft[slot * 2 + b] = target[:, b * 256 : (b + 1) * 256]


def build_items(place, target_count, targets, empty, blocks, items):
    def per_leaf(i, n):
        nb = jnp.int32(0)
        for e in range(8):
            ok, slot, count = place(i, e)
            for b in range(4):
                blocks[nb + b] = slot * 4 + b
            nb = nb + jnp.where(ok, (count + 127) >> 7, 0)
        blocks[nb] = empty
        pairs = (nb + 1) >> 1

        def put(q, carry):
            code = (blocks[2 * q] << 9) | blocks[2 * q + 1]
            items[n + q] = code | ((2 * i) << 18)
            items[n + pairs + q] = code | ((2 * i + 1) << 18)
            return carry

        lax.fori_loop(0, pairs, put, 0)
        return n + jnp.where(target_count(i) > 256, 2 * pairs, pairs)

    n = lax.fori_loop(0, targets, per_leaf, jnp.int32(0))
    for t in range(2 * UNITS):
        items[n + t] = (empty << 9) | empty
    return n


def run_items(items, n, fs, ft, ms, acc, slots):
    def distances(code, u):
        left = jnp.concatenate([fs[(code >> 9) & 511], fs[code & 511]], axis=1)
        u[...] = dot(left, ft[code >> 18], CN)

    def contract(code, u):
        high, low = split(slope_of(u[...]))
        m = jnp.concatenate([ms[(code >> 9) & 511], ms[code & 511]], axis=1)
        acc[code >> 18] += dot(m, high, NN) + dot(m, low, NN)

    for s in range(UNITS):
        distances(items[s], slots[s])

    def body(t, carry):
        for s in range(UNITS):
            contract(items[UNITS * t + s], slots[s])
            distances(items[UNITS * (t + 1) + s], slots[s])
        return carry

    lax.fori_loop(0, (n + UNITS - 1) // UNITS, body, 0)


def rows_of(planes, i, extra):
    rows = [planes[d, pl.ds(i, 1), :] for d in range(3)]
    width = rows[0].shape[1]
    return jnp.concatenate(
        rows + [jnp.full((1, width), extra, F32), jnp.zeros((4, width), F32)], axis=0
    )


def moments_kernel(counts, me, probes, points, leafp, boxp, page, dev, fp, *, leaves, factor):
    c = rows_of(points, 0, 0.0)[:, 0:1]
    (own_target,) = features(rows_of(boxp, me[0], 0.0), c, False, True)
    own_target = own_target.astype(BF16)
    lane = lax.broadcasted_iota(jnp.int32, probes.shape[1:], 1)

    def prep(i):
        count = counts[i]
        masked = jnp.where(lane < count, probes[i], 0.0)
        rows = rows_of(points, i, count.astype(F32))
        for b in range(4):
            page[i, 16 * b : 16 * b + 8, :] = masked[:, b * 128 : (b + 1) * 128]
            page[i, 16 * b + 8 : 16 * b + 16, :] = rows[:, b * 128 : (b + 1) * 128]
        proxies = twice(rows_of(leafp, i, 0.0))
        page[i, 72:80, :] = proxies
        (target,) = features(rows, c, False, True)
        (fp[i],) = features(proxies, c, True, False)
        return masked, target.astype(BF16)

    def body(t, carry):
        for s in range(4):
            i = t * 8 + 2 * s
            (left, left_points), (right, right_points) = prep(i), prep(i + 1)
            both = jnp.concatenate([left_points, right_points], axis=0)
            basis = value_of(dot(both, shared(fp[i], fp[i + 1]), CN))
            pair = exact_dot(jnp.concatenate([left, right], axis=0), basis, NN) * factor
            page[i, 64:72, :] = twice(pair[0:8, 0:64])
            page[i + 1, 64:72, :] = twice(pair[8:16, 64:128])
        return carry

    lax.fori_loop(0, leaves // 8, body, 0)
    half = left_half((FEATURES, 128))
    half8 = left_half((8, 128))
    total = jnp.zeros((8, 64), F32)
    for g in range(leaves // 8):
        sources, moments = [], []
        for q in range(4):
            i = 8 * g + 2 * q
            sources.append(jnp.where(half, fp[i], fp[i + 1]).astype(BF16))
            moments.append(jnp.where(half8, page[i, 64:72, :], page[i + 1, 64:72, :]))
        panel = value_of(dot(jnp.concatenate(sources, axis=1), own_target, CN))
        total = total + exact_dot(jnp.concatenate(moments, axis=1), panel, NN)
    dev[...] = twice(total * (1.0 / 64))


def assign(count_of, leaves, order):
    def tally(i, n):
        return n + (count_of(i) > 256).astype(jnp.int32)

    odd = lax.fori_loop(0, leaves, tally, jnp.int32(0)) & 1

    def deal(i, carry):
        large, taken = carry
        wide_leaf = (count_of(i) > 256).astype(jnp.int32)
        rank = jnp.where(wide_leaf == 1, large, i - large + odd)
        side = rank & 1
        place = jnp.where(side == 1, taken, i - taken)
        order[side * (leaves // 2) + place] = i
        return large + wide_leaf, taken + side

    lax.fori_loop(0, leaves, deal, (jnp.int32(0), jnp.int32(0)))


def clear_empty(empty, fs, ms):
    fs[empty] = jnp.zeros(fs.shape[1:], BF16)
    ms[empty] = jnp.zeros(ms.shape[1:], BF16)


def own_kernel(
    near, counts, me, page, partner, acc,
    fs, ms, ft, blocks, items, order, *slots, leaves, targets,
):
    c = center_of(page)
    assign(lambda i: counts[i], leaves, order)
    first = me[1] * targets

    def prep(t, carry):
        for s in range(8):
            i = 8 * t + s
            store_source(i, page, i, partner[i], c, fs, ms)
        for s in range(4):
            i = 4 * t + s
            store_target(i, page, order[first + i], c, ft)
        return carry

    lax.fori_loop(0, leaves // 8, prep, 0)
    clear_empty(leaves * 4, fs, ms)
    acc[...] = jnp.zeros_like(acc)

    def place(i, e):
        j = near[e, order[first + i]] - me[0] * leaves
        ok = (j >= 0) & (j < leaves)
        slot = jnp.where(ok, j, 0)
        return ok, slot, counts[slot]

    n = build_items(place, lambda i: counts[order[first + i]], targets, leaves * 4, blocks, items)
    run_items(items, n, fs, ft, ms, acc, slots)


def halo_kernel(
    near, counts, me, own, low, high, acc0,
    mine, theirs,
    acc, fs, ms, ft, blocks, items, order, *slots, leaves, targets, factor,
):
    c = center_of(own)
    assign(lambda i: counts[leaves + i], leaves, order)
    first = me[1] * targets

    def prep(t, carry):
        for s in range(4):
            i = 4 * t + s
            store_source(i, low, i, partner_of(low, i), c, fs, ms)
            store_source(leaves + i, high, i, partner_of(high, i), c, fs, ms)
        for s in range(2):
            i = 2 * t + s
            store_target(i, own, order[first + i], c, ft)
        return carry

    lax.fori_loop(0, leaves // 4, prep, 0)
    empty = 2 * leaves * 4
    clear_empty(empty, fs, ms)
    acc[...] = acc0[...]

    def place(i, e):
        j = near[e, order[first + i]] - (me[0] - 1) * leaves
        ok = (j < leaves) | (j >= 2 * leaves)
        slot = jnp.where(ok, jnp.where(j < leaves, j, j - leaves), 0)
        return ok, slot, counts[jnp.where(ok, j, 0)]

    n = build_items(place, lambda i: counts[leaves + order[first + i]], targets, empty, blocks, items)
    run_items(items, n, fs, ft, ms, acc, slots)
    scale = SLOPE * factor

    def finish(t, carry):
        for s in range(4):
            i = 4 * t + s
            for b in range(2):
                total = acc[2 * i + b]
                total = (total[0:16] + total[16:32]) * scale
                mine[i, :, b * 256 : (b + 1) * 256] = total[0:8]
                theirs[i, :, b * 256 : (b + 1) * 256] = total[8:16]
        return carry

    lax.fori_loop(0, targets // 4, finish, 0)


def far_sum(lists, count, source_of, moment_of, target):
    half = left_half((FEATURES, 128))
    half8 = left_half((8, 128))
    total = jnp.zeros((8, 64), F32)
    for chunk in range(count // 8):
        sources, moments = [], []
        for q in range(4):
            a, b = lists(chunk * 8 + 2 * q), lists(chunk * 8 + 2 * q + 1)
            sources.append(jnp.where(half, source_of(a), source_of(b)).astype(BF16))
            moments.append(jnp.where(half8, moment_of(a), moment_of(b)))
        sources = jnp.concatenate(sources, axis=1)
        moments = jnp.concatenate(moments, axis=1)
        total = total + exact_dot(moments, slope_of(dot(sources, target, CN)), NN)
    return total * (SLOPE / 64)


def shared(left, right):
    half = left_half(left.shape)
    pair = [jnp.where(half, left, 0.0), jnp.where(half, 0.0, right)]
    return jnp.concatenate(pair, axis=0).astype(BF16)


def own_halves(rows):
    return jnp.where(left_half((8, 128)), rows[0:8], rows[8:16])


def far_pair(lists, source_of, moment_of, target):
    half = left_half((FEATURES, 128))
    half8 = left_half((8, 128))
    total = jnp.zeros((16, 128), F32)
    for chunk in range(4):
        sources, moments = [], []
        for of in lists:
            row, moment = [], []
            for q in range(4):
                a, b = of(chunk * 8 + 2 * q), of(chunk * 8 + 2 * q + 1)
                row.append(jnp.where(half, source_of(a), source_of(b)).astype(BF16))
                moment.append(jnp.where(half8, moment_of(a), moment_of(b)))
            sources.append(jnp.concatenate(row, axis=1))
            moments.append(jnp.concatenate(moment, axis=1))
        panel = slope_of(dot(jnp.concatenate(sources, axis=0), target, CN))
        total = total + exact_dot(jnp.concatenate(moments, axis=0), panel, NN)
    return own_halves(total) * (SLOPE / 64)


class Relative:
    def __init__(self, array, me):
        self.array, self.me = array, me

    def __getitem__(self, n):
        return self.array[n ^ self.me]


def upper_levels(coarse, me, box8, roots, c, fbs, fbt, pm, qm):
    def prep(t, carry):
        for s in range(8):
            b = 8 * t + s
            fbs[b], fbt[b] = features(twice(rows_of(box8, b, 0.0)), c, True, True)
        return carry

    lax.fori_loop(0, 7, prep, 0)
    half = left_half((FEATURES, 128))
    half8 = left_half((8, 128))

    def merge(child, parent, moments, out, count):
        def body(t, carry):
            for s in range(8):
                m = t * 8 + s
                source = jnp.where(half, fbs[child + 2 * m], fbs[child + 2 * m + 1]).astype(BF16)
                target = fbt[parent + m].astype(BF16)[:, :64]
                panel = value_of(dot(source, target, CN))
                pair = jnp.where(half8, moments[2 * m], moments[2 * m + 1])
                out[m] = twice(exact_dot(pair, panel, NN) * (1.0 / 64))
            return carry

        lax.fori_loop(0, count // 8, body, 0)

    merge(0, 32, Relative(roots, me), pm, 16)
    merge(32, 48, pm, qm, 8)
    n = me
    m = n >> 1
    t = n >> 2

    def far(base, row, moments):
        target = fbt[row].astype(BF16)[:, :64]
        return far_sum(
            lambda e: coarse[e, row], 16, lambda b: fbs[base + b], lambda b: moments[b], target
        )

    def down(local, source, target):
        panel = value_of(dot(fbs[source].astype(BF16)[:, :64], fbt[target].astype(BF16)[:, :64], CN))
        return exact_dot(local, panel, NN) * (1.0 / 64)

    quad = far(48, 48 + t, qm)
    pair = down(quad, 48 + t, 32 + m) + far(32, 32 + m, pm)
    return down(pair, 32 + m, n) + far(0, n, Relative(roots, me))


def far_kernel(
    far, coarse, me, own, low, high, box8, *rest, leaves, factor
):
    *parts, out, fps, fpt, mps, fbs, fbt, pm, qm, local, roots = rest
    roots[0] = parts[0][0]
    for part in parts[1:]:
        count = part.shape[0]
        roots[count : 2 * count] = part[...]
    c = center_of(own)

    def prep_far(t, carry):
        for s in range(4):
            i = t * 4 + s
            for k, (page, at) in enumerate(((low, 0), (own, 64), (high, 0))):
                (fps[k * leaves + i],) = features(page[i, at + 8 : at + 16], c, True, False)
                mps[k * leaves + i] = page[i, at : at + 8]
            (fpt[i],) = features(own[i, 72:80], c, False, True)
        return carry

    lax.fori_loop(0, leaves // 4, prep_far, 0)
    dev = me[0]
    base = (dev - 1) * leaves

    def gather(t, carry):
        for s in range(2):
            k = t * 2 + s
            local[k] = far_pair(
                [lambda e: far[2 * k, e] - base, lambda e: far[2 * k + 1, e] - base],
                lambda b: fps[b], lambda b: mps[b], shared(fpt[2 * k], fpt[2 * k + 1]),
            )
        return carry

    lax.fori_loop(0, leaves // 4, gather, 0)
    local_dev = upper_levels(coarse, dev, box8, roots, c, fbs, fbt, pm, qm)
    own_source = fbs[dev].astype(BF16)[:, :64]
    half = left_half((FEATURES, 128))

    def down(t, carry):
        for s in range(8):
            k = t * 8 + s
            target = jnp.where(half, fpt[2 * k], fpt[2 * k + 1]).astype(BF16)
            panel = value_of(dot(own_source, target, CN))
            local[k] += exact_dot(local_dev, panel, NN) * (1.0 / 64)
        return carry

    lax.fori_loop(0, leaves // 16, down, 0)

    def finish(t, carry):
        for s in range(8):
            i = t * 8 + s
            source = fps[leaves + i].astype(BF16)[:, :64]
            (points,) = features(lanes_of(own, i, 8), c, False, True)
            basis = value_of(dot(source, points.astype(BF16), CN))
            part = local[t * 4 + s // 2][:, (s % 2) * 64 : (s % 2) * 64 + 64]
            out[i] = exact_dot(part, basis, NN) * factor
        return carry

    lax.fori_loop(0, leaves // 8, finish, 0)


def sum_kernel(counts, me, far, mine, back, out, order, *, leaves):
    assign(lambda i: counts[i], leaves, order)
    half = leaves // 2
    lane = lax.broadcasted_iota(jnp.int32, far.shape[1:], 1)

    def body(t, carry):
        for s in range(4):
            k = 4 * t + s
            for side, part in ((me[1], mine), (1 - me[1], back)):
                i = order[side * half + k]
                out[i] = jnp.where(lane < counts[i], far[i] + part[k], 0.0)
        return carry

    lax.fori_loop(0, half // 4, body, 0)


def cost(microseconds):
    flops = int(microseconds * 1.1e9)
    return pl.CostEstimate(flops=flops, transcendentals=0, bytes_accessed=1 << 20)


def local(points, probes, counts, near_list, far_list, coarse_list, leaf_proxy, box_proxy):
    leaves = points.shape[0]
    size = points.shape[2]
    nodes = lax.axis_size("space")
    device = lax.axis_index("space")
    factor = size ** (-0.5)
    half = lax.axis_index("probe") & 1
    me = jnp.stack([device, half]).astype(jnp.int32)
    points = jnp.transpose(points, (1, 0, 2))
    leafp = jnp.transpose(leaf_proxy, (1, 0, 2))
    boxp = jnp.transpose(box_proxy, (1, 0, 2))
    near = near_list.T
    forward = [(i, i + 1) for i in range(nodes - 1)]
    backward = [(i + 1, i) for i in range(nodes - 1)]
    pairs = [(i, i ^ 1) for i in range(lax.axis_size("probe"))]
    partner = lax.ppermute(probes, "probe", pairs)
    params = pltpu.CompilerParams(vmem_limit_bytes=56 << 20)
    vm = pltpu.VMEM
    vmem = pl.BlockSpec(memory_space=vm)
    smem = pl.BlockSpec(memory_space=pltpu.SMEM)
    shape = jax.ShapeDtypeStruct
    page, dev = pl.pallas_call(
        functools.partial(moments_kernel, leaves=leaves, factor=factor),
        out_shape=(shape((leaves, 80, 128), F32), shape((8, 128), F32)),
        in_specs=[smem] * 2 + [vmem] * 4,
        out_specs=(vmem, vmem),
        scratch_shapes=[vm((leaves, FEATURES, 128), F32)],
        compiler_params=params,
        cost_estimate=cost(8),
        name="moments",
    )(counts, me, probes, points, leafp, boxp)
    parts = [dev[None]]
    for bit in range(nodes.bit_length() - 1):
        swap = [(i, i ^ (1 << bit)) for i in range(nodes)]
        parts.append(lax.ppermute(jnp.concatenate(parts, axis=0), "space", swap))
    tiles = jnp.transpose(partner.reshape(leaves, 8, size // 128, 128), (0, 2, 1, 3))
    both = jnp.concatenate([page, tiles.reshape(leaves, size // 16, 128)], axis=1)
    low = lax.ppermute(both, "space", forward)
    high = lax.ppermute(both, "space", backward)
    targets = leaves // 2

    def work(blocks):
        return (
            [
                vm((blocks, FEATURES, 128), BF16),
                vm((blocks, 32, 128), BF16),
                vm((targets * 2, FEATURES, 256), BF16),
                pltpu.SMEM((48,), jnp.int32),
                pltpu.SMEM((targets * 32 + 64,), jnp.int32),
                pltpu.SMEM((leaves,), jnp.int32),
            ]
            + [vm((256, 256), F32)] * UNITS
        )

    page, *parts = lax.optimization_barrier((page, *parts))
    acc0 = pl.pallas_call(
        functools.partial(own_kernel, leaves=leaves, targets=targets),
        out_shape=shape((targets * 2, 32, 256), F32),
        in_specs=[smem] * 3 + [vmem] * 2,
        out_specs=vmem,
        scratch_shapes=work(leaves * 4 + 1),
        compiler_params=params,
        cost_estimate=cost(28),
        name="near_own",
    )(near, counts, me, page, partner)
    counts3 = jnp.concatenate(
        [low[:, 11, 0].astype(jnp.int32), counts, high[:, 11, 0].astype(jnp.int32)]
    )
    mine, theirs = pl.pallas_call(
        functools.partial(halo_kernel, leaves=leaves, targets=targets, factor=factor),
        out_shape=(shape((targets, 8, size), F32),) * 2,
        in_specs=[smem] * 3 + [vmem] * 4,
        out_specs=(vmem, vmem),
        scratch_shapes=[vm((targets * 2, 32, 256), F32)] + work(2 * leaves * 4 + 1),
        compiler_params=params,
        cost_estimate=cost(30),
        name="near_halo",
    )(near, counts3, me, page, low, high, acc0)
    back = lax.ppermute(theirs, "probe", pairs)
    whole = lambda dims: pl.BlockSpec(dims, lambda i: (0,) * len(dims))
    tail = pl.BlockSpec((leaves, 16, 128), lambda i: (0, 4, 0))
    far = pl.pallas_call(
        functools.partial(far_kernel, leaves=leaves, factor=factor),
        out_shape=shape(probes.shape, F32),
        grid=(1,),
        in_specs=[smem] * 3 + [whole(page.shape), tail, tail, whole(boxp.shape)]
        + [whole(part.shape) for part in parts],
        out_specs=whole(probes.shape),
        scratch_shapes=[
            vm((3 * leaves, FEATURES, 128), F32),
            vm((leaves, FEATURES, 128), F32),
            vm((3 * leaves, 8, 128), F32),
            vm((56, FEATURES, 128), F32),
            vm((56, FEATURES, 128), F32),
            vm((nodes // 2, 8, 128), F32),
            vm((nodes // 4, 8, 128), F32),
            vm((leaves // 2, 8, 128), F32),
            vm((nodes, 8, 128), F32),
        ],
        compiler_params=params,
        cost_estimate=cost(30),
        name="far",
    )(far_list, coarse_list.T, me, page, low, high, boxp, *parts)
    return pl.pallas_call(
        functools.partial(sum_kernel, leaves=leaves),
        out_shape=shape(probes.shape, F32),
        in_specs=[smem] * 2 + [vmem] * 3,
        out_specs=vmem,
        scratch_shapes=[pltpu.SMEM((leaves,), jnp.int32)],
        compiler_params=params,
        name="sum",
    )(counts, me, far, mine, back)


def solution(mesh):
    return jax.shard_map(
        local,
        mesh=mesh,
        in_specs=(
            P("space", None, None),
            P("space", "probe", None),
            P("space"),
            P("space", None),
            P("space", None),
            P(),
            P("space", None, None),
            P(),
        ),
        out_specs=P("space", "probe", None),
        check_vma=False,
    )
```

```python
import functools

import jax
import jax.numpy as jnp
from jax import lax
from jax.experimental import pallas as pl
from jax.experimental.pallas import tpu as pltpu
from jax.sharding import PartitionSpec as P

F32 = jnp.float32
BF16 = jnp.bfloat16
LOG2E = 1.4426950408889634
LN2 = 0.6931471805599453
SCALE = LOG2E * 1.7320508075688772 / 2.0
SLOPE = 0.5 / (LOG2E * LOG2E)
TINY = 1e-30
FEATURES = 48
UNITS = 8
CN = (((0,), (0,)), ((), ()))
NT = (((1,), (1,)), ((), ()))
NN = (((1,), (0,)), ((), ()))


def dot(left, right, dims):
    return lax.dot_general(left, right, dims, preferred_element_type=F32)


def split(value):
    high = value.astype(BF16)
    return high, (value - high.astype(F32)).astype(BF16)


def stacked(value):
    high = value.astype(BF16).astype(F32)
    return jnp.concatenate([high, value - high], axis=0).astype(BF16)


def exact_dot(left, right, dims):
    rows = left.shape[0]
    high, low = split(right)
    both = stacked(left)
    total = dot(both, high, dims) + dot(both, low, dims)
    return total[:rows] + total[rows:]


def slope_of(u):
    u = jnp.maximum(u, TINY)
    return u * jnp.exp2(-(u * lax.rsqrt(u)))


def value_of(u):
    u = jnp.maximum(u, TINY)
    w = u * lax.rsqrt(u)
    return (1.0 + LN2 * w) * jnp.exp2(-w)


def pieces(value):
    high = value.astype(BF16).astype(F32)
    rest = value - high
    middle = rest.astype(BF16).astype(F32)
    return high, middle, rest - middle


def features(rows, center, source, target):
    row = lax.broadcasted_iota(jnp.int32, rows.shape, 0)
    scaled = jnp.where(row < 3, (rows - center) * SCALE, 0.0)
    norm = jnp.sum(scaled * scaled, axis=0, keepdims=True)
    out = []
    if source:
        h, m, l = pieces(jnp.where(row == 3, norm, jnp.where(row == 4, 1.0, scaled)))
        out.append(jnp.concatenate([h, h, m, h, l, m], axis=0))
    if target:
        h, m, l = pieces(jnp.where(row == 3, 1.0, jnp.where(row == 4, norm, -2.0 * scaled)))
        out.append(jnp.concatenate([h, m, h, l, h, m], axis=0))
    return out


def twice(value):
    return jnp.concatenate([value, value], axis=1)


def left_half(shape):
    return lax.broadcasted_iota(jnp.int32, shape, 1) < 64


def lanes_of(page, i, start):
    return jnp.concatenate([page[i, 16 * b + start : 16 * b + start + 8, :] for b in range(4)], axis=1)


def partner_of(page, i):
    return jnp.concatenate([page[i, 80 + 8 * b : 88 + 8 * b, :] for b in range(4)], axis=1)


def center_of(page):
    return page[0, 8:16, 0:1]


def store_source(slot, page, i, partner, center, fs, ms):
    rows = lanes_of(page, i, 8)
    (source,) = features(rows, center, True, False)
    source = source.astype(BF16)
    lane = lax.broadcasted_iota(jnp.int32, partner.shape, 1).astype(F32)
    other = jnp.where(lane < rows[3:4], partner, 0.0)
    moments = stacked(jnp.concatenate([lanes_of(page, i, 0), other], axis=0))
    for b in range(4):
        fs[slot * 4 + b] = source[:, b * 128 : (b + 1) * 128]
        ms[slot * 4 + b] = moments[:, b * 128 : (b + 1) * 128]


def store_target(slot, page, i, center, ft):
    (target,) = features(lanes_of(page, i, 8), center, False, True)
    target = target.astype(BF16)
    for b in range(2):
        ft[slot * 2 + b] = target[:, b * 256 : (b + 1) * 256]


def build_items(place, target_count, targets, empty, blocks, items):
    def per_leaf(i, n):
        nb = jnp.int32(0)
        for e in range(8):
            ok, slot, count = place(i, e)
            for b in range(4):
                blocks[nb + b] = slot * 4 + b
            nb = nb + jnp.where(ok, (count + 127) >> 7, 0)
        blocks[nb] = empty
        pairs = (nb + 1) >> 1

        def put(q, carry):
            code = (blocks[2 * q] << 9) | blocks[2 * q + 1]
            items[n + q] = code | ((2 * i) << 18)
            items[n + pairs + q] = code | ((2 * i + 1) << 18)
            return carry

        lax.fori_loop(0, pairs, put, 0)
        return n + jnp.where(target_count(i) > 256, 2 * pairs, pairs)

    n = lax.fori_loop(0, targets, per_leaf, jnp.int32(0))
    for t in range(2 * UNITS):
        items[n + t] = (empty << 9) | empty
    return n


def run_items(items, n, fs, ft, ms, acc, slots):
    def distances(code, u):
        left = jnp.concatenate([fs[(code >> 9) & 511], fs[code & 511]], axis=1)
        u[...] = dot(left, ft[code >> 18], CN)

    def contract(code, u):
        high, low = split(slope_of(u[...]))
        m = jnp.concatenate([ms[(code >> 9) & 511], ms[code & 511]], axis=1)
        acc[code >> 18] += dot(m, high, NN) + dot(m, low, NN)

    for s in range(UNITS):
        distances(items[s], slots[s])

    def body(t, carry):
        for s in range(UNITS):
            contract(items[UNITS * t + s], slots[s])
            distances(items[UNITS * (t + 1) + s], slots[s])
        return carry

    lax.fori_loop(0, (n + UNITS - 1) // UNITS, body, 0)


def rows_of(planes, i, extra):
    rows = [planes[d, pl.ds(i, 1), :] for d in range(3)]
    width = rows[0].shape[1]
    return jnp.concatenate(
        rows + [jnp.full((1, width), extra, F32), jnp.zeros((4, width), F32)], axis=0
    )


def moments_kernel(counts, me, probes, points, leafp, boxp, page, dev, fp, *, leaves, factor):
    c = rows_of(points, 0, 0.0)[:, 0:1]
    (own_target,) = features(rows_of(boxp, me[0], 0.0), c, False, True)
    own_target = own_target.astype(BF16)
    lane = lax.broadcasted_iota(jnp.int32, probes.shape[1:], 1)

    def prep(i):
        count = counts[i]
        masked = jnp.where(lane < count, probes[i], 0.0)
        rows = rows_of(points, i, count.astype(F32))
        for b in range(4):
            page[i, 16 * b : 16 * b + 8, :] = masked[:, b * 128 : (b + 1) * 128]
            page[i, 16 * b + 8 : 16 * b + 16, :] = rows[:, b * 128 : (b + 1) * 128]
        proxies = twice(rows_of(leafp, i, 0.0))
        page[i, 72:80, :] = proxies
        (target,) = features(rows, c, False, True)
        (fp[i],) = features(proxies, c, True, False)
        return masked, target.astype(BF16)

    def body(t, carry):
        for s in range(4):
            i = t * 8 + 2 * s
            (left, left_points), (right, right_points) = prep(i), prep(i + 1)
            both = jnp.concatenate([left_points, right_points], axis=0)
            basis = value_of(dot(both, shared(fp[i], fp[i + 1]), CN))
            pair = exact_dot(jnp.concatenate([left, right], axis=0), basis, NN) * factor
            page[i, 64:72, :] = twice(pair[0:8, 0:64])
            page[i + 1, 64:72, :] = twice(pair[8:16, 64:128])
        return carry

    lax.fori_loop(0, leaves // 8, body, 0)
    half = left_half((FEATURES, 128))
    half8 = left_half((8, 128))
    total = jnp.zeros((8, 64), F32)
    for g in range(leaves // 8):
        sources, moments = [], []
        for q in range(4):
            i = 8 * g + 2 * q
            sources.append(jnp.where(half, fp[i], fp[i + 1]).astype(BF16))
            moments.append(jnp.where(half8, page[i, 64:72, :], page[i + 1, 64:72, :]))
        panel = value_of(dot(jnp.concatenate(sources, axis=1), own_target, CN))
        total = total + exact_dot(jnp.concatenate(moments, axis=1), panel, NN)
    dev[...] = twice(total * (1.0 / 64))


def assign(count_of, leaves, order):
    def tally(i, n):
        return n + (count_of(i) > 256).astype(jnp.int32)

    odd = lax.fori_loop(0, leaves, tally, jnp.int32(0)) & 1

    def deal(i, carry):
        large, taken = carry
        wide_leaf = (count_of(i) > 256).astype(jnp.int32)
        rank = jnp.where(wide_leaf == 1, large, i - large + odd)
        side = rank & 1
        place = jnp.where(side == 1, taken, i - taken)
        order[side * (leaves // 2) + place] = i
        return large + wide_leaf, taken + side

    lax.fori_loop(0, leaves, deal, (jnp.int32(0), jnp.int32(0)))


def clear_empty(empty, fs, ms):
    fs[empty] = jnp.zeros(fs.shape[1:], BF16)
    ms[empty] = jnp.zeros(ms.shape[1:], BF16)


def own_kernel(
    near, counts, me, page, partner, acc,
    fs, ms, ft, blocks, items, order, *slots, leaves, targets,
):
    c = center_of(page)
    assign(lambda i: counts[i], leaves, order)
    first = me[1] * targets

    def prep(t, carry):
        for s in range(8):
            i = 8 * t + s
            store_source(i, page, i, partner[i], c, fs, ms)
        for s in range(4):
            i = 4 * t + s
            store_target(i, page, order[first + i], c, ft)
        return carry

    lax.fori_loop(0, leaves // 8, prep, 0)
    clear_empty(leaves * 4, fs, ms)
    acc[...] = jnp.zeros_like(acc)

    def place(i, e):
        j = near[e, order[first + i]] - me[0] * leaves
        ok = (j >= 0) & (j < leaves)
        slot = jnp.where(ok, j, 0)
        return ok, slot, counts[slot]

    n = build_items(place, lambda i: counts[order[first + i]], targets, leaves * 4, blocks, items)
    run_items(items, n, fs, ft, ms, acc, slots)


def halo_kernel(
    near, counts, me, own, low, high, acc0,
    mine, theirs,
    acc, fs, ms, ft, blocks, items, order, *slots, leaves, targets, factor,
):
    c = center_of(own)
    assign(lambda i: counts[leaves + i], leaves, order)
    first = me[1] * targets

    def prep(t, carry):
        for s in range(4):
            i = 4 * t + s
            store_source(i, low, i, partner_of(low, i), c, fs, ms)
            store_source(leaves + i, high, i, partner_of(high, i), c, fs, ms)
        for s in range(2):
            i = 2 * t + s
            store_target(i, own, order[first + i], c, ft)
        return carry

    lax.fori_loop(0, leaves // 4, prep, 0)
    empty = 2 * leaves * 4
    clear_empty(empty, fs, ms)
    acc[...] = acc0[...]

    def place(i, e):
        j = near[e, order[first + i]] - (me[0] - 1) * leaves
        ok = (j < leaves) | (j >= 2 * leaves)
        slot = jnp.where(ok, jnp.where(j < leaves, j, j - leaves), 0)
        return ok, slot, counts[jnp.where(ok, j, 0)]

    n = build_items(place, lambda i: counts[leaves + order[first + i]], targets, empty, blocks, items)
    run_items(items, n, fs, ft, ms, acc, slots)
    scale = SLOPE * factor

    def finish(t, carry):
        for s in range(4):
            i = 4 * t + s
            for b in range(2):
                total = acc[2 * i + b]
                total = (total[0:16] + total[16:32]) * scale
                mine[i, :, b * 256 : (b + 1) * 256] = total[0:8]
                theirs[i, :, b * 256 : (b + 1) * 256] = total[8:16]
        return carry

    lax.fori_loop(0, targets // 4, finish, 0)


def far_sum(lists, count, source_of, moment_of, target):
    half = left_half((FEATURES, 128))
    half8 = left_half((8, 128))
    total = jnp.zeros((8, 64), F32)
    for chunk in range(count // 8):
        sources, moments = [], []
        for q in range(4):
            a, b = lists(chunk * 8 + 2 * q), lists(chunk * 8 + 2 * q + 1)
            sources.append(jnp.where(half, source_of(a), source_of(b)).astype(BF16))
            moments.append(jnp.where(half8, moment_of(a), moment_of(b)))
        sources = jnp.concatenate(sources, axis=1)
        moments = jnp.concatenate(moments, axis=1)
        total = total + exact_dot(moments, slope_of(dot(sources, target, CN)), NN)
    return total * (SLOPE / 64)


def shared(left, right):
    half = left_half(left.shape)
    pair = [jnp.where(half, left, 0.0), jnp.where(half, 0.0, right)]
    return jnp.concatenate(pair, axis=0).astype(BF16)


def own_halves(rows):
    return jnp.where(left_half((8, 128)), rows[0:8], rows[8:16])


def far_pair(lists, source_of, moment_of, target):
    half = left_half((FEATURES, 128))
    half8 = left_half((8, 128))
    total = jnp.zeros((16, 128), F32)
    for chunk in range(4):
        sources, moments = [], []
        for of in lists:
            row, moment = [], []
            for q in range(4):
                a, b = of(chunk * 8 + 2 * q), of(chunk * 8 + 2 * q + 1)
                row.append(jnp.where(half, source_of(a), source_of(b)).astype(BF16))
                moment.append(jnp.where(half8, moment_of(a), moment_of(b)))
            sources.append(jnp.concatenate(row, axis=1))
            moments.append(jnp.concatenate(moment, axis=1))
        panel = slope_of(dot(jnp.concatenate(sources, axis=0), target, CN))
        total = total + exact_dot(jnp.concatenate(moments, axis=0), panel, NN)
    return own_halves(total) * (SLOPE / 64)


def upper_levels(coarse, me, box8, roots, c, fbs, fbt, pm, qm):
    def prep(t, carry):
        for s in range(8):
            b = 8 * t + s
            fbs[b], fbt[b] = features(twice(rows_of(box8, b, 0.0)), c, True, True)
        return carry

    lax.fori_loop(0, 7, prep, 0)
    half = left_half((FEATURES, 128))
    half8 = left_half((8, 128))

    def merge(child, parent, moments, out, count):
        def body(t, carry):
            for s in range(8):
                m = t * 8 + s
                source = jnp.where(half, fbs[child + 2 * m], fbs[child + 2 * m + 1]).astype(BF16)
                target = fbt[parent + m].astype(BF16)[:, :64]
                panel = value_of(dot(source, target, CN))
                pair = jnp.where(half8, moments[2 * m], moments[2 * m + 1])
                out[m] = twice(exact_dot(pair, panel, NN) * (1.0 / 64))
            return carry

        lax.fori_loop(0, count // 8, body, 0)

    merge(0, 32, roots, pm, 16)
    merge(32, 48, pm, qm, 8)
    n = me
    m = n >> 1
    t = n >> 2

    def far(base, row, moments):
        target = fbt[row].astype(BF16)[:, :64]
        return far_sum(
            lambda e: coarse[e, row], 16, lambda b: fbs[base + b], lambda b: moments[b], target
        )

    def down(local, source, target):
        panel = value_of(dot(fbs[source].astype(BF16)[:, :64], fbt[target].astype(BF16)[:, :64], CN))
        return exact_dot(local, panel, NN) * (1.0 / 64)

    quad = far(48, 48 + t, qm)
    pair = down(quad, 48 + t, 32 + m) + far(32, 32 + m, pm)
    return down(pair, 32 + m, n) + far(0, n, roots)


def far_kernel(
    far, coarse, me, own, low, high, box8, roots,
    out,
    fps, fpt, mps, fbs, fbt, pm, qm, local,
    *, leaves, factor,
):
    c = center_of(own)

    def prep_far(t, carry):
        for s in range(4):
            i = t * 4 + s
            for k, (page, at) in enumerate(((low, 0), (own, 64), (high, 0))):
                (fps[k * leaves + i],) = features(page[i, at + 8 : at + 16], c, True, False)
                mps[k * leaves + i] = page[i, at : at + 8]
            (fpt[i],) = features(own[i, 72:80], c, False, True)
        return carry

    lax.fori_loop(0, leaves // 4, prep_far, 0)
    dev = me[0]
    base = (dev - 1) * leaves

    def gather(t, carry):
        for s in range(2):
            k = t * 2 + s
            local[k] = far_pair(
                [lambda e: far[2 * k, e] - base, lambda e: far[2 * k + 1, e] - base],
                lambda b: fps[b], lambda b: mps[b], shared(fpt[2 * k], fpt[2 * k + 1]),
            )
        return carry

    lax.fori_loop(0, leaves // 4, gather, 0)
    local_dev = upper_levels(coarse, dev, box8, roots, c, fbs, fbt, pm, qm)
    own_source = fbs[dev].astype(BF16)[:, :64]
    half = left_half((FEATURES, 128))

    def down(t, carry):
        for s in range(8):
            k = t * 8 + s
            target = jnp.where(half, fpt[2 * k], fpt[2 * k + 1]).astype(BF16)
            panel = value_of(dot(own_source, target, CN))
            local[k] += exact_dot(local_dev, panel, NN) * (1.0 / 64)
        return carry

    lax.fori_loop(0, leaves // 16, down, 0)

    def finish(t, carry):
        for s in range(8):
            i = t * 8 + s
            source = fps[leaves + i].astype(BF16)[:, :64]
            (points,) = features(lanes_of(own, i, 8), c, False, True)
            basis = value_of(dot(source, points.astype(BF16), CN))
            part = local[t * 4 + s // 2][:, (s % 2) * 64 : (s % 2) * 64 + 64]
            out[i] = exact_dot(part, basis, NN) * factor
        return carry

    lax.fori_loop(0, leaves // 8, finish, 0)


def sum_kernel(counts, me, far, mine, back, out, order, *, leaves):
    assign(lambda i: counts[i], leaves, order)
    half = leaves // 2
    lane = lax.broadcasted_iota(jnp.int32, far.shape[1:], 1)

    def body(t, carry):
        for s in range(4):
            k = 4 * t + s
            for side, part in ((me[1], mine), (1 - me[1], back)):
                i = order[side * half + k]
                out[i] = jnp.where(lane < counts[i], far[i] + part[k], 0.0)
        return carry

    lax.fori_loop(0, half // 4, body, 0)


def cost(microseconds):
    flops = int(microseconds * 1.1e9)
    return pl.CostEstimate(flops=flops, transcendentals=0, bytes_accessed=1 << 20)


def local(points, probes, counts, near_list, far_list, coarse_list, leaf_proxy, box_proxy):
    leaves = points.shape[0]
    size = points.shape[2]
    nodes = lax.axis_size("space")
    device = lax.axis_index("space")
    factor = size ** (-0.5)
    half = lax.axis_index("probe") & 1
    me = jnp.stack([device, half]).astype(jnp.int32)
    points = jnp.transpose(points, (1, 0, 2))
    leafp = jnp.transpose(leaf_proxy, (1, 0, 2))
    boxp = jnp.transpose(box_proxy, (1, 0, 2))
    near = near_list.T
    forward = [(i, i + 1) for i in range(nodes - 1)]
    backward = [(i + 1, i) for i in range(nodes - 1)]
    pairs = [(i, i ^ 1) for i in range(lax.axis_size("probe"))]
    partner = lax.ppermute(probes, "probe", pairs)
    params = pltpu.CompilerParams(vmem_limit_bytes=56 << 20)
    vm = pltpu.VMEM
    vmem = pl.BlockSpec(memory_space=vm)
    smem = pl.BlockSpec(memory_space=pltpu.SMEM)
    shape = jax.ShapeDtypeStruct
    page, dev = pl.pallas_call(
        functools.partial(moments_kernel, leaves=leaves, factor=factor),
        out_shape=(shape((leaves, 80, 128), F32), shape((8, 128), F32)),
        in_specs=[smem] * 2 + [vmem] * 4,
        out_specs=(vmem, vmem),
        scratch_shapes=[vm((leaves, FEATURES, 128), F32)],
        compiler_params=params,
        cost_estimate=cost(8),
        name="moments",
    )(counts, me, probes, points, leafp, boxp)
    roots = lax.all_to_all(
        jnp.broadcast_to(dev[None], (nodes, 8, 128)), "space", split_axis=0, concat_axis=0, tiled=True
    )
    tiles = jnp.transpose(partner.reshape(leaves, 8, size // 128, 128), (0, 2, 1, 3))
    both = jnp.concatenate([page, tiles.reshape(leaves, size // 16, 128)], axis=1)
    low = lax.ppermute(both, "space", forward)
    high = lax.ppermute(both, "space", backward)
    targets = leaves // 2

    def work(blocks):
        return (
            [
                vm((blocks, FEATURES, 128), BF16),
                vm((blocks, 32, 128), BF16),
                vm((targets * 2, FEATURES, 256), BF16),
                pltpu.SMEM((48,), jnp.int32),
                pltpu.SMEM((targets * 32 + 64,), jnp.int32),
                pltpu.SMEM((leaves,), jnp.int32),
            ]
            + [vm((256, 256), F32)] * UNITS
        )

    page, roots = lax.optimization_barrier((page, roots))
    acc0 = pl.pallas_call(
        functools.partial(own_kernel, leaves=leaves, targets=targets),
        out_shape=shape((targets * 2, 32, 256), F32),
        in_specs=[smem] * 3 + [vmem] * 2,
        out_specs=vmem,
        scratch_shapes=work(leaves * 4 + 1),
        compiler_params=params,
        cost_estimate=cost(28),
        name="near_own",
    )(near, counts, me, page, partner)
    counts3 = jnp.concatenate(
        [low[:, 11, 0].astype(jnp.int32), counts, high[:, 11, 0].astype(jnp.int32)]
    )
    mine, theirs = pl.pallas_call(
        functools.partial(halo_kernel, leaves=leaves, targets=targets, factor=factor),
        out_shape=(shape((targets, 8, size), F32),) * 2,
        in_specs=[smem] * 3 + [vmem] * 4,
        out_specs=(vmem, vmem),
        scratch_shapes=[vm((targets * 2, 32, 256), F32)] + work(2 * leaves * 4 + 1),
        compiler_params=params,
        cost_estimate=cost(30),
        name="near_halo",
    )(near, counts3, me, page, low, high, acc0)
    back = lax.ppermute(theirs, "probe", pairs)
    whole = lambda dims: pl.BlockSpec(dims, lambda i: (0,) * len(dims))
    tail = pl.BlockSpec((leaves, 16, 128), lambda i: (0, 4, 0))
    far = pl.pallas_call(
        functools.partial(far_kernel, leaves=leaves, factor=factor),
        out_shape=shape(probes.shape, F32),
        grid=(1,),
        in_specs=[smem] * 3 + [whole(page.shape), tail, tail, whole(boxp.shape), whole(roots.shape)],
        out_specs=whole(probes.shape),
        scratch_shapes=[
            vm((3 * leaves, FEATURES, 128), F32),
            vm((leaves, FEATURES, 128), F32),
            vm((3 * leaves, 8, 128), F32),
            vm((56, FEATURES, 128), F32),
            vm((56, FEATURES, 128), F32),
            vm((nodes // 2, 8, 128), F32),
            vm((nodes // 4, 8, 128), F32),
            vm((leaves // 2, 8, 128), F32),
        ],
        compiler_params=params,
        cost_estimate=cost(30),
        name="far",
    )(far_list, coarse_list.T, me, page, low, high, boxp, roots)
    return pl.pallas_call(
        functools.partial(sum_kernel, leaves=leaves),
        out_shape=shape(probes.shape, F32),
        in_specs=[smem] * 2 + [vmem] * 3,
        out_specs=vmem,
        scratch_shapes=[pltpu.SMEM((leaves,), jnp.int32)],
        compiler_params=params,
        name="sum",
    )(counts, me, far, mine, back)


def solution(mesh):
    return jax.shard_map(
        local,
        mesh=mesh,
        in_specs=(
            P("space", None, None),
            P("space", "probe", None),
            P("space"),
            P("space", None),
            P("space", None),
            P(),
            P("space", None, None),
            P(),
        ),
        out_specs=P("space", "probe", None),
        check_vma=False,
    )
```

```python
import functools

import jax
import jax.numpy as jnp
from jax import lax
from jax.experimental import pallas as pl
from jax.experimental.pallas import tpu as pltpu
from jax.sharding import PartitionSpec as P

F32 = jnp.float32
BF16 = jnp.bfloat16
LOG2E = 1.4426950408889634
LN2 = 0.6931471805599453
SCALE = LOG2E * 1.7320508075688772 / 2.0
SLOPE = 0.5 / (LOG2E * LOG2E)
TINY = 1e-30
FEATURES = 48
UNITS = 12
CN = (((0,), (0,)), ((), ()))
NT = (((1,), (1,)), ((), ()))
NN = (((1,), (0,)), ((), ()))


def dot(left, right, dims):
    return lax.dot_general(left, right, dims, preferred_element_type=F32)


def split(value):
    high = value.astype(BF16)
    return high, (value - high.astype(F32)).astype(BF16)


def stacked(value):
    high = value.astype(BF16).astype(F32)
    return jnp.concatenate([high, value - high], axis=0).astype(BF16)


def exact_dot(left, right, dims):
    rows = left.shape[0]
    high, low = split(right)
    both = stacked(left)
    total = dot(both, high, dims) + dot(both, low, dims)
    return total[:rows] + total[rows:]


def slope_of(u):
    u = jnp.maximum(u, TINY)
    return u * jnp.exp2(-(u * lax.rsqrt(u)))


def value_of(u):
    u = jnp.maximum(u, TINY)
    w = u * lax.rsqrt(u)
    return (1.0 + LN2 * w) * jnp.exp2(-w)


def pieces(value):
    high = value.astype(BF16).astype(F32)
    rest = value - high
    middle = rest.astype(BF16).astype(F32)
    return high, middle, rest - middle


def features(rows, center, source, target):
    row = lax.broadcasted_iota(jnp.int32, rows.shape, 0)
    scaled = jnp.where(row < 3, (rows - center) * SCALE, 0.0)
    norm = jnp.sum(scaled * scaled, axis=0, keepdims=True)
    out = []
    if source:
        h, m, l = pieces(jnp.where(row == 3, norm, jnp.where(row == 4, 1.0, scaled)))
        out.append(jnp.concatenate([h, h, m, h, l, m], axis=0))
    if target:
        h, m, l = pieces(jnp.where(row == 3, 1.0, jnp.where(row == 4, norm, -2.0 * scaled)))
        out.append(jnp.concatenate([h, m, h, l, h, m], axis=0))
    return out


def twice(value):
    return jnp.concatenate([value, value], axis=1)


def left_half(shape):
    return lax.broadcasted_iota(jnp.int32, shape, 1) < 64


def lanes_of(page, i, start):
    return jnp.concatenate([page[i, 16 * b + start : 16 * b + start + 8, :] for b in range(4)], axis=1)


def partner_of(page, i):
    return jnp.concatenate([page[i, 80 + 8 * b : 88 + 8 * b, :] for b in range(4)], axis=1)


def center_of(page):
    return page[0, 8:16, 0:1]


def store_source(slot, page, i, partner, center, fs, ms):
    rows = lanes_of(page, i, 8)
    (source,) = features(rows, center, True, False)
    source = source.astype(BF16)
    lane = lax.broadcasted_iota(jnp.int32, partner.shape, 1).astype(F32)
    other = jnp.where(lane < rows[3:4], partner, 0.0)
    moments = stacked(jnp.concatenate([lanes_of(page, i, 0), other], axis=0))
    for b in range(4):
        fs[slot * 4 + b] = source[:, b * 128 : (b + 1) * 128]
        ms[slot * 4 + b] = moments[:, b * 128 : (b + 1) * 128]


def store_target(slot, page, i, center, ft):
    (target,) = features(lanes_of(page, i, 8), center, False, True)
    target = target.astype(BF16)
    for b in range(2):
        ft[slot * 2 + b] = target[:, b * 256 : (b + 1) * 256]


def build_items(place, target_count, targets, empty, blocks, items):
    def per_leaf(i, n):
        nb = jnp.int32(0)
        for e in range(8):
            ok, slot, count = place(i, e)
            for b in range(4):
                blocks[nb + b] = slot * 4 + b
            nb = nb + jnp.where(ok, (count + 127) >> 7, 0)
        blocks[nb] = empty
        pairs = (nb + 1) >> 1

        def put(q, carry):
            code = (blocks[2 * q] << 9) | blocks[2 * q + 1]
            items[n + q] = code | ((2 * i) << 18)
            items[n + pairs + q] = code | ((2 * i + 1) << 18)
            return carry

        lax.fori_loop(0, pairs, put, 0)
        return n + jnp.where(target_count(i) > 256, 2 * pairs, pairs)

    n = lax.fori_loop(0, targets, per_leaf, jnp.int32(0))
    for t in range(2 * UNITS):
        items[n + t] = (empty << 9) | empty
    return n


def run_items(items, n, fs, ft, ms, acc, slots):
    def distances(code, u):
        left = jnp.concatenate([fs[(code >> 9) & 511], fs[code & 511]], axis=1)
        u[...] = dot(left, ft[code >> 18], CN)

    def contract(code, u):
        high, low = split(slope_of(u[...]))
        m = jnp.concatenate([ms[(code >> 9) & 511], ms[code & 511]], axis=1)
        acc[code >> 18] += dot(m, high, NN) + dot(m, low, NN)

    for s in range(UNITS):
        distances(items[s], slots[s])

    def body(t, carry):
        for s in range(UNITS):
            contract(items[UNITS * t + s], slots[s])
            distances(items[UNITS * (t + 1) + s], slots[s])
        return carry

    lax.fori_loop(0, (n + UNITS - 1) // UNITS, body, 0)


def rows_of(planes, i, extra):
    rows = [planes[d, pl.ds(i, 1), :] for d in range(3)]
    width = rows[0].shape[1]
    return jnp.concatenate(
        rows + [jnp.full((1, width), extra, F32), jnp.zeros((4, width), F32)], axis=0
    )


def moments_kernel(counts, me, probes, points, leafp, boxp, page, dev, fp, *, leaves, factor):
    c = rows_of(points, 0, 0.0)[:, 0:1]
    (own_target,) = features(rows_of(boxp, me[0], 0.0), c, False, True)
    own_target = own_target.astype(BF16)
    lane = lax.broadcasted_iota(jnp.int32, probes.shape[1:], 1)

    def prep(i):
        count = counts[i]
        masked = jnp.where(lane < count, probes[i], 0.0)
        rows = rows_of(points, i, count.astype(F32))
        for b in range(4):
            page[i, 16 * b : 16 * b + 8, :] = masked[:, b * 128 : (b + 1) * 128]
            page[i, 16 * b + 8 : 16 * b + 16, :] = rows[:, b * 128 : (b + 1) * 128]
        proxies = twice(rows_of(leafp, i, 0.0))
        page[i, 72:80, :] = proxies
        (target,) = features(rows, c, False, True)
        (fp[i],) = features(proxies, c, True, False)
        return masked, target.astype(BF16)

    def body(t, carry):
        for s in range(4):
            i = t * 8 + 2 * s
            (left, left_points), (right, right_points) = prep(i), prep(i + 1)
            both = jnp.concatenate([left_points, right_points], axis=0)
            basis = value_of(dot(both, shared(fp[i], fp[i + 1]), CN))
            pair = exact_dot(jnp.concatenate([left, right], axis=0), basis, NN) * factor
            page[i, 64:72, :] = twice(pair[0:8, 0:64])
            page[i + 1, 64:72, :] = twice(pair[8:16, 64:128])
        return carry

    lax.fori_loop(0, leaves // 8, body, 0)
    half = left_half((FEATURES, 128))
    half8 = left_half((8, 128))
    total = jnp.zeros((8, 64), F32)
    for g in range(leaves // 8):
        sources, moments = [], []
        for q in range(4):
            i = 8 * g + 2 * q
            sources.append(jnp.where(half, fp[i], fp[i + 1]).astype(BF16))
            moments.append(jnp.where(half8, page[i, 64:72, :], page[i + 1, 64:72, :]))
        panel = value_of(dot(jnp.concatenate(sources, axis=1), own_target, CN))
        total = total + exact_dot(jnp.concatenate(moments, axis=1), panel, NN)
    dev[...] = twice(total * (1.0 / 64))


def assign(count_of, leaves, order):
    def tally(i, n):
        return n + (count_of(i) > 256).astype(jnp.int32)

    odd = lax.fori_loop(0, leaves, tally, jnp.int32(0)) & 1

    def deal(i, carry):
        large, taken = carry
        wide_leaf = (count_of(i) > 256).astype(jnp.int32)
        rank = jnp.where(wide_leaf == 1, large, i - large + odd)
        side = rank & 1
        place = jnp.where(side == 1, taken, i - taken)
        order[side * (leaves // 2) + place] = i
        return large + wide_leaf, taken + side

    lax.fori_loop(0, leaves, deal, (jnp.int32(0), jnp.int32(0)))


def clear_empty(empty, fs, ms):
    fs[empty] = jnp.zeros(fs.shape[1:], BF16)
    ms[empty] = jnp.zeros(ms.shape[1:], BF16)


def own_kernel(
    near, counts, me, page, partner, acc,
    fs, ms, ft, blocks, items, order, *slots, leaves, targets,
):
    c = center_of(page)
    assign(lambda i: counts[i], leaves, order)
    first = me[1] * targets

    def prep(t, carry):
        for s in range(8):
            i = 8 * t + s
            store_source(i, page, i, partner[i], c, fs, ms)
        for s in range(4):
            i = 4 * t + s
            store_target(i, page, order[first + i], c, ft)
        return carry

    lax.fori_loop(0, leaves // 8, prep, 0)
    clear_empty(leaves * 4, fs, ms)
    acc[...] = jnp.zeros_like(acc)

    def place(i, e):
        j = near[e, order[first + i]] - me[0] * leaves
        ok = (j >= 0) & (j < leaves)
        slot = jnp.where(ok, j, 0)
        return ok, slot, counts[slot]

    n = build_items(place, lambda i: counts[order[first + i]], targets, leaves * 4, blocks, items)
    run_items(items, n, fs, ft, ms, acc, slots)


def halo_kernel(
    near, counts, me, own, low, high, acc0,
    mine, theirs,
    acc, fs, ms, ft, blocks, items, order, *slots, leaves, targets, factor,
):
    c = center_of(own)
    assign(lambda i: counts[leaves + i], leaves, order)
    first = me[1] * targets

    def prep(t, carry):
        for s in range(4):
            i = 4 * t + s
            store_source(i, low, i, partner_of(low, i), c, fs, ms)
            store_source(leaves + i, high, i, partner_of(high, i), c, fs, ms)
        for s in range(2):
            i = 2 * t + s
            store_target(i, own, order[first + i], c, ft)
        return carry

    lax.fori_loop(0, leaves // 4, prep, 0)
    empty = 2 * leaves * 4
    clear_empty(empty, fs, ms)
    acc[...] = acc0[...]

    def place(i, e):
        j = near[e, order[first + i]] - (me[0] - 1) * leaves
        ok = (j < leaves) | (j >= 2 * leaves)
        slot = jnp.where(ok, jnp.where(j < leaves, j, j - leaves), 0)
        return ok, slot, counts[jnp.where(ok, j, 0)]

    n = build_items(place, lambda i: counts[leaves + order[first + i]], targets, empty, blocks, items)
    run_items(items, n, fs, ft, ms, acc, slots)
    scale = SLOPE * factor

    def finish(t, carry):
        for s in range(4):
            i = 4 * t + s
            for b in range(2):
                total = acc[2 * i + b]
                total = (total[0:16] + total[16:32]) * scale
                mine[i, :, b * 256 : (b + 1) * 256] = total[0:8]
                theirs[i, :, b * 256 : (b + 1) * 256] = total[8:16]
        return carry

    lax.fori_loop(0, targets // 4, finish, 0)


def far_sum(lists, count, source_of, moment_of, target):
    half = left_half((FEATURES, 128))
    half8 = left_half((8, 128))
    total = jnp.zeros((8, 64), F32)
    for chunk in range(count // 8):
        sources, moments = [], []
        for q in range(4):
            a, b = lists(chunk * 8 + 2 * q), lists(chunk * 8 + 2 * q + 1)
            sources.append(jnp.where(half, source_of(a), source_of(b)).astype(BF16))
            moments.append(jnp.where(half8, moment_of(a), moment_of(b)))
        sources = jnp.concatenate(sources, axis=1)
        moments = jnp.concatenate(moments, axis=1)
        total = total + exact_dot(moments, slope_of(dot(sources, target, CN)), NN)
    return total * (SLOPE / 64)


def shared(left, right):
    half = left_half(left.shape)
    pair = [jnp.where(half, left, 0.0), jnp.where(half, 0.0, right)]
    return jnp.concatenate(pair, axis=0).astype(BF16)


def own_halves(rows):
    return jnp.where(left_half((8, 128)), rows[0:8], rows[8:16])


def far_pair(lists, source_of, moment_of, target):
    half = left_half((FEATURES, 128))
    half8 = left_half((8, 128))
    total = jnp.zeros((16, 128), F32)
    for chunk in range(4):
        sources, moments = [], []
        for of in lists:
            row, moment = [], []
            for q in range(4):
                a, b = of(chunk * 8 + 2 * q), of(chunk * 8 + 2 * q + 1)
                row.append(jnp.where(half, source_of(a), source_of(b)).astype(BF16))
                moment.append(jnp.where(half8, moment_of(a), moment_of(b)))
            sources.append(jnp.concatenate(row, axis=1))
            moments.append(jnp.concatenate(moment, axis=1))
        panel = slope_of(dot(jnp.concatenate(sources, axis=0), target, CN))
        total = total + exact_dot(jnp.concatenate(moments, axis=0), panel, NN)
    return own_halves(total) * (SLOPE / 64)


def upper_levels(coarse, me, box8, roots, c, fbs, fbt, pm, qm):
    def prep(t, carry):
        for s in range(14):
            b = 14 * t + s
            fbs[b], fbt[b] = features(twice(rows_of(box8, b, 0.0)), c, True, True)
        return carry

    lax.fori_loop(0, 4, prep, 0)
    half = left_half((FEATURES, 128))
    half8 = left_half((8, 128))

    def merge(child, parent, moments, out, count):
        def body(t, carry):
            for s in range(8):
                m = t * 8 + s
                source = jnp.where(half, fbs[child + 2 * m], fbs[child + 2 * m + 1]).astype(BF16)
                target = fbt[parent + m].astype(BF16)[:, :64]
                panel = value_of(dot(source, target, CN))
                pair = jnp.where(half8, moments[2 * m], moments[2 * m + 1])
                out[m] = twice(exact_dot(pair, panel, NN) * (1.0 / 64))
            return carry

        lax.fori_loop(0, count // 8, body, 0)

    merge(0, 32, roots, pm, 16)
    merge(32, 48, pm, qm, 8)
    n = me
    m = n >> 1
    t = n >> 2

    def far(base, row, moments):
        target = fbt[row].astype(BF16)[:, :64]
        return far_sum(
            lambda e: coarse[e, row], 16, lambda b: fbs[base + b], lambda b: moments[b], target
        )

    def down(local, source, target):
        panel = value_of(dot(fbs[source].astype(BF16)[:, :64], fbt[target].astype(BF16)[:, :64], CN))
        return exact_dot(local, panel, NN) * (1.0 / 64)

    quad = far(48, 48 + t, qm)
    pair = down(quad, 48 + t, 32 + m) + far(32, 32 + m, pm)
    return down(pair, 32 + m, n) + far(0, n, roots)


def far_kernel(
    far, coarse, me, own, low, high, box8, roots,
    out,
    fps, fpt, mps, fbs, fbt, pm, qm, local,
    *, leaves, factor,
):
    c = center_of(own)

    def prep_far(t, carry):
        for s in range(8):
            i = t * 8 + s
            for k, (page, at) in enumerate(((low, 0), (own, 64), (high, 0))):
                (fps[k * leaves + i],) = features(page[i, at + 8 : at + 16], c, True, False)
                mps[k * leaves + i] = page[i, at : at + 8]
            (fpt[i],) = features(own[i, 72:80], c, False, True)
        return carry

    lax.fori_loop(0, leaves // 8, prep_far, 0)
    dev = me[0]
    base = (dev - 1) * leaves

    def gather(t, carry):
        for s in range(4):
            k = t * 4 + s
            local[k] = far_pair(
                [lambda e: far[2 * k, e] - base, lambda e: far[2 * k + 1, e] - base],
                lambda b: fps[b], lambda b: mps[b], shared(fpt[2 * k], fpt[2 * k + 1]),
            )
        return carry

    lax.fori_loop(0, leaves // 8, gather, 0)
    local_dev = upper_levels(coarse, dev, box8, roots, c, fbs, fbt, pm, qm)
    own_source = fbs[dev].astype(BF16)[:, :64]
    half = left_half((FEATURES, 128))

    def down(t, carry):
        for s in range(8):
            k = t * 8 + s
            target = jnp.where(half, fpt[2 * k], fpt[2 * k + 1]).astype(BF16)
            panel = value_of(dot(own_source, target, CN))
            local[k] += exact_dot(local_dev, panel, NN) * (1.0 / 64)
        return carry

    lax.fori_loop(0, leaves // 16, down, 0)

    def finish(t, carry):
        for s in range(16):
            i = t * 16 + s
            source = fps[leaves + i].astype(BF16)[:, :64]
            (points,) = features(lanes_of(own, i, 8), c, False, True)
            basis = value_of(dot(source, points.astype(BF16), CN))
            part = local[t * 8 + s // 2][:, (s % 2) * 64 : (s % 2) * 64 + 64]
            out[i] = exact_dot(part, basis, NN) * factor
        return carry

    lax.fori_loop(0, leaves // 16, finish, 0)


def sum_kernel(counts, me, far, mine, back, out, order, *, leaves):
    assign(lambda i: counts[i], leaves, order)
    half = leaves // 2
    lane = lax.broadcasted_iota(jnp.int32, far.shape[1:], 1)

    def body(t, carry):
        for s in range(4):
            k = 4 * t + s
            for side, part in ((me[1], mine), (1 - me[1], back)):
                i = order[side * half + k]
                out[i] = jnp.where(lane < counts[i], far[i] + part[k], 0.0)
        return carry

    lax.fori_loop(0, half // 4, body, 0)


def cost(microseconds):
    flops = int(microseconds * 1.1e9)
    return pl.CostEstimate(flops=flops, transcendentals=0, bytes_accessed=1 << 20)


def local(points, probes, counts, near_list, far_list, coarse_list, leaf_proxy, box_proxy):
    leaves = points.shape[0]
    size = points.shape[2]
    nodes = lax.axis_size("space")
    device = lax.axis_index("space")
    factor = size ** (-0.5)
    half = lax.axis_index("probe") & 1
    me = jnp.stack([device, half]).astype(jnp.int32)
    points = jnp.transpose(points, (1, 0, 2))
    leafp = jnp.transpose(leaf_proxy, (1, 0, 2))
    boxp = jnp.transpose(box_proxy, (1, 0, 2))
    near = near_list.T
    forward = [(i, i + 1) for i in range(nodes - 1)]
    backward = [(i + 1, i) for i in range(nodes - 1)]
    pairs = [(i, i ^ 1) for i in range(lax.axis_size("probe"))]
    partner = lax.ppermute(probes, "probe", pairs)
    params = pltpu.CompilerParams(vmem_limit_bytes=56 << 20)
    vm = pltpu.VMEM
    vmem = pl.BlockSpec(memory_space=vm)
    smem = pl.BlockSpec(memory_space=pltpu.SMEM)
    shape = jax.ShapeDtypeStruct
    page, dev = pl.pallas_call(
        functools.partial(moments_kernel, leaves=leaves, factor=factor),
        out_shape=(shape((leaves, 80, 128), F32), shape((8, 128), F32)),
        in_specs=[smem] * 2 + [vmem] * 4,
        out_specs=(vmem, vmem),
        scratch_shapes=[vm((leaves, FEATURES, 128), F32)],
        compiler_params=params,
        cost_estimate=cost(8),
        name="moments",
    )(counts, me, probes, points, leafp, boxp)
    roots = lax.all_to_all(
        jnp.broadcast_to(dev[None], (nodes, 8, 128)), "space", split_axis=0, concat_axis=0, tiled=True
    )
    tiles = jnp.transpose(partner.reshape(leaves, 8, size // 128, 128), (0, 2, 1, 3))
    both = jnp.concatenate([page, tiles.reshape(leaves, size // 16, 128)], axis=1)
    low = lax.ppermute(both, "space", forward)
    high = lax.ppermute(both, "space", backward)
    targets = leaves // 2

    def work(blocks):
        return (
            [
                vm((blocks, FEATURES, 128), BF16),
                vm((blocks, 32, 128), BF16),
                vm((targets * 2, FEATURES, 256), BF16),
                pltpu.SMEM((48,), jnp.int32),
                pltpu.SMEM((targets * 32 + 96,), jnp.int32),
                pltpu.SMEM((leaves,), jnp.int32),
            ]
            + [vm((256, 256), F32)] * UNITS
        )

    page, roots = lax.optimization_barrier((page, roots))
    acc0 = pl.pallas_call(
        functools.partial(own_kernel, leaves=leaves, targets=targets),
        out_shape=shape((targets * 2, 32, 256), F32),
        in_specs=[smem] * 3 + [vmem] * 2,
        out_specs=vmem,
        scratch_shapes=work(leaves * 4 + 1),
        compiler_params=params,
        cost_estimate=cost(28),
        name="near_own",
    )(near, counts, me, page, partner)
    counts3 = jnp.concatenate(
        [low[:, 11, 0].astype(jnp.int32), counts, high[:, 11, 0].astype(jnp.int32)]
    )
    mine, theirs = pl.pallas_call(
        functools.partial(halo_kernel, leaves=leaves, targets=targets, factor=factor),
        out_shape=(shape((targets, 8, size), F32),) * 2,
        in_specs=[smem] * 3 + [vmem] * 4,
        out_specs=(vmem, vmem),
        scratch_shapes=[vm((targets * 2, 32, 256), F32)] + work(2 * leaves * 4 + 1),
        compiler_params=params,
        cost_estimate=cost(30),
        name="near_halo",
    )(near, counts3, me, page, low, high, acc0)
    back = lax.ppermute(theirs, "probe", pairs)
    whole = lambda dims: pl.BlockSpec(dims, lambda i: (0,) * len(dims))
    tail = pl.BlockSpec((leaves, 16, 128), lambda i: (0, 4, 0))
    far = pl.pallas_call(
        functools.partial(far_kernel, leaves=leaves, factor=factor),
        out_shape=shape(probes.shape, F32),
        grid=(1,),
        in_specs=[smem] * 3 + [whole(page.shape), tail, tail, whole(boxp.shape), whole(roots.shape)],
        out_specs=whole(probes.shape),
        scratch_shapes=[
            vm((3 * leaves, FEATURES, 128), F32),
            vm((leaves, FEATURES, 128), F32),
            vm((3 * leaves, 8, 128), F32),
            vm((56, FEATURES, 128), F32),
            vm((56, FEATURES, 128), F32),
            vm((nodes // 2, 8, 128), F32),
            vm((nodes // 4, 8, 128), F32),
            vm((leaves // 2, 8, 128), F32),
        ],
        compiler_params=params,
        cost_estimate=cost(30),
        name="far",
    )(far_list, coarse_list.T, me, page, low, high, boxp, roots)
    return pl.pallas_call(
        functools.partial(sum_kernel, leaves=leaves),
        out_shape=shape(probes.shape, F32),
        in_specs=[smem] * 2 + [vmem] * 3,
        out_specs=vmem,
        scratch_shapes=[pltpu.SMEM((leaves,), jnp.int32)],
        compiler_params=params,
        name="sum",
    )(counts, me, far, mine, back)


def solution(mesh):
    return jax.shard_map(
        local,
        mesh=mesh,
        in_specs=(
            P("space", None, None),
            P("space", "probe", None),
            P("space"),
            P("space", None),
            P("space", None),
            P(),
            P("space", None, None),
            P(),
        ),
        out_specs=P("space", "probe", None),
        check_vma=False,
    )
```

```python
import functools

import jax
import jax.numpy as jnp
from jax import lax
from jax.experimental import pallas as pl
from jax.experimental.pallas import tpu as pltpu
from jax.sharding import PartitionSpec as P

F32 = jnp.float32
BF16 = jnp.bfloat16
LOG2E = 1.4426950408889634
LN2 = 0.6931471805599453
SCALE = LOG2E * 1.7320508075688772 / 2.0
SLOPE = 0.5 / (LOG2E * LOG2E)
TINY = 1e-30
FEATURES = 48
UNITS = 16
CN = (((0,), (0,)), ((), ()))
NT = (((1,), (1,)), ((), ()))
NN = (((1,), (0,)), ((), ()))


def dot(left, right, dims):
    return lax.dot_general(left, right, dims, preferred_element_type=F32)


def split(value):
    high = value.astype(BF16)
    return high, (value - high.astype(F32)).astype(BF16)


def stacked(value):
    high = value.astype(BF16).astype(F32)
    return jnp.concatenate([high, value - high], axis=0).astype(BF16)


def exact_dot(left, right, dims):
    rows = left.shape[0]
    high, low = split(right)
    both = stacked(left)
    total = dot(both, high, dims) + dot(both, low, dims)
    return total[:rows] + total[rows:]


def slope_of(u):
    u = jnp.maximum(u, TINY)
    return u * jnp.exp2(-(u * lax.rsqrt(u)))


def value_of(u):
    u = jnp.maximum(u, TINY)
    w = u * lax.rsqrt(u)
    return (1.0 + LN2 * w) * jnp.exp2(-w)


def pieces(value):
    high = value.astype(BF16).astype(F32)
    rest = value - high
    middle = rest.astype(BF16).astype(F32)
    return high, middle, rest - middle


def features(rows, center, source, target):
    row = lax.broadcasted_iota(jnp.int32, rows.shape, 0)
    scaled = jnp.where(row < 3, (rows - center) * SCALE, 0.0)
    norm = jnp.sum(scaled * scaled, axis=0, keepdims=True)
    out = []
    if source:
        h, m, l = pieces(jnp.where(row == 3, norm, jnp.where(row == 4, 1.0, scaled)))
        out.append(jnp.concatenate([h, h, m, h, l, m], axis=0))
    if target:
        h, m, l = pieces(jnp.where(row == 3, 1.0, jnp.where(row == 4, norm, -2.0 * scaled)))
        out.append(jnp.concatenate([h, m, h, l, h, m], axis=0))
    return out


def twice(value):
    return jnp.concatenate([value, value], axis=1)


def left_half(shape):
    return lax.broadcasted_iota(jnp.int32, shape, 1) < 64


def lanes_of(page, i, start):
    return jnp.concatenate([page[i, 16 * b + start : 16 * b + start + 8, :] for b in range(4)], axis=1)


def partner_of(page, i):
    return jnp.concatenate([page[i, 80 + 8 * b : 88 + 8 * b, :] for b in range(4)], axis=1)


def center_of(page):
    return page[0, 8:16, 0:1]


def store_source(slot, page, i, partner, center, fs, ms):
    rows = lanes_of(page, i, 8)
    (source,) = features(rows, center, True, False)
    source = source.astype(BF16)
    lane = lax.broadcasted_iota(jnp.int32, partner.shape, 1).astype(F32)
    other = jnp.where(lane < rows[3:4], partner, 0.0)
    moments = stacked(jnp.concatenate([lanes_of(page, i, 0), other], axis=0))
    for b in range(4):
        fs[slot * 4 + b] = source[:, b * 128 : (b + 1) * 128]
        ms[slot * 4 + b] = moments[:, b * 128 : (b + 1) * 128]


def store_target(slot, page, i, center, ft):
    (target,) = features(lanes_of(page, i, 8), center, False, True)
    target = target.astype(BF16)
    for b in range(2):
        ft[slot * 2 + b] = target[:, b * 256 : (b + 1) * 256]


def build_items(place, target_count, targets, empty, blocks, items):
    def per_leaf(i, n):
        nb = jnp.int32(0)
        for e in range(8):
            ok, slot, count = place(i, e)
            for b in range(4):
                blocks[nb + b] = slot * 4 + b
            nb = nb + jnp.where(ok, (count + 127) >> 7, 0)
        blocks[nb] = empty
        pairs = (nb + 1) >> 1

        def put(q, carry):
            code = (blocks[2 * q] << 9) | blocks[2 * q + 1]
            items[n + q] = code | ((2 * i) << 18)
            items[n + pairs + q] = code | ((2 * i + 1) << 18)
            return carry

        lax.fori_loop(0, pairs, put, 0)
        return n + jnp.where(target_count(i) > 256, 2 * pairs, pairs)

    n = lax.fori_loop(0, targets, per_leaf, jnp.int32(0))
    for t in range(2 * UNITS):
        items[n + t] = (empty << 9) | empty
    return n


def run_items(items, n, fs, ft, ms, acc, slots):
    def distances(code, u):
        left = jnp.concatenate([fs[(code >> 9) & 511], fs[code & 511]], axis=1)
        u[...] = dot(left, ft[code >> 18], CN)

    def contract(code, u):
        high, low = split(slope_of(u[...]))
        m = jnp.concatenate([ms[(code >> 9) & 511], ms[code & 511]], axis=1)
        acc[code >> 18] += dot(m, high, NN) + dot(m, low, NN)

    for s in range(UNITS):
        distances(items[s], slots[s])

    def body(t, carry):
        for s in range(UNITS):
            contract(items[UNITS * t + s], slots[s])
            distances(items[UNITS * (t + 1) + s], slots[s])
        return carry

    lax.fori_loop(0, (n + UNITS - 1) // UNITS, body, 0)


def rows_of(planes, i, extra):
    rows = [planes[d, pl.ds(i, 1), :] for d in range(3)]
    width = rows[0].shape[1]
    return jnp.concatenate(
        rows + [jnp.full((1, width), extra, F32), jnp.zeros((4, width), F32)], axis=0
    )


def moments_kernel(counts, me, probes, points, leafp, boxp, page, dev, fp, *, leaves, factor):
    c = rows_of(points, 0, 0.0)[:, 0:1]
    (own_target,) = features(rows_of(boxp, me[0], 0.0), c, False, True)
    own_target = own_target.astype(BF16)
    lane = lax.broadcasted_iota(jnp.int32, probes.shape[1:], 1)

    def prep(i):
        count = counts[i]
        masked = jnp.where(lane < count, probes[i], 0.0)
        rows = rows_of(points, i, count.astype(F32))
        for b in range(4):
            page[i, 16 * b : 16 * b + 8, :] = masked[:, b * 128 : (b + 1) * 128]
            page[i, 16 * b + 8 : 16 * b + 16, :] = rows[:, b * 128 : (b + 1) * 128]
        proxies = twice(rows_of(leafp, i, 0.0))
        page[i, 72:80, :] = proxies
        (target,) = features(rows, c, False, True)
        (fp[i],) = features(proxies, c, True, False)
        return masked, target.astype(BF16)

    def body(t, carry):
        for s in range(4):
            i = t * 8 + 2 * s
            (left, left_points), (right, right_points) = prep(i), prep(i + 1)
            both = jnp.concatenate([left_points, right_points], axis=0)
            basis = value_of(dot(both, shared(fp[i], fp[i + 1]), CN))
            pair = exact_dot(jnp.concatenate([left, right], axis=0), basis, NN) * factor
            page[i, 64:72, :] = twice(pair[0:8, 0:64])
            page[i + 1, 64:72, :] = twice(pair[8:16, 64:128])
        return carry

    lax.fori_loop(0, leaves // 8, body, 0)
    half = left_half((FEATURES, 128))
    half8 = left_half((8, 128))
    total = jnp.zeros((8, 64), F32)
    for g in range(leaves // 8):
        sources, moments = [], []
        for q in range(4):
            i = 8 * g + 2 * q
            sources.append(jnp.where(half, fp[i], fp[i + 1]).astype(BF16))
            moments.append(jnp.where(half8, page[i, 64:72, :], page[i + 1, 64:72, :]))
        panel = value_of(dot(jnp.concatenate(sources, axis=1), own_target, CN))
        total = total + exact_dot(jnp.concatenate(moments, axis=1), panel, NN)
    dev[...] = twice(total * (1.0 / 64))


def assign(count_of, leaves, order):
    def tally(i, n):
        return n + (count_of(i) > 256).astype(jnp.int32)

    odd = lax.fori_loop(0, leaves, tally, jnp.int32(0)) & 1

    def deal(i, carry):
        large, taken = carry
        wide_leaf = (count_of(i) > 256).astype(jnp.int32)
        rank = jnp.where(wide_leaf == 1, large, i - large + odd)
        side = rank & 1
        place = jnp.where(side == 1, taken, i - taken)
        order[side * (leaves // 2) + place] = i
        return large + wide_leaf, taken + side

    lax.fori_loop(0, leaves, deal, (jnp.int32(0), jnp.int32(0)))


def clear_empty(empty, fs, ms):
    fs[empty] = jnp.zeros(fs.shape[1:], BF16)
    ms[empty] = jnp.zeros(ms.shape[1:], BF16)


def own_kernel(
    near, counts, me, page, partner, acc,
    fs, ms, ft, blocks, items, order, *slots, leaves, targets,
):
    c = center_of(page)
    assign(lambda i: counts[i], leaves, order)
    first = me[1] * targets

    def prep(t, carry):
        for s in range(8):
            i = 8 * t + s
            store_source(i, page, i, partner[i], c, fs, ms)
        for s in range(4):
            i = 4 * t + s
            store_target(i, page, order[first + i], c, ft)
        return carry

    lax.fori_loop(0, leaves // 8, prep, 0)
    clear_empty(leaves * 4, fs, ms)
    acc[...] = jnp.zeros_like(acc)

    def place(i, e):
        j = near[e, order[first + i]] - me[0] * leaves
        ok = (j >= 0) & (j < leaves)
        slot = jnp.where(ok, j, 0)
        return ok, slot, counts[slot]

    n = build_items(place, lambda i: counts[order[first + i]], targets, leaves * 4, blocks, items)
    run_items(items, n, fs, ft, ms, acc, slots)


def halo_kernel(
    near, counts, me, own, low, high, acc0,
    mine, theirs,
    acc, fs, ms, ft, blocks, items, order, *slots, leaves, targets, factor,
):
    c = center_of(own)
    assign(lambda i: counts[leaves + i], leaves, order)
    first = me[1] * targets

    def prep(t, carry):
        for s in range(4):
            i = 4 * t + s
            store_source(i, low, i, partner_of(low, i), c, fs, ms)
            store_source(leaves + i, high, i, partner_of(high, i), c, fs, ms)
        for s in range(2):
            i = 2 * t + s
            store_target(i, own, order[first + i], c, ft)
        return carry

    lax.fori_loop(0, leaves // 4, prep, 0)
    empty = 2 * leaves * 4
    clear_empty(empty, fs, ms)
    acc[...] = acc0[...]

    def place(i, e):
        j = near[e, order[first + i]] - (me[0] - 1) * leaves
        ok = (j < leaves) | (j >= 2 * leaves)
        slot = jnp.where(ok, jnp.where(j < leaves, j, j - leaves), 0)
        return ok, slot, counts[jnp.where(ok, j, 0)]

    n = build_items(place, lambda i: counts[leaves + order[first + i]], targets, empty, blocks, items)
    run_items(items, n, fs, ft, ms, acc, slots)
    scale = SLOPE * factor

    def finish(t, carry):
        for s in range(4):
            i = 4 * t + s
            for b in range(2):
                total = acc[2 * i + b]
                total = (total[0:16] + total[16:32]) * scale
                mine[i, :, b * 256 : (b + 1) * 256] = total[0:8]
                theirs[i, :, b * 256 : (b + 1) * 256] = total[8:16]
        return carry

    lax.fori_loop(0, targets // 4, finish, 0)


def far_sum(lists, count, source_of, moment_of, target):
    half = left_half((FEATURES, 128))
    half8 = left_half((8, 128))
    total = jnp.zeros((8, 64), F32)
    for chunk in range(count // 8):
        sources, moments = [], []
        for q in range(4):
            a, b = lists(chunk * 8 + 2 * q), lists(chunk * 8 + 2 * q + 1)
            sources.append(jnp.where(half, source_of(a), source_of(b)).astype(BF16))
            moments.append(jnp.where(half8, moment_of(a), moment_of(b)))
        sources = jnp.concatenate(sources, axis=1)
        moments = jnp.concatenate(moments, axis=1)
        total = total + exact_dot(moments, slope_of(dot(sources, target, CN)), NN)
    return total * (SLOPE / 64)


def shared(left, right):
    half = left_half(left.shape)
    pair = [jnp.where(half, left, 0.0), jnp.where(half, 0.0, right)]
    return jnp.concatenate(pair, axis=0).astype(BF16)


def own_halves(rows):
    return jnp.where(left_half((8, 128)), rows[0:8], rows[8:16])


def far_pair(lists, source_of, moment_of, target):
    half = left_half((FEATURES, 128))
    half8 = left_half((8, 128))
    total = jnp.zeros((16, 128), F32)
    for chunk in range(4):
        sources, moments = [], []
        for of in lists:
            row, moment = [], []
            for q in range(4):
                a, b = of(chunk * 8 + 2 * q), of(chunk * 8 + 2 * q + 1)
                row.append(jnp.where(half, source_of(a), source_of(b)).astype(BF16))
                moment.append(jnp.where(half8, moment_of(a), moment_of(b)))
            sources.append(jnp.concatenate(row, axis=1))
            moments.append(jnp.concatenate(moment, axis=1))
        panel = slope_of(dot(jnp.concatenate(sources, axis=0), target, CN))
        total = total + exact_dot(jnp.concatenate(moments, axis=0), panel, NN)
    return own_halves(total) * (SLOPE / 64)


def upper_levels(coarse, me, box8, roots, c, fbs, fbt, pm, qm):
    def prep(t, carry):
        for s in range(14):
            b = 14 * t + s
            fbs[b], fbt[b] = features(twice(rows_of(box8, b, 0.0)), c, True, True)
        return carry

    lax.fori_loop(0, 4, prep, 0)
    half = left_half((FEATURES, 128))
    half8 = left_half((8, 128))

    def merge(child, parent, moments, out, count):
        def body(t, carry):
            for s in range(8):
                m = t * 8 + s
                source = jnp.where(half, fbs[child + 2 * m], fbs[child + 2 * m + 1]).astype(BF16)
                target = fbt[parent + m].astype(BF16)[:, :64]
                panel = value_of(dot(source, target, CN))
                pair = jnp.where(half8, moments[2 * m], moments[2 * m + 1])
                out[m] = twice(exact_dot(pair, panel, NN) * (1.0 / 64))
            return carry

        lax.fori_loop(0, count // 8, body, 0)

    merge(0, 32, roots, pm, 16)
    merge(32, 48, pm, qm, 8)
    n = me
    m = n >> 1
    t = n >> 2

    def far(base, row, moments):
        target = fbt[row].astype(BF16)[:, :64]
        return far_sum(
            lambda e: coarse[e, row], 16, lambda b: fbs[base + b], lambda b: moments[b], target
        )

    def down(local, source, target):
        panel = value_of(dot(fbs[source].astype(BF16)[:, :64], fbt[target].astype(BF16)[:, :64], CN))
        return exact_dot(local, panel, NN) * (1.0 / 64)

    quad = far(48, 48 + t, qm)
    pair = down(quad, 48 + t, 32 + m) + far(32, 32 + m, pm)
    return down(pair, 32 + m, n) + far(0, n, roots)


def far_kernel(
    far, coarse, me, own, low, high, box8, roots,
    out,
    fps, fpt, mps, fbs, fbt, pm, qm, local,
    *, leaves, factor,
):
    c = center_of(own)

    def prep_far(t, carry):
        for s in range(8):
            i = t * 8 + s
            for k, (page, at) in enumerate(((low, 0), (own, 64), (high, 0))):
                (fps[k * leaves + i],) = features(page[i, at + 8 : at + 16], c, True, False)
                mps[k * leaves + i] = page[i, at : at + 8]
            (fpt[i],) = features(own[i, 72:80], c, False, True)
        return carry

    lax.fori_loop(0, leaves // 8, prep_far, 0)
    dev = me[0]
    base = (dev - 1) * leaves

    def gather(t, carry):
        for s in range(4):
            k = t * 4 + s
            local[k] = far_pair(
                [lambda e: far[2 * k, e] - base, lambda e: far[2 * k + 1, e] - base],
                lambda b: fps[b], lambda b: mps[b], shared(fpt[2 * k], fpt[2 * k + 1]),
            )
        return carry

    lax.fori_loop(0, leaves // 8, gather, 0)
    local_dev = upper_levels(coarse, dev, box8, roots, c, fbs, fbt, pm, qm)
    own_source = fbs[dev].astype(BF16)[:, :64]
    half = left_half((FEATURES, 128))

    def down(t, carry):
        for s in range(8):
            k = t * 8 + s
            target = jnp.where(half, fpt[2 * k], fpt[2 * k + 1]).astype(BF16)
            panel = value_of(dot(own_source, target, CN))
            local[k] += exact_dot(local_dev, panel, NN) * (1.0 / 64)
        return carry

    lax.fori_loop(0, leaves // 16, down, 0)

    def finish(t, carry):
        for s in range(16):
            i = t * 16 + s
            source = fps[leaves + i].astype(BF16)[:, :64]
            (points,) = features(lanes_of(own, i, 8), c, False, True)
            basis = value_of(dot(source, points.astype(BF16), CN))
            part = local[t * 8 + s // 2][:, (s % 2) * 64 : (s % 2) * 64 + 64]
            out[i] = exact_dot(part, basis, NN) * factor
        return carry

    lax.fori_loop(0, leaves // 16, finish, 0)


def sum_kernel(counts, me, far, mine, back, out, order, *, leaves):
    assign(lambda i: counts[i], leaves, order)
    half = leaves // 2
    lane = lax.broadcasted_iota(jnp.int32, far.shape[1:], 1)

    def body(t, carry):
        for s in range(8):
            k = 8 * t + s
            for side, part in ((me[1], mine), (1 - me[1], back)):
                i = order[side * half + k]
                out[i] = jnp.where(lane < counts[i], far[i] + part[k], 0.0)
        return carry

    lax.fori_loop(0, half // 8, body, 0)


def cost(microseconds):
    flops = int(microseconds * 1.1e9)
    return pl.CostEstimate(flops=flops, transcendentals=0, bytes_accessed=1 << 20)


def local(points, probes, counts, near_list, far_list, coarse_list, leaf_proxy, box_proxy):
    leaves = points.shape[0]
    size = points.shape[2]
    nodes = lax.axis_size("space")
    device = lax.axis_index("space")
    factor = size ** (-0.5)
    half = lax.axis_index("probe") & 1
    me = jnp.stack([device, half]).astype(jnp.int32)
    points = jnp.transpose(points, (1, 0, 2))
    leafp = jnp.transpose(leaf_proxy, (1, 0, 2))
    boxp = jnp.transpose(box_proxy, (1, 0, 2))
    near = near_list.T
    forward = [(i, i + 1) for i in range(nodes - 1)]
    backward = [(i + 1, i) for i in range(nodes - 1)]
    pairs = [(i, i ^ 1) for i in range(lax.axis_size("probe"))]
    partner = lax.ppermute(probes, "probe", pairs)
    params = pltpu.CompilerParams(vmem_limit_bytes=56 << 20)
    vm = pltpu.VMEM
    vmem = pl.BlockSpec(memory_space=vm)
    smem = pl.BlockSpec(memory_space=pltpu.SMEM)
    shape = jax.ShapeDtypeStruct
    page, dev = pl.pallas_call(
        functools.partial(moments_kernel, leaves=leaves, factor=factor),
        out_shape=(shape((leaves, 80, 128), F32), shape((8, 128), F32)),
        in_specs=[smem] * 2 + [vmem] * 4,
        out_specs=(vmem, vmem),
        scratch_shapes=[vm((leaves, FEATURES, 128), F32)],
        compiler_params=params,
        cost_estimate=cost(8),
        name="moments",
    )(counts, me, probes, points, leafp, boxp)
    roots = lax.all_to_all(
        jnp.broadcast_to(dev[None], (nodes, 8, 128)), "space", split_axis=0, concat_axis=0, tiled=True
    )
    tiles = jnp.transpose(partner.reshape(leaves, 8, size // 128, 128), (0, 2, 1, 3))
    both = jnp.concatenate([page, tiles.reshape(leaves, size // 16, 128)], axis=1)
    low = lax.ppermute(both, "space", forward)
    high = lax.ppermute(both, "space", backward)
    targets = leaves // 2

    def work(blocks):
        return (
            [
                vm((blocks, FEATURES, 128), BF16),
                vm((blocks, 32, 128), BF16),
                vm((targets * 2, FEATURES, 256), BF16),
                pltpu.SMEM((48,), jnp.int32),
                pltpu.SMEM((targets * 32 + 96,), jnp.int32),
                pltpu.SMEM((leaves,), jnp.int32),
            ]
            + [vm((256, 256), F32)] * UNITS
        )

    page, roots = lax.optimization_barrier((page, roots))
    acc0 = pl.pallas_call(
        functools.partial(own_kernel, leaves=leaves, targets=targets),
        out_shape=shape((targets * 2, 32, 256), F32),
        in_specs=[smem] * 3 + [vmem] * 2,
        out_specs=vmem,
        scratch_shapes=work(leaves * 4 + 1),
        compiler_params=params,
        cost_estimate=cost(28),
        name="near_own",
    )(near, counts, me, page, partner)
    counts3 = jnp.concatenate(
        [low[:, 11, 0].astype(jnp.int32), counts, high[:, 11, 0].astype(jnp.int32)]
    )
    mine, theirs = pl.pallas_call(
        functools.partial(halo_kernel, leaves=leaves, targets=targets, factor=factor),
        out_shape=(shape((targets, 8, size), F32),) * 2,
        in_specs=[smem] * 3 + [vmem] * 4,
        out_specs=(vmem, vmem),
        scratch_shapes=[vm((targets * 2, 32, 256), F32)] + work(2 * leaves * 4 + 1),
        compiler_params=params,
        cost_estimate=cost(30),
        name="near_halo",
    )(near, counts3, me, page, low, high, acc0)
    back = lax.ppermute(theirs, "probe", pairs)
    whole = lambda dims: pl.BlockSpec(dims, lambda i: (0,) * len(dims))
    tail = pl.BlockSpec((leaves, 16, 128), lambda i: (0, 4, 0))
    far = pl.pallas_call(
        functools.partial(far_kernel, leaves=leaves, factor=factor),
        out_shape=shape(probes.shape, F32),
        grid=(1,),
        in_specs=[smem] * 3 + [whole(page.shape), tail, tail, whole(boxp.shape), whole(roots.shape)],
        out_specs=whole(probes.shape),
        scratch_shapes=[
            vm((3 * leaves, FEATURES, 128), F32),
            vm((leaves, FEATURES, 128), F32),
            vm((3 * leaves, 8, 128), F32),
            vm((56, FEATURES, 128), F32),
            vm((56, FEATURES, 128), F32),
            vm((nodes // 2, 8, 128), F32),
            vm((nodes // 4, 8, 128), F32),
            vm((leaves // 2, 8, 128), F32),
        ],
        compiler_params=params,
        cost_estimate=cost(30),
        name="far",
    )(far_list, coarse_list.T, me, page, low, high, boxp, roots)
    return pl.pallas_call(
        functools.partial(sum_kernel, leaves=leaves),
        out_shape=shape(probes.shape, F32),
        in_specs=[smem] * 2 + [vmem] * 3,
        out_specs=vmem,
        scratch_shapes=[pltpu.SMEM((leaves,), jnp.int32)],
        compiler_params=params,
        name="sum",
    )(counts, me, far, mine, back)


def solution(mesh):
    return jax.shard_map(
        local,
        mesh=mesh,
        in_specs=(
            P("space", None, None),
            P("space", "probe", None),
            P("space"),
            P("space", None),
            P("space", None),
            P(),
            P("space", None, None),
            P(),
        ),
        out_specs=P("space", "probe", None),
        check_vma=False,
    )
```
